32 devices in a mesh: dp: 32 (over z, y, x, core).
Axes of the slice: x: 2, y: 2, z: 4, core: 2. Of those that a mesh axis runs over, the one named last changes fastest.
Arguments:
- image_tokens: bfloat16 [27840, 384], P('dp'), may hold values from -6 to 6
- image_lengths: int32 [192], replicated, may hold values from 50 to 145, as said below
- caption_tokens: bfloat16 [14784, 384], P('dp'), may hold values from -6 to 6
- caption_eot: int32 [192], P('dp'), may hold values from 5 to 76
- image_gains: bfloat16 [3, 384], replicated, may hold values from 0.5 to 1.5
- image_shifts: bfloat16 [7, 384], replicated, may hold values from -1.1953125 to 1.1953125
- image_attn_in: bfloat16 [384, 1152], replicated, may hold values from -0.3125 to 0.3125
- image_attn_out: bfloat16 [384, 384], replicated, may hold values from -2.5 to 2.5
- image_up: bfloat16 [384, 1536], replicated, may hold values from -0.3125 to 0.3125
- image_up_bias: bfloat16 [1536], replicated, may hold values from -3 to 3
- image_down: bfloat16 [1536, 384], replicated, may hold values from -0.15625 to 0.15625
- image_proj: bfloat16 [384, 384], replicated, may hold values from -0.3125 to 0.3125
- caption_gains: bfloat16 [3, 384], replicated, may hold values from 0.5 to 1.5
- caption_shifts: bfloat16 [7, 384], replicated, may hold values from -1.1953125 to 1.1953125
- caption_attn_in: bfloat16 [384, 1152], replicated, may hold values from -0.3125 to 0.3125
- caption_attn_out: bfloat16 [384, 384], replicated, may hold values from -1.25 to 1.25
- caption_up: bfloat16 [384, 1536], replicated, may hold values from -0.3125 to 0.3125
- caption_up_bias: bfloat16 [1536], replicated, may hold values from -3 to 3
- caption_down: bfloat16 [1536, 384], replicated, may hold values from -0.15625 to 0.15625
- caption_proj: bfloat16 [384, 384], replicated, may hold values from -0.3125 to 0.3125
- logit_scale: float32 [], replicated, may hold values from 3.6 to 4.3
Outputs:
- loss: float32 [], replicated
- image_grad: bfloat16 [27840, 384], P('dp')
- caption_grad: bfloat16 [14784, 384], P('dp')
- image_gains_grad: float32 [3, 384], replicated
- image_shifts_grad: float32 [7, 384], replicated
- image_attn_in_grad: float32 [442368], P('dp')
- image_attn_out_grad: float32 [147456], P('dp')
- image_up_grad: float32 [589824], P('dp')
- image_up_bias_grad: float32 [1536], replicated
- image_down_grad: float32 [589824], P('dp')
- image_proj_grad: float32 [147456], P('dp')
- caption_gains_grad: float32 [3, 384], replicated
- caption_shifts_grad: float32 [7, 384], replicated
- caption_attn_in_grad: float32 [442368], P('dp')
- caption_attn_out_grad: float32 [147456], P('dp')
- caption_up_grad: float32 [589824], P('dp')
- caption_up_bias_grad: float32 [1536], replicated
- caption_down_grad: float32 [589824], P('dp')
- caption_proj_grad: float32 [147456], P('dp')
- logit_scale_grad: float32 [], replicated
The draws below stay inside these ranges and needn't reach their ends.
Inputs may be any that keep to these rules, and one draw needn't show every extreme that they name: `image_lengths`: each entry is 50 (a 224 px image) or 145 (a 384 px image), each image's own. Device 0 holds only 145-token images, and every device in the upper half of dp only 50-token ones; images of the other devices of the lower half have either length, in any order.
All inputs are finite; a program needn't handle non-finite values.
Results may differ from the reference program's by a relative error of at most 0.022.
Values may be sent and summed in bfloat16 or wider, within the bound.
No kernel may reach another device: no remote copies, remote signals or barrier semaphores. Data moves between devices by JAX's collectives and lax.ppermute only.
A program may use at most 192 MiB of HBM per device.

```python
import jax
import jax.numpy as jnp
from jax import lax

D = 384
FF = 1536
DT = 384
FFT = 1536
E = 384
HEAD = 64
CTX = 77
LONG = 145
SHORT = 50
IMG_DEV = 6
TOK_DEV = 870
PAIRS = 192
TOK_ROWS = 27840
N_DP = 32


def draw_image_lengths(key, part):
    places = jnp.arange(PAIRS, dtype=jnp.int32)
    coins = jax.random.randint(jax.random.fold_in(key, 17), (PAIRS,), 0, 2)
    first_device = places < IMG_DEV
    upper_half = places >= PAIRS // 2
    is_long = jnp.where(first_device, 1, jnp.where(upper_half, 0, coins))
    return jnp.where(is_long == 1, LONG, SHORT).astype(jnp.int32)


def plant(values, key, low, high):
    spot = [jax.random.randint(jax.random.fold_in(key, axis), (), 0, length) for axis, length in enumerate(values.shape)]
    main_axis = values.shape.index(max(values.shape))
    next_to = spot[:main_axis] + [(spot[main_axis] + 1) % values.shape[main_axis]] + spot[main_axis + 1:]
    return values.at[tuple(spot)].set(low).at[tuple(next_to)].set(high)


def levels(stream_key, shape, shards, smallest, high):
    level = 1.0
    for axis_at, blocks in shards:
        steps = jax.random.uniform(jax.random.fold_in(jax.random.fold_in(stream_key, 6), axis_at), (blocks,), jnp.float32, smallest / len(shards), high / len(shards))
        level = level * jnp.repeat(jnp.exp(steps), shape[axis_at] // blocks).reshape((-1,) + (1,) * (len(shape) - 1 - axis_at))
    return level


def normal_values(stream_key, shape, deviation, bound, split=(), kind=jnp.bfloat16):
    level = levels(stream_key, shape, split, -0.22, 0.18) if split else 1.0
    entries = jax.random.normal(stream_key, shape, jnp.float32) * deviation * level
    return jnp.minimum(jnp.maximum(entries, -bound), bound).astype(kind)


def setup_inputs(seed: int = 0) -> dict:
    seeds = jax.random.split(jax.random.key(seed), 22)
    return {
        "image_tokens": normal_values(seeds[0], (TOK_ROWS, D), 1.0, 6.0, ((0, 32),)),
        "image_lengths": draw_image_lengths(jax.random.fold_in(seeds[21], 71), 0),
        "caption_tokens": normal_values(seeds[2], (PAIRS * CTX, DT), 1.0, 6.0, ((0, 32),)),
        "caption_eot": plant(jax.random.randint(seeds[3], (PAIRS,), 5, CTX), jax.random.fold_in(seeds[3], 1), 5, CTX - 1).astype(jnp.int32),
        "image_gains": jnp.clip(1.0 + 0.1 * jax.random.normal(seeds[4], (3, D), jnp.float32), 0.5, 1.5).astype(jnp.bfloat16),
        "image_shifts": normal_values(seeds[5], (7, D), 0.2, 1.1953125),
        "image_attn_in": normal_values(seeds[6], (D, 3 * D), D ** -0.5, 0.3125),
        "image_attn_out": normal_values(seeds[7], (D, D), (D // 64) ** -0.5, 2.5),
        "image_up": normal_values(seeds[8], (D, FF), D ** -0.5, 0.3125),
        "image_up_bias": normal_values(seeds[9], (FF,), 0.5, 3.0),
        "image_down": normal_values(seeds[10], (FF, D), FF ** -0.5, 0.15625),
        "image_proj": normal_values(seeds[11], (D, E), D ** -0.5, 0.3125),
        "caption_gains": jnp.clip(1.0 + 0.1 * jax.random.normal(seeds[12], (3, DT), jnp.float32), 0.5, 1.5).astype(jnp.bfloat16),
        "caption_shifts": normal_values(seeds[13], (7, DT), 0.2, 1.1953125),
        "caption_attn_in": normal_values(seeds[14], (DT, 3 * DT), DT ** -0.5, 0.3125),
        "caption_attn_out": normal_values(seeds[15], (DT, DT), (DT // 16) ** -0.5, 1.25),
        "caption_up": normal_values(seeds[16], (DT, FFT), DT ** -0.5, 0.3125),
        "caption_up_bias": normal_values(seeds[17], (FFT,), 0.5, 3.0),
        "caption_down": normal_values(seeds[18], (FFT, DT), FFT ** -0.5, 0.15625),
        "caption_proj": normal_values(seeds[19], (DT, E), DT ** -0.5, 0.3125),
        "logit_scale": jnp.clip(jax.random.uniform(seeds[20], (), jnp.float32, 3.6, 4.3), 3.6, 4.3),
    }


@jax.custom_vjp
def low(v):
    return lax.optimization_barrier(v.astype(jnp.bfloat16)).astype(jnp.float32)

@jax.custom_vjp
def low_back(v):
    return v

def low_keep(v):
    return (low(v), None)

def low_pass(kept, grad):
    return (grad,)

def back_keep(v):
    return (v, None)

def back_low(kept, grad):
    return (low(grad),)
low.defvjp(low_keep, low_pass)
low_back.defvjp(back_keep, back_low)
LAYER_EPSILON = 1e-05
UNIT_EPSILON = 1e-06

def matmul(left, right):
    return jnp.dot(left, right, precision=lax.Precision.HIGHEST, preferred_element_type=jnp.float32)

def layer_norm(values, gain, shift):
    centred = values - lax.optimization_barrier(jnp.mean(values, axis=-1, keepdims=True))
    return centred * lax.rsqrt(lax.optimization_barrier(jnp.mean(centred * centred, axis=-1, keepdims=True)) + LAYER_EPSILON) * gain + shift

def block(inputs, allowed, gains, shifts, attn_in, attn_out, up_weight, up_bias, down_weight):
    row_count, width = inputs.shape
    heads = width // HEAD
    first = low(layer_norm(inputs, gains[0], shifts[0]))
    in_bias = jnp.concatenate([shifts[1], jnp.zeros_like(shifts[1]), shifts[2]])
    packed = low(low_back(matmul(first, attn_in) + in_bias))
    parts = packed.reshape(row_count, 3, heads, HEAD)
    scores = jnp.einsum('qhd,khd->hqk', parts[:, 0], parts[:, 1], precision=lax.Precision.HIGHEST) * 0.125
    scores = low_back(jnp.where(allowed[None], scores, -1e+30))
    top_score = lax.optimization_barrier(jnp.max(scores, axis=-1, keepdims=True))
    expo = jnp.exp(scores - top_score)
    probs = low(expo / lax.optimization_barrier(jnp.sum(expo, axis=-1, keepdims=True)))
    mixed = jnp.einsum('hqk,khd->qhd', probs, parts[:, 2], precision=lax.Precision.HIGHEST).reshape(row_count, width)
    mixed = low(low_back(mixed))
    middle = inputs + low_back(matmul(mixed, attn_out) + shifts[3])
    second = low(layer_norm(middle, gains[1], shifts[4]))
    pre_act = low_back(matmul(second, up_weight) + up_bias)
    activated = low(pre_act * jax.nn.sigmoid(1.702 * pre_act))
    return middle + low_back(matmul(activated, down_weight) + shifts[5])

def head(pooled, gain, shift, projection):
    normed = low(layer_norm(pooled, gain, shift))
    embedding = low_back(matmul(normed, projection))
    return low(embedding * lax.rsqrt(lax.optimization_barrier(jnp.sum(embedding * embedding, axis=-1, keepdims=True)) + UNIT_EPSILON))

def image_device(tokens, lengths, weights):
    gains, shifts, attn_in, attn_out, up_weight, up_bias, down_weight, projection = weights
    row_count = tokens.shape[0]
    row_ends = jnp.cumsum(lengths).astype(jnp.int32)
    row_starts = (row_ends - lengths).astype(jnp.int32)
    places = jnp.arange(row_count, dtype=jnp.int32)
    groups = lax.optimization_barrier(jnp.sum((places[:, None] >= row_ends[None, :]).astype(jnp.int32), axis=1))
    allowed = groups[:, None] == groups[None, :]
    output = block(tokens, allowed, gains, shifts, attn_in, attn_out, up_weight, up_bias, down_weight)
    return head(output[row_starts], gains[2], shifts[6], projection)

def caption_device(tokens, last_token, weights):
    gains, shifts, attn_in, attn_out, up_weight, up_bias, down_weight, projection = weights
    row_count = tokens.shape[0]
    places = jnp.arange(row_count, dtype=jnp.int32)
    caption_of = places // CTX
    within = places % CTX
    allowed = (caption_of[:, None] == caption_of[None, :]) & (within[None, :] <= within[:, None])
    output = block(tokens, allowed, gains, shifts, attn_in, attn_out, up_weight, up_bias, down_weight)
    targets = (jnp.arange(last_token.shape[0], dtype=jnp.int32) * CTX + last_token).astype(jnp.int32)
    return head(output[targets], gains[2], shifts[6], projection)

def log_total(values, axis):
    top_value = lax.optimization_barrier(jnp.max(values, axis=axis, keepdims=True))
    return jnp.squeeze(top_value, axis) + jnp.log(lax.optimization_barrier(jnp.sum(jnp.exp(values - top_value), axis=axis)))

def contrastive(image_units, caption_units, scale_log):
    similar = low_back(matmul(image_units, caption_units.T))
    logits = jnp.exp(scale_log) * similar
    diagonal = jnp.diagonal(logits)
    return 0.5 * jnp.sum(log_total(logits, 1) - diagonal) + 0.5 * jnp.sum(log_total(logits, 0) - diagonal)

def reference(image_tokens, image_lengths, caption_tokens, caption_eot, image_gains, image_shifts, image_attn_in, image_attn_out, image_up, image_up_bias, image_down, image_proj, caption_gains, caption_shifts, caption_attn_in, caption_attn_out, caption_up, caption_up_bias, caption_down, caption_proj, logit_scale):
    lengths = image_lengths.reshape(N_DP, IMG_DEV)
    last_tokens = caption_eot.reshape(N_DP, IMG_DEV)

    def forward(img_tokens, cap_tokens, img_gains, img_shifts, img_in, img_out, img_up, img_up_bias, img_down, img_proj, cap_gains, cap_shifts, cap_in, cap_out, cap_up, cap_up_bias, cap_down, cap_proj, scale_log):
        image_weights = (img_gains, img_shifts, img_in, img_out, img_up, img_up_bias, img_down, img_proj)
        caption_weights = (cap_gains, cap_shifts, cap_in, cap_out, cap_up, cap_up_bias, cap_down, cap_proj)

        def image_one(pair_in):
            return image_device(pair_in[0], pair_in[1], image_weights)

        def caption_one(pair_in):
            return caption_device(pair_in[0], pair_in[1], caption_weights)
        image_units = lax.map(jax.checkpoint(image_one), (img_tokens.reshape(N_DP, TOK_DEV, D), lengths))
        caption_units = lax.map(jax.checkpoint(caption_one), (cap_tokens.reshape(N_DP, IMG_DEV * CTX, DT), last_tokens))
        return contrastive(image_units.reshape(PAIRS, E), caption_units.reshape(PAIRS, E), scale_log)
    total, pullback = jax.vjp(forward, image_tokens.astype(jnp.float32), caption_tokens.astype(jnp.float32), image_gains.astype(jnp.float32), image_shifts.astype(jnp.float32), image_attn_in.astype(jnp.float32), image_attn_out.astype(jnp.float32), image_up.astype(jnp.float32), image_up_bias.astype(jnp.float32), image_down.astype(jnp.float32), image_proj.astype(jnp.float32), caption_gains.astype(jnp.float32), caption_shifts.astype(jnp.float32), caption_attn_in.astype(jnp.float32), caption_attn_out.astype(jnp.float32), caption_up.astype(jnp.float32), caption_up_bias.astype(jnp.float32), caption_down.astype(jnp.float32), caption_proj.astype(jnp.float32), logit_scale.astype(jnp.float32))
    grads = pullback(jnp.ones_like(total))
    return (total / PAIRS, grads[0].astype(jnp.bfloat16), grads[1].astype(jnp.bfloat16), grads[2], grads[3], grads[4].reshape(-1), grads[5].reshape(-1), grads[6].reshape(-1), grads[7], grads[8].reshape(-1), grads[9].reshape(-1), grads[10], grads[11], grads[12].reshape(-1), grads[13].reshape(-1), grads[14].reshape(-1), grads[15], grads[16].reshape(-1), grads[17].reshape(-1), grads[18])
```

```python
import jax
import jax.numpy as jnp
from jax import lax
from jax.sharding import PartitionSpec as P

HEAD = 64
CTX = 77

LAYER_EPSILON = 1e-05
UNIT_EPSILON = 1e-06

BF = jnp.bfloat16
F32 = jnp.float32


def dot(left, right, dims=((1,), (0,))):
    return lax.dot_general(left.astype(BF), right.astype(BF), (dims, ((), ())), preferred_element_type=F32)


NT = ((1,), (1,))
TN = ((0,), (0,))


def normalize(values):
    centred = values - jnp.mean(values, axis=-1, keepdims=True)
    inverse = lax.rsqrt(jnp.mean(centred * centred, axis=-1, keepdims=True) + LAYER_EPSILON)
    return centred * inverse, inverse


def norm_back(incoming, normal, inverse, gain):
    scaled = incoming * gain
    return inverse * (
        scaled
        - jnp.mean(scaled, axis=-1, keepdims=True)
        - normal * jnp.mean(scaled * normal, axis=-1, keepdims=True)
    )


def head_mask(count, width):
    heads = width // HEAD
    rows = lax.broadcasted_iota(jnp.int32, (heads * count, width), 0) // count
    lanes = lax.broadcasted_iota(jnp.int32, (heads * count, width), 1) // HEAD
    return rows == lanes


def spread(values):
    count, width = values.shape
    tiled = jnp.tile(values, (width // HEAD, 1))
    return jnp.where(head_mask(count, width), tiled, jnp.zeros_like(tiled))


def collect(values, count):
    rows, width = values.shape
    kept = jnp.where(head_mask(count, width), values, 0.0)
    return jnp.sum(kept.reshape(rows // count, count, width), axis=0)


def attend_forward(tokens, low, high, place, gains, shifts, attn_in):
    rows, width = tokens.shape
    count = low.shape[0]
    heads = width // HEAD
    normal, inverse = normalize(tokens.astype(F32))
    normal_low = normal.astype(BF)
    picked = place[:, None] == jnp.arange(rows, dtype=jnp.int32)[None, :]
    pooled = dot(picked, tokens).astype(BF)
    pooled_normal, _ = normalize(pooled.astype(F32))
    first = (pooled_normal * gains[0] + shifts[0]).astype(BF)
    query = (dot(first, attn_in[:, :width]) + shifts[1]).astype(BF)
    key_back = dot(spread(query), attn_in[:, width : 2 * width], NT) * 0.125
    offset = jnp.sum(key_back * shifts[0], axis=-1, keepdims=True)
    scores = dot(key_back * gains[0], normal_low, NT) + offset
    columns = jnp.arange(rows, dtype=jnp.int32)[None, :]
    allowed = (columns >= jnp.tile(low, heads)[:, None]) & (columns < jnp.tile(high, heads)[:, None])
    scores = jnp.where(allowed, scores, -1e30)
    expo = jnp.where(allowed, jnp.exp(scores - jnp.max(scores, axis=-1, keepdims=True)), 0.0)
    probs = expo / jnp.sum(expo, axis=-1, keepdims=True)
    probs_low = probs.astype(BF)
    probs_sum = jnp.sum(probs_low.astype(F32), axis=-1, keepdims=True)
    blend_normal = dot(probs_low, normal_low)
    blend = blend_normal * gains[0] + shifts[0] * probs_sum
    mixed = collect(dot(blend, attn_in[:, 2 * width :]) + probs_sum * shifts[2], count).astype(BF)
    kept = (normal, inverse, normal_low, picked, pooled_normal, key_back, probs, probs_low, probs_sum, blend_normal)
    return pooled, mixed, blend.astype(BF), kept


def attend_backward(grad_mixed, grad_middle, kept, gains, shifts, attn_in):
    normal, inverse, normal_low, picked, pooled_normal, key_back, probs, probs_low, probs_sum, blend_normal = kept
    rows, width = normal.shape
    count = grad_mixed.shape[0]
    wide = spread(grad_mixed)
    value_back = dot(wide, attn_in[:, 2 * width :], NT)
    offset = jnp.sum(value_back * shifts[0] + wide.astype(F32) * shifts[2], axis=-1, keepdims=True)
    grad_probs = dot(value_back * gains[0], normal_low, NT) + offset
    grad_scores = probs * (grad_probs - jnp.sum(grad_probs * probs, axis=-1, keepdims=True))
    scores_low = grad_scores.astype(BF)
    scores_sum = jnp.sum(scores_low.astype(F32), axis=-1, keepdims=True)
    turn_normal = dot(scores_low, normal_low)
    turn = turn_normal * gains[0] + shifts[0] * scores_sum
    grad_query = (collect(dot(turn, attn_in[:, width : 2 * width]), count) * 0.125).astype(BF)
    query_back = dot(grad_query, attn_in[:, :width], NT)
    gain_part = (
        jnp.sum(turn_normal * key_back, axis=0)
        + jnp.sum(blend_normal * value_back, axis=0)
        + jnp.sum(pooled_normal * query_back, axis=0)
    )
    shift_part = (
        jnp.sum(scores_sum * key_back, axis=0)
        + jnp.sum(probs_sum * value_back, axis=0)
        + jnp.sum(query_back, axis=0)
    )
    grad_first = (
        dot(scores_low, key_back, TN) + dot(probs_low, value_back, TN) + dot(picked, query_back, TN)
    )
    high = grad_middle.astype(BF)
    rest = (grad_middle - high.astype(F32)).astype(BF)
    grad_tokens = (
        norm_back(grad_first, normal, inverse, gains[0]) + dot(picked, high, TN) + dot(picked, rest, TN)
    )
    return grad_tokens.astype(BF), grad_query, turn.astype(BF), jnp.stack([gain_part, shift_part])


def pooled_forward(pooled, mixed, gains, shifts, attn_out, up, up_bias, down, proj):
    middle = pooled.astype(F32) + dot(mixed, attn_out) + shifts[3]
    second_normal, second_inv = normalize(middle)
    second = (second_normal * gains[1] + shifts[4]).astype(BF)
    pre = dot(second, up) + up_bias
    gate = jax.nn.sigmoid(1.702 * pre)
    act = (pre * gate).astype(BF)
    out = middle + dot(act, down) + shifts[5]
    post_normal, post_inv = normalize(out)
    post = (post_normal * gains[2] + shifts[6]).astype(BF)
    embed = dot(post, proj)
    radius = lax.rsqrt(jnp.sum(embed * embed, axis=-1, keepdims=True) + UNIT_EPSILON)
    unit = (embed * radius).astype(BF)
    return unit, (second_normal, second_inv, second, pre, gate, act, post_normal, post_inv, post, embed, radius)


def pooled_backward(grad_unit, kept, gains, attn_out, up, down, proj):
    second_normal, second_inv, second, pre, gate, act, post_normal, post_inv, post, embed, radius = kept
    along = jnp.sum(embed * grad_unit, axis=-1, keepdims=True)
    grad_embed = (radius * grad_unit - radius * radius * radius * embed * along).astype(BF)
    grad_post = dot(grad_embed, proj, NT)
    grad_out = norm_back(grad_post, post_normal, post_inv, gains[2])
    grad_z = grad_out.astype(BF)
    slope = gate + 1.702 * pre * gate * (1.0 - gate)
    grad_pre = (dot(grad_z, down, NT) * slope).astype(BF)
    grad_second = dot(grad_pre, up, NT)
    grad_middle = grad_out + norm_back(grad_second, second_normal, second_inv, gains[1])
    grad_y = grad_middle.astype(BF)
    grad_mixed = dot(grad_y, attn_out, NT).astype(BF)
    gain_rows = (
        jnp.sum(grad_second * second_normal, axis=0),
        jnp.sum(grad_post * post_normal, axis=0),
    )

    def total(values):
        return jnp.sum(values.astype(F32), axis=0)

    shift_rows = (total(grad_mixed), total(grad_y), total(grad_second), total(grad_z), total(grad_post))
    return grad_mixed, grad_middle, gain_rows, shift_rows, total(grad_pre), (grad_y, grad_pre, grad_z, grad_embed)


def window(total_rows, columns, devices, index):
    part = total_rows * columns // devices
    start = index * part
    first = start // columns
    if part % columns == 0:
        span = part // columns
    else:
        span = max((d * part + part - 1) // columns - d * part // columns + 1 for d in range(devices))
    first = jnp.minimum(first, total_rows - span)
    return first, span, start - first * columns, part


def cut(left, right, devices, index):
    total_rows, columns = left.shape[1], right.shape[1]
    first, span, offset, part = window(total_rows, columns, devices, index)
    rows = dot(lax.dynamic_slice_in_dim(left, first, span, 1), right, TN)
    return finish(rows, offset, part)


def finish(rows, offset, part):
    flat = rows.reshape(-1)
    if flat.shape[0] == part:
        return flat
    return lax.dynamic_slice_in_dim(flat, offset, part)


def slices_out(values, count, columns, devices):
    width = values.shape[1]
    heads = values.shape[0] // count
    cuts = []
    if (width * columns // devices) % columns == 0:
        span = width // devices
        return values.reshape(heads, count, devices, span).transpose(2, 1, 0, 3)
    for d in range(devices):
        part = width * columns // devices
        span = max((e * part + part - 1) // columns - e * part // columns + 1 for e in range(devices))
        first = min(d * part // columns, width - span)
        cuts.append(values[:, first : first + span].reshape(heads, count, span).transpose(1, 0, 2))
    return jnp.stack(cuts)


def exchange(parts):
    devices = parts[0].shape[0]
    flat = jnp.concatenate([part.reshape(devices, -1).astype(BF) for part in parts], axis=1)
    got = lax.all_to_all(flat, "dp", 0, 0, tiled=True)
    outs = []
    at = 0
    for part in parts:
        size = part[0].size
        outs.append(got[:, at : at + size].reshape(part.shape))
        at += size
    return outs


def body(
    image_tokens,
    image_lengths,
    caption_tokens,
    caption_eot,
    image_gains,
    image_shifts,
    image_attn_in,
    image_attn_out,
    image_up,
    image_up_bias,
    image_down,
    image_proj,
    caption_gains,
    caption_shifts,
    caption_attn_in,
    caption_attn_out,
    caption_up,
    caption_up_bias,
    caption_down,
    caption_proj,
    logit_scale,
):
    index = lax.axis_index("dp")
    devices = lax.axis_size("dp")
    count = caption_eot.shape[0]
    width = image_tokens.shape[1]
    heads = width // HEAD
    lengths = lax.dynamic_slice_in_dim(image_lengths, index * count, count)
    image_high = jnp.cumsum(lengths)
    image_low = image_high - lengths
    caption_low = jnp.arange(count, dtype=jnp.int32) * CTX
    caption_place = caption_low + caption_eot
    towers = (
        (
            image_tokens, image_low, image_high, image_low,
            image_gains.astype(F32), image_shifts.astype(F32), image_attn_in, image_attn_out,
            image_up, image_up_bias.astype(F32), image_down, image_proj,
        ),
        (
            caption_tokens, caption_low, caption_place + 1, caption_place,
            caption_gains.astype(F32), caption_shifts.astype(F32), caption_attn_in, caption_attn_out,
            caption_up, caption_up_bias.astype(F32), caption_down, caption_proj,
        ),
    )
    ahead = [attend_forward(t[0], t[1], t[2], t[3], t[4], t[5], t[6]) for t in towers]
    own = jnp.stack([ahead[0][0], ahead[0][1], ahead[1][0], ahead[1][1]])
    sent = [jnp.broadcast_to(own[None], (devices, *own.shape))]
    sent += [slices_out(a[2], count, 3 * width, devices) for a in ahead]
    got = exchange(sent)
    pairs = devices * count
    everyone = got[0].transpose(1, 0, 2, 3).reshape(4, pairs, width)
    blends = got[1:]

    units, kepts = [], []
    for k, t in enumerate(towers):
        unit, kept = pooled_forward(everyone[2 * k], everyone[2 * k + 1], t[4], t[5], t[7], t[8], t[9], t[10], t[11])
        units.append(unit)
        kepts.append(kept)
    scale = jnp.exp(logit_scale)
    logits = scale * dot(units[0], units[1], NT)
    row_top = jnp.max(logits, axis=1, keepdims=True)
    row_expo = jnp.exp(logits - row_top)
    row_sum = jnp.sum(row_expo, axis=1, keepdims=True)
    column_top = jnp.max(logits, axis=0, keepdims=True)
    column_expo = jnp.exp(logits - column_top)
    column_sum = jnp.sum(column_expo, axis=0, keepdims=True)
    diagonal = (
        lax.broadcasted_iota(jnp.int32, logits.shape, 0) == lax.broadcasted_iota(jnp.int32, logits.shape, 1)
    ).astype(F32)
    grad_logits = 0.5 * (row_expo / row_sum - diagonal) + 0.5 * (column_expo / column_sum - diagonal)
    total = (
        0.5 * jnp.sum(row_top + jnp.log(row_sum))
        + 0.5 * jnp.sum(column_top + jnp.log(column_sum))
        - jnp.sum(diagonal * logits)
    )
    scale_grad = jnp.sum(grad_logits * logits)
    grad_sim = (scale * grad_logits).astype(BF)
    grad_units = (dot(grad_sim, units[1]), dot(grad_sim, units[0], TN))

    backs, attends = [], []
    for k, t in enumerate(towers):
        back = pooled_backward(grad_units[k], kepts[k], t[4], t[7], t[8], t[10], t[11])
        backs.append(back)
        mine = lax.dynamic_slice_in_dim(back[0], index * count, count)
        mine_middle = lax.dynamic_slice_in_dim(back[1], index * count, count)
        attends.append(attend_backward(mine, mine_middle, ahead[k][3], t[4], t[5], t[6]))
    sent = []
    for a in attends:
        sent.append(jnp.broadcast_to(a[1][None], (devices, count, width)))
        sent.append(slices_out(a[2], count, 3 * width, devices))
        sent.append(jnp.broadcast_to(a[3].astype(BF)[None], (devices, 2, width)))
    got = exchange(sent)

    results = []
    for k, t in enumerate(towers):
        gains, shifts, attn_in = t[4], t[5], t[6]
        grad_query = got[3 * k].reshape(pairs, width)
        turns = got[3 * k + 1].reshape(pairs, heads, -1)
        blend = blends[k].reshape(pairs, heads, -1)
        sums = jnp.sum(got[3 * k + 2].astype(F32), axis=0)
        grad_mixed, _, gain_rows, shift_rows, up_bias_grad, factors = backs[k]
        second, act, post = kepts[k][2], kepts[k][5], kepts[k][8]
        grad_y, grad_pre, grad_z, grad_embed = factors
        pooled_normal, _ = normalize(everyone[2 * k].astype(F32))
        first_rows = (pooled_normal * gains[0] + shifts[0]).astype(BF)
        query = (dot(first_rows, attn_in[:, :width]) + shifts[1]).astype(BF)
        first, span, offset, part = window(width, 3 * width, devices, index)
        pieces = [dot(lax.dynamic_slice_in_dim(first_rows, first, span, 1), grad_query, TN)]
        for left, right, factor in ((turns, query, 0.125), (blend, grad_mixed, 1.0)):
            piece = jnp.einsum(
                "phc,phe->che", left, right.reshape(pairs, heads, HEAD), preferred_element_type=F32
            )
            pieces.append(factor * piece.reshape(span, width))
        attn_in_grad = finish(jnp.concatenate(pieces, axis=1), offset, part)
        query_shift = jnp.sum(grad_query.astype(F32), axis=0)
        gain_grad = jnp.stack([sums[0], gain_rows[0], gain_rows[1]])
        shift_grad = jnp.stack(
            [sums[1], query_shift, shift_rows[0], shift_rows[1], shift_rows[2], shift_rows[3], shift_rows[4]]
        )
        results.append(
            (
                gain_grad,
                shift_grad,
                attn_in_grad,
                cut(everyone[2 * k + 1], grad_y, devices, index),
                cut(second, grad_pre, devices, index),
                up_bias_grad,
                cut(act, grad_z, devices, index),
                cut(post, grad_embed, devices, index),
            )
        )
    return (total / pairs, attends[0][0], attends[1][0], *results[0], *results[1], scale_grad)


def solution(mesh):
    rows = P("dp", None)
    part = P("dp")
    whole = P()
    tower = (whole, whole, part, part, part, whole, part, part)
    return jax.shard_map(
        body,
        mesh=mesh,
        in_specs=(rows, whole, rows, part) + (whole,) * 17,
        out_specs=(whole, rows, rows, *tower, *tower, whole),
        check_vma=False,
    )
```

```python
from types import SimpleNamespace

import jax
import jax.numpy as jnp
from jax import lax
from jax.experimental import pallas as pl
from jax.experimental.pallas import tpu as pltpu
from jax.sharding import PartitionSpec as P

HEAD = 64
CTX = 77

LAYER_EPSILON = 1e-05
UNIT_EPSILON = 1e-06

BF = jnp.bfloat16
F32 = jnp.float32


def dot(left, right, dims=((1,), (0,))):
    return lax.dot_general(left.astype(BF), right.astype(BF), (dims, ((), ())), preferred_element_type=F32)


NT = ((1,), (1,))
TN = ((0,), (0,))


def normalize(values):
    centred = values - jnp.mean(values, axis=-1, keepdims=True)
    inverse = lax.rsqrt(jnp.mean(centred * centred, axis=-1, keepdims=True) + LAYER_EPSILON)
    return centred * inverse, inverse


def norm_back(incoming, normal, inverse, gain):
    scaled = incoming * gain
    return inverse * (
        scaled
        - jnp.mean(scaled, axis=-1, keepdims=True)
        - normal * jnp.mean(scaled * normal, axis=-1, keepdims=True)
    )


def head_mask(count, width):
    heads = width // HEAD
    rows = lax.broadcasted_iota(jnp.int32, (heads * count, width), 0) // count
    lanes = lax.broadcasted_iota(jnp.int32, (heads * count, width), 1) // HEAD
    return rows == lanes


def spread(values):
    count, width = values.shape
    tiled = jnp.tile(values, (width // HEAD, 1))
    return jnp.where(head_mask(count, width), tiled, jnp.zeros_like(tiled))


def collect(values, count):
    rows, width = values.shape
    kept = jnp.where(head_mask(count, width), values, 0.0)
    return jnp.sum(kept.reshape(rows // count, count, width), axis=0)


def attend_forward(tokens, low, high, place, gains, shifts, attn_in):
    rows, width = tokens.shape
    count = low.shape[0]
    heads = width // HEAD
    normal, inverse = normalize(tokens.astype(F32))
    normal_low = normal.astype(BF)
    picked = place[:, None] == jnp.arange(rows, dtype=jnp.int32)[None, :]
    pooled = dot(picked, tokens).astype(BF)
    pooled_normal, _ = normalize(pooled.astype(F32))
    first = (pooled_normal * gains[0] + shifts[0]).astype(BF)
    query = (dot(first, attn_in[:, :width]) + shifts[1]).astype(BF)
    key_back = dot(spread(query), attn_in[:, width : 2 * width], NT) * 0.125
    offset = jnp.sum(key_back * shifts[0], axis=-1, keepdims=True)
    scores = dot(key_back * gains[0], normal_low, NT) + offset
    columns = jnp.arange(rows, dtype=jnp.int32)[None, :]
    allowed = (columns >= jnp.tile(low, heads)[:, None]) & (columns < jnp.tile(high, heads)[:, None])
    scores = jnp.where(allowed, scores, -1e30)
    expo = jnp.where(allowed, jnp.exp(scores - jnp.max(scores, axis=-1, keepdims=True)), 0.0)
    probs = expo / jnp.sum(expo, axis=-1, keepdims=True)
    probs_low = probs.astype(BF)
    probs_sum = jnp.sum(probs_low.astype(F32), axis=-1, keepdims=True)
    blend_normal = dot(probs_low, normal_low)
    blend = blend_normal * gains[0] + shifts[0] * probs_sum
    mixed = collect(dot(blend, attn_in[:, 2 * width :]) + probs_sum * shifts[2], count).astype(BF)
    kept = (normal, inverse, normal_low, picked, pooled_normal, key_back, probs, probs_low, probs_sum, blend_normal)
    return pooled, mixed, blend.astype(BF), kept


def attend_backward(grad_mixed, grad_middle, kept, gains, shifts, attn_in):
    normal, inverse, normal_low, picked, pooled_normal, key_back, probs, probs_low, probs_sum, blend_normal = kept
    rows, width = normal.shape
    count = grad_mixed.shape[0]
    wide = spread(grad_mixed)
    value_back = dot(wide, attn_in[:, 2 * width :], NT)
    offset = jnp.sum(value_back * shifts[0] + wide.astype(F32) * shifts[2], axis=-1, keepdims=True)
    grad_probs = dot(value_back * gains[0], normal_low, NT) + offset
    grad_scores = probs * (grad_probs - jnp.sum(grad_probs * probs, axis=-1, keepdims=True))
    scores_low = grad_scores.astype(BF)
    scores_sum = jnp.sum(scores_low.astype(F32), axis=-1, keepdims=True)
    turn_normal = dot(scores_low, normal_low)
    turn = turn_normal * gains[0] + shifts[0] * scores_sum
    grad_query = (collect(dot(turn, attn_in[:, width : 2 * width]), count) * 0.125).astype(BF)
    query_back = dot(grad_query, attn_in[:, :width], NT)
    gain_part = (
        jnp.sum(turn_normal * key_back, axis=0)
        + jnp.sum(blend_normal * value_back, axis=0)
        + jnp.sum(pooled_normal * query_back, axis=0)
    )
    shift_part = (
        jnp.sum(scores_sum * key_back, axis=0)
        + jnp.sum(probs_sum * value_back, axis=0)
        + jnp.sum(query_back, axis=0)
    )
    grad_first = (
        dot(scores_low, key_back, TN) + dot(probs_low, value_back, TN) + dot(picked, query_back, TN)
    )
    high = grad_middle.astype(BF)
    rest = (grad_middle - high.astype(F32)).astype(BF)
    grad_tokens = (
        norm_back(grad_first, normal, inverse, gains[0]) + dot(picked, high, TN) + dot(picked, rest, TN)
    )
    return grad_tokens.astype(BF), grad_query, turn.astype(BF), jnp.stack([gain_part, shift_part])


def pooled_forward(pooled, mixed, gains, shifts, attn_out, up, up_bias, down, proj):
    middle = pooled.astype(F32) + dot(mixed, attn_out) + shifts[3]
    second_normal, second_inv = normalize(middle)
    second = (second_normal * gains[1] + shifts[4]).astype(BF)
    pre = dot(second, up) + up_bias
    gate = jax.nn.sigmoid(1.702 * pre)
    act = (pre * gate).astype(BF)
    out = middle + dot(act, down) + shifts[5]
    post_normal, post_inv = normalize(out)
    post = (post_normal * gains[2] + shifts[6]).astype(BF)
    embed = dot(post, proj)
    radius = lax.rsqrt(jnp.sum(embed * embed, axis=-1, keepdims=True) + UNIT_EPSILON)
    unit = (embed * radius).astype(BF)
    return unit, (second_normal, second_inv, second, pre, gate, act, post_normal, post_inv, post, embed, radius)


def pooled_backward(grad_unit, kept, gains, attn_out, up, down, proj):
    second_normal, second_inv, second, pre, gate, act, post_normal, post_inv, post, embed, radius = kept
    along = jnp.sum(embed * grad_unit, axis=-1, keepdims=True)
    grad_embed = (radius * grad_unit - radius * radius * radius * embed * along).astype(BF)
    grad_post = dot(grad_embed, proj, NT)
    grad_out = norm_back(grad_post, post_normal, post_inv, gains[2])
    grad_z = grad_out.astype(BF)
    slope = gate + 1.702 * pre * gate * (1.0 - gate)
    grad_pre = (dot(grad_z, down, NT) * slope).astype(BF)
    grad_second = dot(grad_pre, up, NT)
    grad_middle = grad_out + norm_back(grad_second, second_normal, second_inv, gains[1])
    grad_y = grad_middle.astype(BF)
    grad_mixed = dot(grad_y, attn_out, NT).astype(BF)
    gain_rows = (
        jnp.sum(grad_second * second_normal, axis=0),
        jnp.sum(grad_post * post_normal, axis=0),
    )

    def total(values):
        return jnp.sum(values.astype(F32), axis=0)

    shift_rows = (total(grad_mixed), total(grad_y), total(grad_second), total(grad_z), total(grad_post))
    return grad_mixed, grad_middle, gain_rows, shift_rows, total(grad_pre), (grad_y, grad_pre, grad_z, grad_embed)


def window(total_rows, columns, devices, index):
    part = total_rows * columns // devices
    start = index * part
    first = start // columns
    if part % columns == 0:
        span = part // columns
    else:
        span = max((d * part + part - 1) // columns - d * part // columns + 1 for d in range(devices))
    first = jnp.minimum(first, total_rows - span)
    return first, span, start - first * columns, part


def cut(left, right, devices, index):
    total_rows, columns = left.shape[1], right.shape[1]
    first, span, offset, part = window(total_rows, columns, devices, index)
    rows = dot(lax.dynamic_slice_in_dim(left, first, span, 1), right, TN)
    return finish(rows, offset, part)


def finish(rows, offset, part):
    flat = rows.reshape(-1)
    if flat.shape[0] == part:
        return flat
    return lax.dynamic_slice_in_dim(flat, offset, part)


def slices_out(values, count, columns, devices):
    width = values.shape[1]
    heads = values.shape[0] // count
    cuts = []
    if (width * columns // devices) % columns == 0:
        span = width // devices
        return values.reshape(heads, count, devices, span).transpose(2, 1, 0, 3)
    for d in range(devices):
        part = width * columns // devices
        span = max((e * part + part - 1) // columns - e * part // columns + 1 for e in range(devices))
        first = min(d * part // columns, width - span)
        cuts.append(values[:, first : first + span].reshape(heads, count, span).transpose(1, 0, 2))
    return jnp.stack(cuts)


def exchange(parts):
    devices = parts[0].shape[0]
    flat = jnp.concatenate([part.reshape(devices, -1).astype(BF) for part in parts], axis=1)
    got = lax.all_to_all(flat, "dp", 0, 0, tiled=True)
    outs = []
    at = 0
    for part in parts:
        size = part[0].size
        outs.append(got[:, at : at + size].reshape(part.shape))
        at += size
    return outs


def general_body(
    image_tokens,
    image_lengths,
    caption_tokens,
    caption_eot,
    image_gains,
    image_shifts,
    image_attn_in,
    image_attn_out,
    image_up,
    image_up_bias,
    image_down,
    image_proj,
    caption_gains,
    caption_shifts,
    caption_attn_in,
    caption_attn_out,
    caption_up,
    caption_up_bias,
    caption_down,
    caption_proj,
    logit_scale,
):
    index = lax.axis_index("dp")
    devices = lax.axis_size("dp")
    count = caption_eot.shape[0]
    width = image_tokens.shape[1]
    heads = width // HEAD
    lengths = lax.dynamic_slice_in_dim(image_lengths, index * count, count)
    image_high = jnp.cumsum(lengths)
    image_low = image_high - lengths
    caption_low = jnp.arange(count, dtype=jnp.int32) * CTX
    caption_place = caption_low + caption_eot
    towers = (
        (
            image_tokens, image_low, image_high, image_low,
            image_gains.astype(F32), image_shifts.astype(F32), image_attn_in, image_attn_out,
            image_up, image_up_bias.astype(F32), image_down, image_proj,
        ),
        (
            caption_tokens, caption_low, caption_place + 1, caption_place,
            caption_gains.astype(F32), caption_shifts.astype(F32), caption_attn_in, caption_attn_out,
            caption_up, caption_up_bias.astype(F32), caption_down, caption_proj,
        ),
    )
    ahead = [attend_forward(t[0], t[1], t[2], t[3], t[4], t[5], t[6]) for t in towers]
    own = jnp.stack([ahead[0][0], ahead[0][1], ahead[1][0], ahead[1][1]])
    sent = [jnp.broadcast_to(own[None], (devices, *own.shape))]
    sent += [slices_out(a[2], count, 3 * width, devices) for a in ahead]
    got = exchange(sent)
    pairs = devices * count
    everyone = got[0].transpose(1, 0, 2, 3).reshape(4, pairs, width)
    blends = got[1:]

    units, kepts = [], []
    for k, t in enumerate(towers):
        unit, kept = pooled_forward(everyone[2 * k], everyone[2 * k + 1], t[4], t[5], t[7], t[8], t[9], t[10], t[11])
        units.append(unit)
        kepts.append(kept)
    scale = jnp.exp(logit_scale)
    logits = scale * dot(units[0], units[1], NT)
    row_top = jnp.max(logits, axis=1, keepdims=True)
    row_expo = jnp.exp(logits - row_top)
    row_sum = jnp.sum(row_expo, axis=1, keepdims=True)
    column_top = jnp.max(logits, axis=0, keepdims=True)
    column_expo = jnp.exp(logits - column_top)
    column_sum = jnp.sum(column_expo, axis=0, keepdims=True)
    diagonal = (
        lax.broadcasted_iota(jnp.int32, logits.shape, 0) == lax.broadcasted_iota(jnp.int32, logits.shape, 1)
    ).astype(F32)
    grad_logits = 0.5 * (row_expo / row_sum - diagonal) + 0.5 * (column_expo / column_sum - diagonal)
    total = (
        0.5 * jnp.sum(row_top + jnp.log(row_sum))
        + 0.5 * jnp.sum(column_top + jnp.log(column_sum))
        - jnp.sum(diagonal * logits)
    )
    scale_grad = jnp.sum(grad_logits * logits)
    grad_sim = (scale * grad_logits).astype(BF)
    grad_units = (dot(grad_sim, units[1]), dot(grad_sim, units[0], TN))

    backs, attends = [], []
    for k, t in enumerate(towers):
        back = pooled_backward(grad_units[k], kepts[k], t[4], t[7], t[8], t[10], t[11])
        backs.append(back)
        mine = lax.dynamic_slice_in_dim(back[0], index * count, count)
        mine_middle = lax.dynamic_slice_in_dim(back[1], index * count, count)
        attends.append(attend_backward(mine, mine_middle, ahead[k][3], t[4], t[5], t[6]))
    sent = []
    for a in attends:
        sent.append(jnp.broadcast_to(a[1][None], (devices, count, width)))
        sent.append(slices_out(a[2], count, 3 * width, devices))
        sent.append(jnp.broadcast_to(a[3].astype(BF)[None], (devices, 2, width)))
    got = exchange(sent)

    results = []
    for k, t in enumerate(towers):
        gains, shifts, attn_in = t[4], t[5], t[6]
        grad_query = got[3 * k].reshape(pairs, width)
        turns = got[3 * k + 1].reshape(pairs, heads, -1)
        blend = blends[k].reshape(pairs, heads, -1)
        sums = jnp.sum(got[3 * k + 2].astype(F32), axis=0)
        grad_mixed, _, gain_rows, shift_rows, up_bias_grad, factors = backs[k]
        second, act, post = kepts[k][2], kepts[k][5], kepts[k][8]
        grad_y, grad_pre, grad_z, grad_embed = factors
        pooled_normal, _ = normalize(everyone[2 * k].astype(F32))
        first_rows = (pooled_normal * gains[0] + shifts[0]).astype(BF)
        query = (dot(first_rows, attn_in[:, :width]) + shifts[1]).astype(BF)
        first, span, offset, part = window(width, 3 * width, devices, index)
        pieces = [dot(lax.dynamic_slice_in_dim(first_rows, first, span, 1), grad_query, TN)]
        for left, right, factor in ((turns, query, 0.125), (blend, grad_mixed, 1.0)):
            piece = jnp.einsum(
                "phc,phe->che", left, right.reshape(pairs, heads, HEAD), preferred_element_type=F32
            )
            pieces.append(factor * piece.reshape(span, width))
        attn_in_grad = finish(jnp.concatenate(pieces, axis=1), offset, part)
        query_shift = jnp.sum(grad_query.astype(F32), axis=0)
        gain_grad = jnp.stack([sums[0], gain_rows[0], gain_rows[1]])
        shift_grad = jnp.stack(
            [sums[1], query_shift, shift_rows[0], shift_rows[1], shift_rows[2], shift_rows[3], shift_rows[4]]
        )
        results.append(
            (
                gain_grad,
                shift_grad,
                attn_in_grad,
                cut(everyone[2 * k + 1], grad_y, devices, index),
                cut(second, grad_pre, devices, index),
                up_bias_grad,
                cut(act, grad_z, devices, index),
                cut(post, grad_embed, devices, index),
            )
        )
    return (total / pairs, attends[0][0], attends[1][0], *results[0], *results[1], scale_grad)


COUNT_PAD = 8
NEG = -1e30


def refs_call(fn, ins, outs, scratch=(), smem=(), limit=None, cost=None):
    names = [*ins, *outs, *(name for name, _ in scratch)]

    def kernel(*refs):
        fn(SimpleNamespace(**dict(zip(names, refs))))

    results = pl.pallas_call(
        kernel,
        out_shape=tuple(outs.values()),
        in_specs=[pl.BlockSpec(memory_space=pltpu.SMEM if name in smem else pltpu.VMEM) for name in ins],
        out_specs=tuple(pl.BlockSpec(memory_space=pltpu.VMEM) for _ in outs),
        scratch_shapes=[shape for _, shape in scratch],
        compiler_params=pltpu.CompilerParams(vmem_limit_bytes=limit),
        cost_estimate=cost,
        name=fn.__name__,
    )(*ins.values())
    return SimpleNamespace(**dict(zip(outs, results)))


def iota(shape, axis):
    return lax.broadcasted_iota(jnp.int32, shape, axis)


def tiles(values, copies):
    return jnp.concatenate([values] * copies, axis=0)


def spread8(values):
    width = values.shape[1]
    heads = width // HEAD
    tiled = tiles(values, heads)
    keep = (iota(tiled.shape, 0) >> 3) == (iota(tiled.shape, 1) >> 6)
    return jnp.where(keep, tiled, 0.0).astype(BF)


def collect8(values):
    rows, width = values.shape
    total = None
    lane = iota((8, width), 1) >> 6
    for head in range(rows // 8):
        piece = jnp.where(lane == head, values[8 * head : 8 * head + 8], 0.0)
        total = piece if total is None else total + piece
    return total


def row_vector(scalars, rows, rest):
    place = iota((rows, 1), 0) & 7
    values = jnp.full((rows, 1), rest, jnp.int32)
    for k, scalar in enumerate(scalars):
        values = jnp.where(place == k, scalar, values)
    return values


def padded(rows):
    return -(-rows // 128) * 128


def ahead_tower(x, xs, normal, inverse, lows, highs, places, gains, shifts, attn_in, out):
    rows, width = x.shape
    full = normal.shape[0]
    size = 144 if rows % 144 < 16 else 112
    main = rows // size * size

    def norm_rows(at, count):
        raw = x[pl.ds(at, count), :]
        low_normal, inv = normalize(raw.astype(F32))
        xs[pl.ds(at, count), :] = raw
        normal[pl.ds(at, count), :] = low_normal.astype(BF)
        inverse[pl.ds(at, count), :] = inv

    @pl.loop(0, main // size)
    def _(step):
        norm_rows(pl.multiple_of(step * size, 16), size)

    xs[pl.ds(main, full - main), :] = jnp.zeros((full - main, width), BF)
    normal[pl.ds(main, full - main), :] = jnp.zeros((full - main, width), BF)
    inverse[pl.ds(main, full - main), :] = jnp.zeros((full - main, 1), F32)
    if rows > main:
        norm_rows(main, rows - main)

    gain, shift = gains[0:1, :].astype(F32), shifts[0:1, :].astype(F32)
    pick = (row_vector(places, 8, -1) == iota((8, full), 1)).astype(F32)
    pooled = dot(pick, xs[...])
    pooled_normal, _ = normalize(pooled)
    first = pooled_normal * gain + shift
    query = (dot(first, attn_in[:, :width]) + shifts[1:2, :].astype(F32)).astype(BF).astype(F32)
    key_back = dot(spread8(query), attn_in[:, width : 2 * width], NT) * 0.125
    offset = jnp.sum(key_back * shift, axis=-1, keepdims=True)
    scores = dot(key_back * gain, normal[...], NT) + offset
    rows_all = scores.shape[0]
    columns = iota(scores.shape, 1)
    allowed = (columns >= row_vector(lows, rows_all, 0)) & (columns < row_vector(highs, rows_all, 1))
    scores = jnp.where(allowed, scores, NEG)
    expo = jnp.where(allowed, jnp.exp(scores - jnp.max(scores, axis=-1, keepdims=True)), 0.0)
    probs = expo / jnp.sum(expo, axis=-1, keepdims=True)
    probs_low = probs.astype(BF)
    probs_sum = jnp.sum(probs_low.astype(F32), axis=-1, keepdims=True)
    blend_normal = dot(probs_low, normal[...])
    blend = blend_normal * gain + shift * probs_sum
    mixed = collect8(dot(blend, attn_in[:, 2 * width :]) + probs_sum * shifts[2:3, :].astype(F32))
    out("probs")[...] = probs
    out("pick")[...] = pick
    out("pooled_normal")[...] = pooled_normal
    out("key_back")[...] = key_back
    out("probs_sum")[...] = probs_sum
    out("blend_normal")[...] = blend_normal
    out("blend")[...] = blend
    return pooled, mixed


def slots(main, extra):
    row = iota(main.shape, 0)
    return jnp.where(row == 6, extra[0], jnp.where(row == 7, extra[1], main))


def ahead(r):
    me = lax.axis_index("dp")
    at = me * 6
    highs, lows, total = [], [], jnp.int32(0)
    for k in range(6):
        lows.append(total)
        total = total + r.lengths[at + k]
        highs.append(total)
    pooled, mixed = ahead_tower(
        r.x0, r.xs0, r.normal0, r.inverse0, lows, highs, lows, r.gains0, r.shifts0, r.attn_in0,
        lambda name: getattr(r, name + "0"),
    )
    lows = [k * CTX for k in range(6)]
    places = [k * CTX + r.eot[k] for k in range(6)]
    highs = [place + 1 for place in places]
    pooled1, mixed1 = ahead_tower(
        r.x1, r.xs1, r.normal1, r.inverse1, lows, highs, places, r.gains1, r.shifts1, r.attn_in1,
        lambda name: getattr(r, name + "1"),
    )
    width = pooled.shape[1]
    for b, main in enumerate((pooled, mixed, pooled1)):
        r.own[:, b * width : (b + 1) * width] = slots(main, (mixed1[b : b + 1], mixed1[3 + b : 4 + b])).astype(BF)


def packing(r, devices):
    width = r.blend0.shape[1]
    span = width // devices
    rows = devices * 8
    start = (iota((rows, width), 0) >> 3) * span
    lane = iota((rows, width), 1)
    keep = (lane >= start) & (lane < start + span)
    source = iota((width, 128), 0)
    inside = source - span * jnp.floor((source.astype(F32) + 0.5) / span).astype(jnp.int32)
    target = iota((width, 128), 1)
    for name in ("0", "1"):
        blend = getattr(r, "blend" + name)[...]
        total = None
        for head in range(width // HEAD):
            tall = jnp.where(keep, tiles(blend[8 * head : 8 * head + 8], devices), 0.0)
            place = (target == head * 16 + inside).astype(F32)
            piece = dot(tall, place)
            total = piece if total is None else total + piece
        getattr(r, "packed" + name)[...] = total.astype(BF)


def middle_tower(x, mixed, k, r):
    get = lambda name: getattr(r, name + k)
    gains, shifts = get("gains"), get("shifts")
    row = lambda ref, j: ref[j : j + 1, :].astype(F32)
    middle = x + dot(mixed, get("attn_out")[...]) + row(shifts, 3)
    second_normal, second_inv = normalize(middle)
    second = (second_normal * row(gains, 1) + row(shifts, 4)).astype(BF)
    get("second")[...] = second
    get("mixed")[...] = mixed.astype(BF)
    out = middle + row(shifts, 5)
    hidden = get("up").shape[1]
    for at in range(0, hidden, 256):
        cols = slice(at, at + 256)
        pre = dot(second, get("up")[:, cols]) + get("up_bias")[:, cols].astype(F32)
        gate = 1.0 / (1.0 + jnp.exp(-1.702 * pre))
        act = (pre * gate).astype(BF)
        get("act")[:, cols] = act
        get("slope")[:, cols] = gate + 1.702 * pre * gate * (1.0 - gate)
        out = out + dot(act, get("down")[cols, :])
    post_normal, post_inv = normalize(out)
    post = (post_normal * row(gains, 2) + row(shifts, 6)).astype(BF)
    get("post")[...] = post
    embed = dot(post, get("proj")[...])
    radius = lax.rsqrt(jnp.sum(embed * embed, axis=-1, keepdims=True) + UNIT_EPSILON)
    unit = (embed * radius).astype(BF)
    return unit, (second_normal, second_inv, post_normal, post_inv, embed, radius)


def total_row(values):
    return jnp.sum(values.astype(F32), axis=0, keepdims=True)


def middle_back(grad_unit, kept, k, r):
    second_normal, second_inv, post_normal, post_inv, embed, radius = kept
    get = lambda name: getattr(r, name + k)
    gains = get("gains")
    row = lambda ref, j: ref[j : j + 1, :].astype(F32)
    along = jnp.sum(embed * grad_unit, axis=-1, keepdims=True)
    grad_embed = (radius * grad_unit - radius * radius * radius * embed * along).astype(BF)
    get("grad_embed")[...] = grad_embed
    grad_post = dot(grad_embed, get("proj")[...], NT)
    grad_out = norm_back(grad_post, post_normal, post_inv, row(gains, 2))
    grad_z = grad_out.astype(BF)
    get("grad_z")[...] = grad_z
    grad_second = jnp.zeros_like(grad_out)
    for at in range(0, get("up").shape[1], 256):
        cols = slice(at, at + 256)
        grad_pre = (dot(grad_z, get("down")[cols, :], NT) * get("slope")[:, cols]).astype(BF)
        get("grad_pre")[:, cols] = grad_pre
        get("up_bias_grad")[:, cols] = total_row(grad_pre)
        grad_second = grad_second + dot(grad_pre, get("up")[:, cols], NT)
    grad_middle = grad_out + norm_back(grad_second, second_normal, second_inv, row(gains, 1))
    grad_y = grad_middle.astype(BF)
    get("grad_y")[...] = grad_y
    grad_mixed = dot(grad_y, get("attn_out")[...], NT).astype(BF)
    get("grad_mixed")[...] = grad_mixed
    r.full_mixed[...] = grad_mixed.astype(F32)
    r.full_middle[...] = grad_middle
    rows = (
        total_row(grad_second * second_normal),
        total_row(grad_post * post_normal),
        total_row(grad_mixed),
        total_row(grad_y),
        total_row(grad_second),
        total_row(grad_z),
        total_row(grad_post),
    )
    for j, value in enumerate(rows):
        get("rows")[j : j + 1, :] = value


def own_back(k, r):
    get = lambda name: getattr(r, name + k)
    attn_in, normal = get("attn_in"), get("normal")
    row = lambda ref, j: ref[j : j + 1, :].astype(F32)
    gain, shift = row(get("gains"), 0), row(get("shifts"), 0)
    width = gain.shape[1]
    mine = pl.ds(pl.multiple_of(lax.axis_index("dp") * 8, 8), 8)
    wide = spread8(r.full_mixed[mine, :])
    value_back = dot(wide, attn_in[:, 2 * width :], NT)
    offset = jnp.sum(value_back * shift + wide.astype(F32) * row(get("shifts"), 2), axis=-1, keepdims=True)
    grad_probs = dot(value_back * gain, normal[...], NT) + offset
    probs = get("probs")[...]
    grad_scores = probs * (grad_probs - jnp.sum(grad_probs * probs, axis=-1, keepdims=True))
    scores_low = grad_scores.astype(BF)
    scores_sum = jnp.sum(scores_low.astype(F32), axis=-1, keepdims=True)
    turn_normal = dot(scores_low, normal[...])
    turn = turn_normal * gain + shift * scores_sum
    grad_query = (collect8(dot(turn, attn_in[:, width : 2 * width])) * 0.125).astype(BF)
    query_back = dot(grad_query, attn_in[:, :width], NT)
    key_back, probs_sum = get("key_back")[...], get("probs_sum")[...]
    gain_part = total_row(
        turn_normal * key_back + get("blend_normal")[...] * value_back
    ) + total_row(get("pooled_normal")[...] * query_back)
    shift_part = total_row(scores_sum * key_back + probs_sum * value_back) + total_row(query_back)
    heads_rows = key_back.shape[0]
    get("weights")[0:heads_rows, :] = scores_low
    get("weights")[heads_rows : 2 * heads_rows, :] = probs.astype(BF)
    pick = get("pick")[...]
    get("weights")[2 * heads_rows : 2 * heads_rows + 16, :] = jnp.concatenate([pick, pick], axis=0).astype(BF)
    get("weights")[2 * heads_rows + 16 :, :] = jnp.zeros((128 - 2 * heads_rows - 16, probs.shape[1]), BF)
    mine_middle = r.full_middle[mine, :]
    high = mine_middle.astype(BF).astype(F32)
    empty = jnp.zeros((16, width), F32)
    get("terms")[:, :width] = jnp.concatenate(
        [key_back, value_back, query_back, jnp.zeros((128 - 2 * heads_rows - 8, width), F32)], axis=0
    ).astype(BF)
    get("terms")[:, width:] = jnp.concatenate(
        [jnp.zeros((2 * heads_rows, width), F32), high, mine_middle - high, empty], axis=0
    ).astype(BF)
    return turn, slots(grad_query.astype(F32), (gain_part, shift_part)).astype(BF)


def reverse_bits(value, bits):
    out = 0
    for k in range(bits):
        out |= ((value >> k) & 1) << (bits - 1 - k)
    return out


def centre(r, devices):
    width = r.attn_out0.shape[0]
    me = lax.axis_index("dp")
    bits = devices.bit_length() - 1
    rows = devices * 8
    for block in range(devices):
        at = pl.ds(pl.multiple_of((me ^ reverse_bits(block, bits)) * 8, 8), 8)
        r.everyone[at, :] = r.gathered[block].astype(F32)
    row = iota((rows, width), 0)
    real = (row & 7) < 6
    parts = [jnp.where(real, r.everyone[:, b * width : (b + 1) * width], 0.0) for b in range(3)]
    caption_mixed = None
    to, source = iota((rows, rows), 0), iota((rows, rows), 1)
    for b in range(3):
        slot = to & 7
        near = source - (to - slot)
        chosen = ((slot == b) & (near == 6)) | ((slot == 3 + b) & (near == 7))
        piece = dot(chosen.astype(F32), r.everyone[:, b * width : (b + 1) * width])
        caption_mixed = piece if caption_mixed is None else caption_mixed + piece
    r.pooled0[...] = parts[0].astype(BF)
    r.pooled1[...] = parts[2].astype(BF)
    unit0, kept0 = middle_tower(parts[0], parts[1], "0", r)
    unit1, kept1 = middle_tower(parts[2], caption_mixed, "1", r)
    scale = jnp.exp(r.logit_scale[...])
    raw = scale * dot(unit0, unit1, NT)
    row_real, column_real = (to & 7) < 6, (source & 7) < 6
    both = row_real & column_real
    logits = jnp.where(both, raw, NEG)
    row_top = jnp.max(logits, axis=1, keepdims=True)
    row_expo = jnp.exp(logits - row_top)
    row_total = jnp.sum(row_expo, axis=1, keepdims=True)
    column_top = jnp.max(logits, axis=0, keepdims=True)
    column_expo = jnp.exp(logits - column_top)
    column_total = jnp.sum(column_expo, axis=0, keepdims=True)
    diagonal = (to == source).astype(F32)
    grad_logits = jnp.where(
        both,
        0.5 * (row_expo / row_total - diagonal) + 0.5 * (column_expo / column_total - diagonal),
        0.0,
    )
    row_part = jnp.where((iota((rows, 1), 0) & 7) < 6, row_top + jnp.log(row_total), 0.0)
    column_part = jnp.where((iota((1, rows), 1) & 7) < 6, column_top + jnp.log(column_total), 0.0)
    on_diagonal = jnp.where(both, diagonal * raw, 0.0)
    whole = lambda values: jnp.sum(jnp.sum(values, axis=1, keepdims=True), axis=0, keepdims=True)
    total = 0.5 * whole(row_part) + 0.5 * whole(column_part) - whole(on_diagonal)
    r.loss[...] = total / (devices * 6)
    r.scale_grad[...] = whole(grad_logits * jnp.where(both, raw, 0.0))
    grad_sim = (scale * grad_logits).astype(BF)
    middle_back(dot(grad_sim, unit1), kept0, "0", r)
    turn0, query0 = own_back("0", r)
    middle_back(dot(grad_sim, unit0, TN), kept1, "1", r)
    turn1, query1 = own_back("1", r)
    packed = SimpleNamespace(blend0=turn0, blend1=turn1, packed0=r.turned0, packed1=r.turned1)
    packing(packed, devices)
    for d in range(devices):
        r.message[d, :, :width] = query0
        r.message[d, :, width : 2 * width] = query1
    for j, ref in enumerate((r.turned0, r.turned1, r.packed0, r.packed1)):
        lanes = slice(2 * width + 128 * j, 2 * width + 128 * (j + 1))
        r.message[:, :, lanes] = ref[...].reshape(devices, 8, 128)


def store_flat(ref, values):
    span, columns = values.shape
    steps = columns // 128
    for c in range(steps):
        ref[pl.ds(c, span, stride=steps), :] = values[:, 128 * c : 128 * (c + 1)]


def picked_rows(first, span, total):
    tall = -(-span // 16) * 16
    near = iota((tall, total), 1) - first
    return ((near == iota((tall, total), 0)) & (near < span)).astype(F32)


def aside_tower(k, r, devices):
    get = lambda name: getattr(r, name + k)
    me = lax.axis_index("dp")
    width = get("gains").shape[1]
    for left, right, out in (
        ("mixed", "grad_y", "attn_out_grad"),
        ("second", "grad_pre", "up_grad"),
        ("act", "grad_z", "down_grad"),
        ("post", "grad_embed", "proj_grad"),
    ):
        depth = get(left).shape[1]
        span = depth // devices
        chosen = picked_rows(me * span, span, depth)
        cut_rows = dot(chosen, get(left)[...], NT)
        store_flat(get(out), dot(cut_rows, get(right)[...])[:span])
    gain, shift = get("gains")[0:1, :].astype(F32), get("shifts")[0:1, :].astype(F32)
    pooled_normal, _ = normalize(get("pooled")[...].astype(F32))
    first = (pooled_normal * gain + shift).astype(BF)
    get("query")[...] = (dot(first, get("attn_in")[:, :width]) + get("shifts")[1:2, :].astype(F32)).astype(BF)
    span = width // devices
    get("first_cut")[...] = dot(picked_rows(me * span, span, width), first, NT).astype(BF)

    tokens_out = get("grad_tokens")
    rows = tokens_out.shape[0]
    for at in range(0, rows, 128):
        count = min(128, rows - at)
        both = dot(get("weights")[:, at : at + 128], get("terms")[...], TN)
        grad_first, direct = both[:, :width], both[:, width:]
        normal = get("normal")[at : at + 128, :].astype(F32)
        values = norm_back(grad_first, normal, get("inverse")[at : at + 128, :], gain) + direct
        tokens_out[at : at + count, :] = values[:count].astype(BF)


def aside(r, devices):
    for k in ("0", "1"):
        aside_tower(k, r, devices)


def ending_tower(k, at, r, devices):
    get = lambda name: getattr(r, name + k)
    width = get("query").shape[1]
    heads = width // HEAD
    span = width // devices
    rows = devices * 8
    raw = r.got[:, :, at * width : (at + 1) * width].astype(F32).reshape(rows, width)
    slot = iota((rows, width), 0) & 7
    grad_query = jnp.where(slot < 6, raw, 0.0)
    kind, place = iota((8, rows), 0), iota((8, rows), 1) & 7
    chooser = ((kind == 0) & (place == 6)) | ((kind == 1) & (place == 7)) | ((kind == 2) & (place < 6))
    sums = dot(chosen_float(chooser), raw)
    pieces = [dot(get("first_cut")[...], grad_query)]
    for j, right, factor in ((at, "query", 0.125), (2 + at, "grad_mixed", 1.0)):
        lanes = slice(2 * width + 128 * j, 2 * width + 128 * (j + 1))
        left = r.got[:, :, lanes].astype(F32).reshape(rows, 128)
        tall = dot(left, get(right)[...], TN)
        lane = iota((16, width), 1) >> 6
        total = None
        for head in range(heads):
            piece = jnp.where(lane == head, tall[16 * head : 16 * head + 16], 0.0)
            total = piece if total is None else total + piece
        pieces.append(factor * total)
    flat = get("attn_in_grad")
    steps = 3 * width // 128
    for part, values in enumerate(pieces):
        for c in range(width // 128):
            flat[pl.ds(part * (width // 128) + c, span, stride=steps), :] = values[:span, 128 * c : 128 * (c + 1)]
    got_rows = get("rows")[...]
    get("gains_grad")[...] = jnp.concatenate([sums[0:1], got_rows[0:2]], axis=0)
    get("shifts_grad")[...] = jnp.concatenate([sums[1:2], sums[2:3], got_rows[2:7]], axis=0)


def chosen_float(mask):
    return jnp.where(mask, 1.0, 0.0)


def ending(r, devices):
    ending_tower("0", 0, r, devices)
    ending_tower("1", 1, r, devices)


def small_body(args, devices):
    (
        image_tokens, image_lengths, caption_tokens, caption_eot,
        *weights, logit_scale,
    ) = args
    names = ("gains", "shifts", "attn_in", "attn_out", "up", "up_bias", "down", "proj")
    w = {}
    for k in range(2):
        for j, name in enumerate(names):
            value = weights[8 * k + j]
            w[f"{name}{k}"] = value[None] if name == "up_bias" else value
    width = image_tokens.shape[1]
    heads = width // HEAD
    hidden = w["up0"].shape[1]
    rows = devices * 8
    span = width // devices
    struct = jax.ShapeDtypeStruct
    both = ("0", "1")
    full = {"0": padded(image_tokens.shape[0]), "1": padded(caption_tokens.shape[0])}
    hr = heads * 8

    outs = {"own": struct((8, 3 * width), BF)}
    for k in both:
        outs |= {
            "normal" + k: struct((full[k], width), BF),
            "inverse" + k: struct((full[k], 1), F32),
            "probs" + k: struct((hr, full[k]), F32),
            "pick" + k: struct((8, full[k]), F32),
            "pooled_normal" + k: struct((8, width), F32),
            "key_back" + k: struct((hr, width), F32),
            "probs_sum" + k: struct((hr, 1), F32),
            "blend_normal" + k: struct((hr, width), F32),
            "blend" + k: struct((hr, width), F32),
        }
    take = lambda space, *keys: {f"{key}{k}": (space[f"{key}{k}"] if isinstance(space, dict) else getattr(space, f"{key}{k}")) for key in keys for k in both}
    a = refs_call(
        ahead,
        {"lengths": image_lengths, "eot": caption_eot, "x0": image_tokens, "x1": caption_tokens, **take(w, "gains", "shifts", "attn_in")},
        outs,
        scratch=[("xs" + k, pltpu.VMEM((full[k], width), BF)) for k in both],
        smem=("lengths", "eot"),
    )

    gathered = a.own[None]
    bit = devices // 2
    while bit:
        other = lax.ppermute(gathered, "dp", [(d, d ^ bit) for d in range(devices)])
        gathered = jnp.concatenate([gathered, other], axis=0)
        bit //= 2

    def pack_blend(r):
        packing(r, devices)

    p = refs_call(
        pack_blend, take(a, "blend"), {"packed" + k: struct((rows, 128), BF) for k in both},
        cost=pl.CostEstimate(flops=2 * 12 * rows * width * 128, bytes_accessed=400000, transcendentals=0),
    )

    outs = {
        "message": struct((devices, 8, 2 * width + 512), BF),
        "loss": struct((1, 1), F32),
        "scale_grad": struct((1, 1), F32),
    }
    scratch = [
        ("everyone", pltpu.VMEM((rows, 3 * width), F32)),
        ("full_mixed", pltpu.VMEM((rows, width), F32)),
        ("full_middle", pltpu.VMEM((rows, width), F32)),
    ]
    for k in both:
        outs |= {name + k: struct((rows, width), BF) for name in ("pooled", "mixed", "second", "post", "grad_embed", "grad_z", "grad_y", "grad_mixed")}
        outs |= {name + k: struct((rows, hidden), BF) for name in ("act", "grad_pre")}
        outs |= {
            "up_bias_grad" + k: struct((1, hidden), F32),
            "rows" + k: struct((7, width), F32),
            "weights" + k: struct((128, full[k]), BF),
            "terms" + k: struct((128, 2 * width), BF),
        }
        scratch += [("slope" + k, pltpu.VMEM((rows, hidden), F32)), ("turned" + k, pltpu.VMEM((rows, 128), BF))]

    def centre_all(r):
        centre(r, devices)

    b = refs_call(
        centre_all,
        {
            "gathered": gathered,
            "logit_scale": logit_scale.reshape(1, 1),
            **w,
            **take(a, "normal", "probs", "pick", "pooled_normal", "key_back", "probs_sum", "blend_normal"),
            **take(p, "packed"),
        },
        outs,
        scratch=scratch,
        limit=60 * 1024 * 1024,
    )
    got = lax.all_to_all(b.message, "dp", 0, 0, tiled=True)

    outs = {"grad_tokens0": struct(image_tokens.shape, BF), "grad_tokens1": struct(caption_tokens.shape, BF)}
    for k in both:
        outs |= {
            "attn_out_grad" + k: struct((width // devices * width // 128, 128), F32),
            "up_grad" + k: struct((width // devices * hidden // 128, 128), F32),
            "down_grad" + k: struct((hidden // devices * width // 128, 128), F32),
            "proj_grad" + k: struct((width // devices * width // 128, 128), F32),
            "query" + k: struct((rows, width), BF),
            "first_cut" + k: struct((16, rows), BF),
        }

    def aside_all(r):
        aside(r, devices)

    e = refs_call(
        aside_all,
        {
            **take(w, "gains", "shifts", "attn_in"),
            **take(a, "normal", "inverse"),
            **take(b, "pooled", "mixed", "second", "post", "grad_embed", "grad_z", "grad_y", "act", "grad_pre", "weights", "terms"),
        },
        outs,
        cost=pl.CostEstimate(flops=2 * 10**9, bytes_accessed=8 * 10**6, transcendentals=0),
    )

    outs = {}
    for k in both:
        outs |= {
            "attn_in_grad" + k: struct((span * 3 * width // 128, 128), F32),
            "gains_grad" + k: struct((3, width), F32),
            "shifts_grad" + k: struct((7, width), F32),
        }

    def ending_all(r):
        ending(r, devices)

    d = refs_call(
        ending_all,
        {"got": got, **take(e, "query", "first_cut"), **take(b, "grad_mixed", "rows")},
        outs,
    )
    results = []
    for k in both:
        pick = lambda space, name: getattr(space, name + k)
        results += [
            pick(d, "gains_grad"), pick(d, "shifts_grad"), pick(d, "attn_in_grad").reshape(-1),
            pick(e, "attn_out_grad").reshape(-1), pick(e, "up_grad").reshape(-1), pick(b, "up_bias_grad").reshape(-1),
            pick(e, "down_grad").reshape(-1), pick(e, "proj_grad").reshape(-1),
        ]
    return (b.loss.reshape(()), e.grad_tokens0, e.grad_tokens1, *results, b.scale_grad.reshape(()))


def fits(args, devices):
    width = args[0].shape[1]
    return (
        devices & (devices - 1) == 0
        and width % devices == 0
        and width // devices <= 16
        and devices * 8 <= 512
        and args[3].shape[0] == 6
    )


def body(*args):
    devices = lax.axis_size("dp")
    if fits(args, devices):
        return small_body(args, devices)
    return general_body(*args)


def solution(mesh):
    rows = P("dp", None)
    part = P("dp")
    whole = P()
    tower = (whole, whole, part, part, part, whole, part, part)
    return jax.shard_map(
        body,
        mesh=mesh,
        in_specs=(rows, whole, rows, part) + (whole,) * 17,
        out_specs=(whole, rows, rows, *tower, *tower, whole),
        check_vma=False,
    )
```

```python
from types import SimpleNamespace

import jax
import jax.numpy as jnp
from jax import lax
from jax.experimental import pallas as pl
from jax.experimental.pallas import tpu as pltpu
from jax.sharding import PartitionSpec as P

HEAD = 64
CTX = 77

LAYER_EPSILON = 1e-05
UNIT_EPSILON = 1e-06

BF = jnp.bfloat16
F32 = jnp.float32


def dot(left, right, dims=((1,), (0,))):
    return lax.dot_general(left.astype(BF), right.astype(BF), (dims, ((), ())), preferred_element_type=F32)


NT = ((1,), (1,))
TN = ((0,), (0,))


def normalize(values):
    centred = values - jnp.mean(values, axis=-1, keepdims=True)
    inverse = lax.rsqrt(jnp.mean(centred * centred, axis=-1, keepdims=True) + LAYER_EPSILON)
    return centred * inverse, inverse


def norm_back(incoming, normal, inverse, gain):
    scaled = incoming * gain
    return inverse * (
        scaled
        - jnp.mean(scaled, axis=-1, keepdims=True)
        - normal * jnp.mean(scaled * normal, axis=-1, keepdims=True)
    )


def head_mask(count, width):
    heads = width // HEAD
    rows = lax.broadcasted_iota(jnp.int32, (heads * count, width), 0) // count
    lanes = lax.broadcasted_iota(jnp.int32, (heads * count, width), 1) // HEAD
    return rows == lanes


def spread(values):
    count, width = values.shape
    tiled = jnp.tile(values, (width // HEAD, 1))
    return jnp.where(head_mask(count, width), tiled, jnp.zeros_like(tiled))


def collect(values, count):
    rows, width = values.shape
    kept = jnp.where(head_mask(count, width), values, 0.0)
    return jnp.sum(kept.reshape(rows // count, count, width), axis=0)


def attend_forward(tokens, low, high, place, gains, shifts, attn_in):
    rows, width = tokens.shape
    count = low.shape[0]
    heads = width // HEAD
    normal, inverse = normalize(tokens.astype(F32))
    normal_low = normal.astype(BF)
    picked = place[:, None] == jnp.arange(rows, dtype=jnp.int32)[None, :]
    pooled = dot(picked, tokens).astype(BF)
    pooled_normal, _ = normalize(pooled.astype(F32))
    first = (pooled_normal * gains[0] + shifts[0]).astype(BF)
    query = (dot(first, attn_in[:, :width]) + shifts[1]).astype(BF)
    key_back = dot(spread(query), attn_in[:, width : 2 * width], NT) * 0.125
    offset = jnp.sum(key_back * shifts[0], axis=-1, keepdims=True)
    scores = dot(key_back * gains[0], normal_low, NT) + offset
    columns = jnp.arange(rows, dtype=jnp.int32)[None, :]
    allowed = (columns >= jnp.tile(low, heads)[:, None]) & (columns < jnp.tile(high, heads)[:, None])
    scores = jnp.where(allowed, scores, -1e30)
    expo = jnp.where(allowed, jnp.exp(scores - jnp.max(scores, axis=-1, keepdims=True)), 0.0)
    probs = expo / jnp.sum(expo, axis=-1, keepdims=True)
    probs_low = probs.astype(BF)
    probs_sum = jnp.sum(probs_low.astype(F32), axis=-1, keepdims=True)
    blend_normal = dot(probs_low, normal_low)
    blend = blend_normal * gains[0] + shifts[0] * probs_sum
    mixed = collect(dot(blend, attn_in[:, 2 * width :]) + probs_sum * shifts[2], count).astype(BF)
    kept = (normal, inverse, normal_low, picked, pooled_normal, key_back, probs, probs_low, probs_sum, blend_normal)
    return pooled, mixed, blend.astype(BF), kept


def attend_backward(grad_mixed, grad_middle, kept, gains, shifts, attn_in):
    normal, inverse, normal_low, picked, pooled_normal, key_back, probs, probs_low, probs_sum, blend_normal = kept
    rows, width = normal.shape
    count = grad_mixed.shape[0]
    wide = spread(grad_mixed)
    value_back = dot(wide, attn_in[:, 2 * width :], NT)
    offset = jnp.sum(value_back * shifts[0] + wide.astype(F32) * shifts[2], axis=-1, keepdims=True)
    grad_probs = dot(value_back * gains[0], normal_low, NT) + offset
    grad_scores = probs * (grad_probs - jnp.sum(grad_probs * probs, axis=-1, keepdims=True))
    scores_low = grad_scores.astype(BF)
    scores_sum = jnp.sum(scores_low.astype(F32), axis=-1, keepdims=True)
    turn_normal = dot(scores_low, normal_low)
    turn = turn_normal * gains[0] + shifts[0] * scores_sum
    grad_query = (collect(dot(turn, attn_in[:, width : 2 * width]), count) * 0.125).astype(BF)
    query_back = dot(grad_query, attn_in[:, :width], NT)
    gain_part = (
        jnp.sum(turn_normal * key_back, axis=0)
        + jnp.sum(blend_normal * value_back, axis=0)
        + jnp.sum(pooled_normal * query_back, axis=0)
    )
    shift_part = (
        jnp.sum(scores_sum * key_back, axis=0)
        + jnp.sum(probs_sum * value_back, axis=0)
        + jnp.sum(query_back, axis=0)
    )
    grad_first = (
        dot(scores_low, key_back, TN) + dot(probs_low, value_back, TN) + dot(picked, query_back, TN)
    )
    high = grad_middle.astype(BF)
    rest = (grad_middle - high.astype(F32)).astype(BF)
    grad_tokens = (
        norm_back(grad_first, normal, inverse, gains[0]) + dot(picked, high, TN) + dot(picked, rest, TN)
    )
    return grad_tokens.astype(BF), grad_query, turn.astype(BF), jnp.stack([gain_part, shift_part])


def pooled_forward(pooled, mixed, gains, shifts, attn_out, up, up_bias, down, proj):
    middle = pooled.astype(F32) + dot(mixed, attn_out) + shifts[3]
    second_normal, second_inv = normalize(middle)
    second = (second_normal * gains[1] + shifts[4]).astype(BF)
    pre = dot(second, up) + up_bias
    gate = jax.nn.sigmoid(1.702 * pre)
    act = (pre * gate).astype(BF)
    out = middle + dot(act, down) + shifts[5]
    post_normal, post_inv = normalize(out)
    post = (post_normal * gains[2] + shifts[6]).astype(BF)
    embed = dot(post, proj)
    radius = lax.rsqrt(jnp.sum(embed * embed, axis=-1, keepdims=True) + UNIT_EPSILON)
    unit = (embed * radius).astype(BF)
    return unit, (second_normal, second_inv, second, pre, gate, act, post_normal, post_inv, post, embed, radius)


def pooled_backward(grad_unit, kept, gains, attn_out, up, down, proj):
    second_normal, second_inv, second, pre, gate, act, post_normal, post_inv, post, embed, radius = kept
    along = jnp.sum(embed * grad_unit, axis=-1, keepdims=True)
    grad_embed = (radius * grad_unit - radius * radius * radius * embed * along).astype(BF)
    grad_post = dot(grad_embed, proj, NT)
    grad_out = norm_back(grad_post, post_normal, post_inv, gains[2])
    grad_z = grad_out.astype(BF)
    slope = gate + 1.702 * pre * gate * (1.0 - gate)
    grad_pre = (dot(grad_z, down, NT) * slope).astype(BF)
    grad_second = dot(grad_pre, up, NT)
    grad_middle = grad_out + norm_back(grad_second, second_normal, second_inv, gains[1])
    grad_y = grad_middle.astype(BF)
    grad_mixed = dot(grad_y, attn_out, NT).astype(BF)
    gain_rows = (
        jnp.sum(grad_second * second_normal, axis=0),
        jnp.sum(grad_post * post_normal, axis=0),
    )

    def total(values):
        return jnp.sum(values.astype(F32), axis=0)

    shift_rows = (total(grad_mixed), total(grad_y), total(grad_second), total(grad_z), total(grad_post))
    return grad_mixed, grad_middle, gain_rows, shift_rows, total(grad_pre), (grad_y, grad_pre, grad_z, grad_embed)


def window(total_rows, columns, devices, index):
    part = total_rows * columns // devices
    start = index * part
    first = start // columns
    if part % columns == 0:
        span = part // columns
    else:
        span = max((d * part + part - 1) // columns - d * part // columns + 1 for d in range(devices))
    first = jnp.minimum(first, total_rows - span)
    return first, span, start - first * columns, part


def cut(left, right, devices, index):
    total_rows, columns = left.shape[1], right.shape[1]
    first, span, offset, part = window(total_rows, columns, devices, index)
    rows = dot(lax.dynamic_slice_in_dim(left, first, span, 1), right, TN)
    return finish(rows, offset, part)


def finish(rows, offset, part):
    flat = rows.reshape(-1)
    if flat.shape[0] == part:
        return flat
    return lax.dynamic_slice_in_dim(flat, offset, part)


def slices_out(values, count, columns, devices):
    width = values.shape[1]
    heads = values.shape[0] // count
    cuts = []
    if (width * columns // devices) % columns == 0:
        span = width // devices
        return values.reshape(heads, count, devices, span).transpose(2, 1, 0, 3)
    for d in range(devices):
        part = width * columns // devices
        span = max((e * part + part - 1) // columns - e * part // columns + 1 for e in range(devices))
        first = min(d * part // columns, width - span)
        cuts.append(values[:, first : first + span].reshape(heads, count, span).transpose(1, 0, 2))
    return jnp.stack(cuts)


def exchange(parts):
    devices = parts[0].shape[0]
    flat = jnp.concatenate([part.reshape(devices, -1).astype(BF) for part in parts], axis=1)
    got = lax.all_to_all(flat, "dp", 0, 0, tiled=True)
    outs = []
    at = 0
    for part in parts:
        size = part[0].size
        outs.append(got[:, at : at + size].reshape(part.shape))
        at += size
    return outs


def general_body(
    image_tokens,
    image_lengths,
    caption_tokens,
    caption_eot,
    image_gains,
    image_shifts,
    image_attn_in,
    image_attn_out,
    image_up,
    image_up_bias,
    image_down,
    image_proj,
    caption_gains,
    caption_shifts,
    caption_attn_in,
    caption_attn_out,
    caption_up,
    caption_up_bias,
    caption_down,
    caption_proj,
    logit_scale,
):
    index = lax.axis_index("dp")
    devices = lax.axis_size("dp")
    count = caption_eot.shape[0]
    width = image_tokens.shape[1]
    heads = width // HEAD
    lengths = lax.dynamic_slice_in_dim(image_lengths, index * count, count)
    image_high = jnp.cumsum(lengths)
    image_low = image_high - lengths
    caption_low = jnp.arange(count, dtype=jnp.int32) * CTX
    caption_place = caption_low + caption_eot
    towers = (
        (
            image_tokens, image_low, image_high, image_low,
            image_gains.astype(F32), image_shifts.astype(F32), image_attn_in, image_attn_out,
            image_up, image_up_bias.astype(F32), image_down, image_proj,
        ),
        (
            caption_tokens, caption_low, caption_place + 1, caption_place,
            caption_gains.astype(F32), caption_shifts.astype(F32), caption_attn_in, caption_attn_out,
            caption_up, caption_up_bias.astype(F32), caption_down, caption_proj,
        ),
    )
    ahead = [attend_forward(t[0], t[1], t[2], t[3], t[4], t[5], t[6]) for t in towers]
    own = jnp.stack([ahead[0][0], ahead[0][1], ahead[1][0], ahead[1][1]])
    sent = [jnp.broadcast_to(own[None], (devices, *own.shape))]
    sent += [slices_out(a[2], count, 3 * width, devices) for a in ahead]
    got = exchange(sent)
    pairs = devices * count
    everyone = got[0].transpose(1, 0, 2, 3).reshape(4, pairs, width)
    blends = got[1:]

    units, kepts = [], []
    for k, t in enumerate(towers):
        unit, kept = pooled_forward(everyone[2 * k], everyone[2 * k + 1], t[4], t[5], t[7], t[8], t[9], t[10], t[11])
        units.append(unit)
        kepts.append(kept)
    scale = jnp.exp(logit_scale)
    logits = scale * dot(units[0], units[1], NT)
    row_top = jnp.max(logits, axis=1, keepdims=True)
    row_expo = jnp.exp(logits - row_top)
    row_sum = jnp.sum(row_expo, axis=1, keepdims=True)
    column_top = jnp.max(logits, axis=0, keepdims=True)
    column_expo = jnp.exp(logits - column_top)
    column_sum = jnp.sum(column_expo, axis=0, keepdims=True)
    diagonal = (
        lax.broadcasted_iota(jnp.int32, logits.shape, 0) == lax.broadcasted_iota(jnp.int32, logits.shape, 1)
    ).astype(F32)
    grad_logits = 0.5 * (row_expo / row_sum - diagonal) + 0.5 * (column_expo / column_sum - diagonal)
    total = (
        0.5 * jnp.sum(row_top + jnp.log(row_sum))
        + 0.5 * jnp.sum(column_top + jnp.log(column_sum))
        - jnp.sum(diagonal * logits)
    )
    scale_grad = jnp.sum(grad_logits * logits)
    grad_sim = (scale * grad_logits).astype(BF)
    grad_units = (dot(grad_sim, units[1]), dot(grad_sim, units[0], TN))

    backs, attends = [], []
    for k, t in enumerate(towers):
        back = pooled_backward(grad_units[k], kepts[k], t[4], t[7], t[8], t[10], t[11])
        backs.append(back)
        mine = lax.dynamic_slice_in_dim(back[0], index * count, count)
        mine_middle = lax.dynamic_slice_in_dim(back[1], index * count, count)
        attends.append(attend_backward(mine, mine_middle, ahead[k][3], t[4], t[5], t[6]))
    sent = []
    for a in attends:
        sent.append(jnp.broadcast_to(a[1][None], (devices, count, width)))
        sent.append(slices_out(a[2], count, 3 * width, devices))
        sent.append(jnp.broadcast_to(a[3].astype(BF)[None], (devices, 2, width)))
    got = exchange(sent)

    results = []
    for k, t in enumerate(towers):
        gains, shifts, attn_in = t[4], t[5], t[6]
        grad_query = got[3 * k].reshape(pairs, width)
        turns = got[3 * k + 1].reshape(pairs, heads, -1)
        blend = blends[k].reshape(pairs, heads, -1)
        sums = jnp.sum(got[3 * k + 2].astype(F32), axis=0)
        grad_mixed, _, gain_rows, shift_rows, up_bias_grad, factors = backs[k]
        second, act, post = kepts[k][2], kepts[k][5], kepts[k][8]
        grad_y, grad_pre, grad_z, grad_embed = factors
        pooled_normal, _ = normalize(everyone[2 * k].astype(F32))
        first_rows = (pooled_normal * gains[0] + shifts[0]).astype(BF)
        query = (dot(first_rows, attn_in[:, :width]) + shifts[1]).astype(BF)
        first, span, offset, part = window(width, 3 * width, devices, index)
        pieces = [dot(lax.dynamic_slice_in_dim(first_rows, first, span, 1), grad_query, TN)]
        for left, right, factor in ((turns, query, 0.125), (blend, grad_mixed, 1.0)):
            piece = jnp.einsum(
                "phc,phe->che", left, right.reshape(pairs, heads, HEAD), preferred_element_type=F32
            )
            pieces.append(factor * piece.reshape(span, width))
        attn_in_grad = finish(jnp.concatenate(pieces, axis=1), offset, part)
        query_shift = jnp.sum(grad_query.astype(F32), axis=0)
        gain_grad = jnp.stack([sums[0], gain_rows[0], gain_rows[1]])
        shift_grad = jnp.stack(
            [sums[1], query_shift, shift_rows[0], shift_rows[1], shift_rows[2], shift_rows[3], shift_rows[4]]
        )
        results.append(
            (
                gain_grad,
                shift_grad,
                attn_in_grad,
                cut(everyone[2 * k + 1], grad_y, devices, index),
                cut(second, grad_pre, devices, index),
                up_bias_grad,
                cut(act, grad_z, devices, index),
                cut(post, grad_embed, devices, index),
            )
        )
    return (total / pairs, attends[0][0], attends[1][0], *results[0], *results[1], scale_grad)


NEG = -1e30


def both(**entries):
    return {name + k: value for name, value in entries.items() for k in "01"}


class Late:
    def __init__(self, source, buffer, semaphore):
        self.copy = pltpu.make_async_copy(source, buffer, semaphore)
        self.buffer, self.shape = buffer, buffer.shape
        self.here = False
        self.copy.start()

    def ready(self):
        if not self.here:
            self.copy.wait()
            self.here = True
        return self.buffer

    def __getitem__(self, at):
        return self.ready()[at]


class Posted:
    def __init__(self, target, buffer, semaphore):
        self.copy = pltpu.make_async_copy(buffer, target, semaphore)
        self.buffer, self.shape = buffer, buffer.shape
        self.sent = False

    def send(self):
        if not self.sent:
            self.copy.start()
            self.sent = True

    def put(self, value):
        self.buffer[...] = value
        self.send()

    def __setitem__(self, at, value):
        self.buffer[at] = value

    def __getitem__(self, at):
        return self.buffer[at]


def kernel_call(fn, ins, outs, near=(), order=(), scratch=(), cost=None):
    shapes = {**ins, **outs}
    integer = lambda name: shapes[name].ndim == 1 and shapes[name].dtype == jnp.int32
    still = [name for name in shapes if name in near or integer(name)]
    moved = [*order, *(name for name in shapes if name not in still and name not in order)]
    names = [*shapes, *(name for name, _ in scratch)]

    def kernel(*refs):
        r = SimpleNamespace(t=(SimpleNamespace(), SimpleNamespace()))
        found = dict(zip(names, refs))
        semaphores, buffers = refs[-1], refs[len(names) : -1]
        for k, name in enumerate(moved):
            kind = Late if name in ins else Posted
            found[name] = kind(found[name], buffers[k], semaphores.at[k])
        for name, ref in found.items():
            if name[-1] in "01":
                setattr(r.t[int(name[-1])], name[:-1], ref)
            else:
                setattr(r, name, ref)
        fn(r)
        posted = [found[name] for name in moved if name in outs]
        for ref in posted:
            ref.send()
        for ref in posted:
            ref.copy.wait()
        for name in moved:
            if name in ins:
                found[name].ready()

    def spec(name):
        space = pl.ANY if name not in still else pltpu.VMEM if name in near else pltpu.SMEM
        return pl.BlockSpec(memory_space=space)

    results = pl.pallas_call(
        kernel,
        out_shape=tuple(pltpu.VMEM(out.shape, out.dtype) if name in near else out for name, out in outs.items()),
        in_specs=[spec(name) for name in ins],
        out_specs=tuple(spec(name) for name in outs),
        scratch_shapes=[shape for _, shape in scratch]
        + [pltpu.VMEM(shapes[name].shape, shapes[name].dtype) for name in moved]
        + [pltpu.SemaphoreType.DMA((len(moved),))],
        cost_estimate=cost,
        name=fn.__name__,
    )(
        *(
            pltpu.with_memory_space_constraint(value, pltpu.VMEM) if name in near else value
            for name, value in ins.items()
        )
    )
    return dict(zip(outs, results))


def select(space, *names):
    return {name + k: space[name + k] for name in names for k in "01"}


def iota(shape, axis):
    return lax.broadcasted_iota(jnp.int32, shape, axis)


def tiles(values, copies):
    return jnp.concatenate([values] * copies, axis=0)


def spread8(values):
    width = values.shape[1]
    heads = width // HEAD
    tiled = tiles(values, heads)
    keep = (iota(tiled.shape, 0) >> 3) == (iota(tiled.shape, 1) >> 6)
    return jnp.where(keep, tiled, 0.0).astype(BF)


def collect8(values):
    rows, width = values.shape
    total = None
    lane = iota((8, width), 1) >> 6
    for head in range(rows // 8):
        piece = jnp.where(lane == head, values[8 * head : 8 * head + 8], 0.0)
        total = piece if total is None else total + piece
    return total


def row_vector(scalars, rows, rest):
    place = iota((rows, 1), 0) & 7
    values = jnp.full((rows, 1), rest, jnp.int32)
    for k, scalar in enumerate(scalars):
        values = jnp.where(place == k, scalar, values)
    return values


def padded(rows):
    return -(-rows // 128) * 128


def ahead_tower(t, lows, highs, places):
    x, xs, normal, inverse = t.x.ready(), t.xs, t.normal.buffer, t.inverse.buffer
    gains, shifts, attn_in = t.gains, t.shifts, t.attn_in
    rows, width = x.shape
    full = normal.shape[0]
    size = 144 if rows % 144 < 16 else 112
    main = rows // size * size

    def norm_rows(at, count):
        raw = x[pl.ds(at, count), :]
        low_normal, inv = normalize(raw.astype(F32))
        xs[pl.ds(at, count), :] = raw
        normal[pl.ds(at, count), :] = low_normal.astype(BF)
        inverse[pl.ds(at, count), :] = inv

    @pl.loop(0, main // size)
    def _(step):
        norm_rows(pl.multiple_of(step * size, 16), size)

    xs[pl.ds(main, full - main), :] = jnp.zeros((full - main, width), BF)
    normal[pl.ds(main, full - main), :] = jnp.zeros((full - main, width), BF)
    inverse[pl.ds(main, full - main), :] = jnp.zeros((full - main, 1), F32)
    if rows > main:
        norm_rows(main, rows - main)
    t.normal.send()
    t.inverse.send()

    gain, shift = gains[0:1, :].astype(F32), shifts[0:1, :].astype(F32)
    pick = (row_vector(places, 8, -1) == iota((8, full), 1)).astype(F32)
    pooled = dot(pick, xs[...])
    pooled_normal, _ = normalize(pooled)
    first = pooled_normal * gain + shift
    query = (dot(first, attn_in[:, :width]) + shifts[1:2, :].astype(F32)).astype(BF).astype(F32)
    key_back = dot(spread8(query), attn_in[:, width : 2 * width], NT) * 0.125
    offset = jnp.sum(key_back * shift, axis=-1, keepdims=True)
    scores = dot(key_back * gain, normal[...], NT) + offset
    rows_all = scores.shape[0]
    columns = iota(scores.shape, 1)
    allowed = (columns >= row_vector(lows, rows_all, 0)) & (columns < row_vector(highs, rows_all, 1))
    scores = jnp.where(allowed, scores, NEG)
    expo = jnp.where(allowed, jnp.exp(scores - jnp.max(scores, axis=-1, keepdims=True)), 0.0)
    probs = expo / jnp.sum(expo, axis=-1, keepdims=True)
    probs_low = probs.astype(BF)
    probs_sum = jnp.sum(probs_low.astype(F32), axis=-1, keepdims=True)
    blend_normal = dot(probs_low, normal[...])
    blend = blend_normal * gain + shift * probs_sum
    mixed = collect8(dot(blend, attn_in[:, 2 * width :]) + probs_sum * shifts[2:3, :].astype(F32))
    t.probs.put(probs)
    t.pick[...] = pick
    t.pooled_normal[...] = pooled_normal
    t.key_back[...] = key_back
    t.probs_sum[...] = probs_sum
    t.blend_normal[...] = blend_normal
    t.blend[...] = blend
    return pooled, mixed


def slots(main, extra):
    row = iota(main.shape, 0)
    return jnp.where(row == 6, extra[0], jnp.where(row == 7, extra[1], main))


def ahead(r):
    me = lax.axis_index("dp")
    at = me * 6
    highs, lows, total = [], [], jnp.int32(0)
    for k in range(6):
        lows.append(total)
        total = total + r.lengths[at + k]
        highs.append(total)
    pooled, mixed = ahead_tower(r.t[0], lows, highs, lows)
    lows = [k * CTX for k in range(6)]
    places = [k * CTX + r.eot[k] for k in range(6)]
    highs = [place + 1 for place in places]
    pooled1, mixed1 = ahead_tower(r.t[1], lows, highs, places)
    width = pooled.shape[1]
    for b, main in enumerate((pooled, mixed, pooled1)):
        r.own[:, b * width : (b + 1) * width] = slots(main, (mixed1[b : b + 1], mixed1[3 + b : 4 + b])).astype(BF)


def packing(parts, message, devices):
    width = parts[0].shape[1]
    span = width // devices
    source, target = iota((width, devices * 16), 0), iota((width, devices * 16), 1)
    spot = target & 15
    place = ((source == (target >> 4) * span + spot) & (spot < span)).astype(F32)
    lane = iota((8, 128), 1)
    apart = dot(jnp.concatenate(parts, axis=0), place)
    for group in range(devices // 8):
        columns = slice(128 * group, 128 * group + 128)
        found = []
        for j in range(4):
            pieces = [apart[48 * j + 8 * h : 48 * j + 8 * h + 8, columns] for h in range(6)]
            pieces += [jnp.zeros((8, 128), F32)] * 2
            for bit in (1, 2, 4):
                low = (lane & (16 * bit)) == 0
                turned = list(pieces)
                for h in range(8):
                    if h & bit == 0:
                        one, two = pieces[h], pieces[h + bit]
                        turned[h] = jnp.where(low, one, pltpu.roll(two, 16 * bit, 1))
                        turned[h + bit] = jnp.where(low, pltpu.roll(one, 128 - 16 * bit, 1), two)
                pieces = turned
            found.append([pltpu.roll(piece, 96 * j % 128, 1) if j else piece for piece in pieces])
        for d in range(8):
            a, b, c, e = (pieces[d] for pieces in found)
            row3 = (jnp.where(lane < 96, a, b), jnp.where(lane < 64, b, c), jnp.where(lane < 32, c, e))
            message[8 * group + d, :, 2 * width :] = jnp.concatenate(row3, axis=1).astype(BF)


def row(ref, j):
    return ref[j : j + 1, :].astype(F32)


def bias_part(t, at):
    j = at // 128
    return jnp.concatenate([row(t.up_bias, j), row(t.up_bias, j + 1)], axis=1)


def gelu_parts(second, t, cols):
    pre = dot(second, t.up[:, cols]) + bias_part(t, cols.start)
    gate = 1.0 / (1.0 + jnp.exp(-1.702 * pre))
    return pre, gate


def slope_of(pre, gate):
    return gate + 1.702 * pre * gate * (1.0 - gate)


def radius_of(embed):
    return lax.rsqrt(jnp.sum(embed * embed, axis=-1, keepdims=True) + UNIT_EPSILON)


def middle_tower(x, mixed, t):
    middle = x + dot(mixed, t.attn_out[...]) + row(t.shifts, 3)
    second_normal, second_inv = normalize(middle)
    second = (second_normal * row(t.gains, 1) + row(t.shifts, 4)).astype(BF)
    t.pooled.put(x.astype(BF))
    t.mixed.put(mixed.astype(BF))
    t.middle.put(middle)
    own_slope = []
    for at in range(0, t.up.shape[1], 256):
        cols = slice(at, at + 256)
        pre, gate = gelu_parts(second, t, cols)
        t.act[:, cols] = (pre * gate).astype(BF)
        own_slope.append(slope_of(pre[:8], gate[:8]))
    out = middle + row(t.shifts, 5) + dot(t.act[...], t.down[...])
    t.out.put(out)
    post_normal, post_inv = normalize(out)
    post = (post_normal * row(t.gains, 2) + row(t.shifts, 6)).astype(BF)
    embed = dot(post, t.proj[...])
    t.embed.put(embed)
    radius = radius_of(embed)
    own = (second_normal[:8], second_inv[:8], own_slope, post_normal[:8], post_inv[:8], embed[:8], radius[:8])
    return (embed * radius).astype(BF), own


def total_row(values):
    return jnp.sum(values.astype(F32), axis=0, keepdims=True)


def unit_back(grad_unit, embed, radius):
    along = jnp.sum(embed * grad_unit, axis=-1, keepdims=True)
    return (radius * grad_unit - radius * radius * radius * embed * along).astype(BF)


def middle_back(t):
    second_normal, second_inv = normalize(t.middle[...])
    second = (second_normal * row(t.gains, 1) + row(t.shifts, 4)).astype(BF)
    t.second[...] = second
    post_normal, post_inv = normalize(t.out[...])
    t.post[...] = (post_normal * row(t.gains, 2) + row(t.shifts, 6)).astype(BF)
    embed = t.embed[...]
    grad_embed = unit_back(t.grad_unit[...], embed, radius_of(embed))
    t.grad_embed[...] = grad_embed
    grad_post = dot(grad_embed, t.proj[...], NT)
    grad_out = norm_back(grad_post, post_normal, post_inv, row(t.gains, 2))
    grad_z = grad_out.astype(BF)
    t.grad_z[...] = grad_z
    for at in range(0, t.up.shape[1], 256):
        cols = slice(at, at + 256)
        pre, gate = gelu_parts(second, t, cols)
        t.act[:, cols] = (pre * gate).astype(BF)
        grad_pre = (dot(grad_z, t.down[cols, :], NT) * slope_of(pre, gate)).astype(BF)
        t.grad_pre[:, cols] = grad_pre
        bias = total_row(grad_pre)
        for j in range(2):
            t.up_bias_grad[at // 128 + j : at // 128 + j + 1, :] = bias[:, 128 * j : 128 * j + 128]
    grad_second = dot(t.grad_pre[...], t.up[...], NT)
    grad_middle = grad_out + norm_back(grad_second, second_normal, second_inv, row(t.gains, 1))
    grad_y = grad_middle.astype(BF)
    t.grad_y[...] = grad_y
    grad_mixed = dot(grad_y, t.attn_out[...], NT).astype(BF)
    sums = (
        grad_second * second_normal, grad_post * post_normal, grad_mixed, grad_y, grad_second, grad_z, grad_post,
    )
    for j, value in enumerate(sums):
        t.rows[j : j + 1, :] = total_row(value)
    return grad_mixed


def own_back(t, grad_unit, own):
    second_normal, second_inv, own_slope, post_normal, post_inv, embed, radius = own
    gain, shift = row(t.gains, 0), row(t.shifts, 0)
    width = gain.shape[1]
    grad_embed = unit_back(grad_unit, embed, radius)
    grad_post = dot(grad_embed, t.proj[...], NT)
    yield
    grad_out = norm_back(grad_post, post_normal, post_inv, row(t.gains, 2))
    grad_act = dot(grad_out, t.down[...], NT)
    yield
    grad_pre = (grad_act * jnp.concatenate(own_slope, axis=1)).astype(BF)
    grad_second = dot(grad_pre, t.up[...], NT)
    yield
    grad_middle = grad_out + norm_back(grad_second, second_normal, second_inv, row(t.gains, 1))
    grad_mixed = dot(grad_middle, t.attn_out[...], NT).astype(BF)
    yield
    wide = spread8(grad_mixed.astype(F32))
    value_back = dot(wide, t.attn_in[:, 2 * width :], NT)
    yield
    offset = jnp.sum(value_back * shift + wide.astype(F32) * row(t.shifts, 2), axis=-1, keepdims=True)
    grad_probs = dot(value_back * gain, t.normal[...], NT) + offset
    yield
    probs = t.probs[...]
    grad_scores = probs * (grad_probs - jnp.sum(grad_probs * probs, axis=-1, keepdims=True))
    scores_low = grad_scores.astype(BF)
    scores_sum = jnp.sum(scores_low.astype(F32), axis=-1, keepdims=True)
    turn_normal = dot(scores_low, t.normal[...])
    yield
    turn = turn_normal * gain + shift * scores_sum
    grad_query = (collect8(dot(turn, t.attn_in[:, width : 2 * width])) * 0.125).astype(BF)
    yield
    query_back = dot(grad_query, t.attn_in[:, :width], NT)
    yield
    key_back, probs_sum = t.key_back[...], t.probs_sum[...]
    gain_part = total_row(
        turn_normal * key_back + t.blend_normal[...] * value_back
    ) + total_row(t.pooled_normal[...] * query_back)
    shift_part = total_row(scores_sum * key_back + probs_sum * value_back) + total_row(query_back)
    t.weights[0:48, :] = scores_low
    t.weights[48:96, :] = probs.astype(BF)
    pick = t.pick[...]
    t.weights[96:112, :] = jnp.concatenate([pick, pick], axis=0).astype(BF)
    t.weights[112:, :] = jnp.zeros((16, probs.shape[1]), BF)
    t.weights.send()
    high = grad_middle.astype(BF).astype(F32)
    none = jnp.zeros((24, width), F32)
    t.terms[:, :width] = jnp.concatenate([key_back, value_back, query_back, none], axis=0).astype(BF)
    t.terms[:, width:] = jnp.concatenate(
        [jnp.zeros((96, width), F32), high, grad_middle - high, none[:16]], axis=0
    ).astype(BF)
    t.terms.send()
    t.turn, t.sent = turn, slots(grad_query.astype(F32), (gain_part, shift_part)).astype(BF)


def reverse_bits(value, bits):
    out = 0
    for k in range(bits):
        out |= ((value >> k) & 1) << (bits - 1 - k)
    return out


def centre(r, devices):
    width = r.t[0].attn_out.shape[0]
    rows = devices * 8
    steps = width // 128
    for c in range(3 * steps):
        r.stage[c] = r.gathered[:, :, 128 * c : 128 * (c + 1)].astype(F32).reshape(rows, 128)
    for c in range(steps):
        for b in range(3):
            for slot, source in ((b, 6), (3 + b, 7)):
                r.tail[c, pl.ds(slot, devices, stride=8), :] = r.stage[b * steps + c, pl.ds(source, devices, stride=8), :]
        for slot in (6, 7):
            r.tail[c, pl.ds(slot, devices, stride=8), :] = jnp.zeros((devices, 128), F32)
    joined = lambda ref, first: jnp.concatenate([ref[first + c] for c in range(steps)], axis=1)
    to, source = iota((rows, rows), 0), iota((rows, rows), 1)
    unit0, own0 = middle_tower(joined(r.stage, 0), joined(r.stage, steps), r.t[0])
    unit1, own1 = middle_tower(joined(r.stage, 2 * steps), joined(r.tail, 0), r.t[1])
    scale = jnp.exp(r.logit_scale[...])
    raw = scale * dot(unit0, unit1, NT)
    row_real, column_real = (to & 7) < 6, (source & 7) < 6
    both = row_real & column_real
    logits = jnp.where(both, raw, NEG)
    row_top = jnp.max(logits, axis=1, keepdims=True)
    row_expo = jnp.exp(logits - row_top)
    row_total = jnp.sum(row_expo, axis=1, keepdims=True)
    column_top = jnp.max(logits, axis=0, keepdims=True)
    column_expo = jnp.exp(logits - column_top)
    column_total = jnp.sum(column_expo, axis=0, keepdims=True)
    diagonal = (to == source).astype(F32)
    grad_logits = jnp.where(
        both,
        0.5 * (row_expo / row_total - diagonal) + 0.5 * (column_expo / column_total - diagonal),
        0.0,
    )
    row_part = jnp.where((iota((rows, 1), 0) & 7) < 6, row_top + jnp.log(row_total), 0.0)
    column_part = jnp.where((iota((1, rows), 1) & 7) < 6, column_top + jnp.log(column_total), 0.0)
    on_diagonal = jnp.where(both, diagonal * raw, 0.0)
    whole = lambda values: jnp.sum(jnp.sum(values, axis=1, keepdims=True), axis=0, keepdims=True)
    total = 0.5 * whole(row_part) + 0.5 * whole(column_part) - whole(on_diagonal)
    r.loss[...] = total / (devices * 6)
    r.scale_grad[...] = whole(grad_logits * jnp.where(both, raw, 0.0))
    grad_sim = (scale * grad_logits).astype(BF)
    grad_unit0, grad_unit1 = dot(grad_sim, unit1), dot(grad_sim, unit0, TN)
    r.t[0].grad_unit.put(grad_unit0)
    r.t[1].grad_unit.put(grad_unit1)
    for _ in zip(own_back(r.t[0], grad_unit0[:8], own0), own_back(r.t[1], grad_unit1[:8], own1), strict=True):
        pass
    packing([r.t[0].turn, r.t[1].turn, r.t[0].blend[...], r.t[1].blend[...]], r.message, devices)
    for d in range(devices):
        for k, t in enumerate(r.t):
            r.message[d, :, k * width : (k + 1) * width] = t.sent


def store_flat(ref, values):
    span, columns = values.shape
    steps = columns // 128
    for c in range(steps):
        ref[pl.ds(c, span, stride=steps), :] = values[:, 128 * c : 128 * (c + 1)]


def picked_rows(first, span, total):
    tall = -(-span // 16) * 16
    near = iota((tall, total), 1) - first
    return ((near == iota((tall, total), 0)) & (near < span)).astype(F32)


def weight_cuts(t, order, devices):
    me = lax.axis_index("dp")
    width = t.gains.shape[1]
    for left, right, out in (
        (t.mixed, t.grad_y, t.attn_out_grad),
        (t.second, t.grad_pre, t.up_grad),
        (t.act, t.grad_z, t.down_grad),
        (t.post, t.grad_embed, t.proj_grad),
    ):
        depth = left.shape[1]
        span = depth // devices
        chosen = picked_rows(me * span, span, depth)
        cut_rows = dot(chosen, left[...], NT)
        store_flat(out, dot(cut_rows, right[...])[:span])
    pooled_normal, _ = normalize(dot(order, t.pooled[...]))
    first = (pooled_normal * row(t.gains, 0) + row(t.shifts, 0)).astype(BF)
    t.query[...] = (dot(first, t.attn_in[:, :width]) + row(t.shifts, 1)).astype(BF)
    span = width // devices
    t.first_cut[...] = dot(picked_rows(me * span, span, width), first, NT).astype(BF)


def token_grads(t):
    gain = row(t.gains, 0)
    rows, width = t.grad_tokens.shape
    for at in range(0, rows, 128):
        count = min(128, rows - at)
        joint = dot(t.weights[:, at : at + 128], t.terms[...], TN)
        grad_first, direct = joint[:, :width], joint[:, width:]
        normal = t.normal[at : at + 128, :].astype(F32)
        values = norm_back(grad_first, normal, t.inverse[at : at + 128, :], gain) + direct
        t.grad_tokens[at : at + count, :] = values[:count].astype(BF)


def rest(r, devices):
    shape = (devices * 8, devices * 8)
    to, source = iota(shape, 0), iota(shape, 1)
    block = reverse_bits(lax.axis_index("dp") ^ (to >> 3), devices.bit_length() - 1)
    order = jnp.where(source == block * 8 + (to & 7), 1.0, 0.0).astype(BF)
    for t in r.t:
        t.grad_mixed[...] = dot(order, middle_back(t)).astype(BF)
        weight_cuts(t, order, devices)
        token_grads(t)
        t.grad_tokens.send()


def ending_tower(t, got, at, devices):
    width = t.query.shape[1]
    heads = width // HEAD
    span = width // devices
    rows = devices * 8
    raw = got[:, :, at * width : (at + 1) * width].astype(F32).reshape(rows, width)
    slot = iota((rows, width), 0) & 7
    grad_query = jnp.where(slot < 6, raw, 0.0)
    kind, place = iota((8, rows), 0), iota((8, rows), 1) & 7
    chooser = ((kind == 0) & (place == 6)) | ((kind == 1) & (place == 7)) | ((kind == 2) & (place < 6))
    sums = dot(jnp.where(chooser, 1.0, 0.0), raw)
    pieces = [dot(t.first_cut[...], grad_query)]
    for j, right, factor in ((at, t.query, 0.125), (2 + at, t.grad_mixed, 1.0)):
        first = 96 * j // 128 * 128
        left = got[:, :, 2 * width + first : 2 * width + (96 * j + 223) // 128 * 128].astype(F32)
        tall = dot(left.reshape(rows, left.shape[2]), right[...], TN)[96 * j - first :]
        lane = iota((16, width), 1) >> 6
        total = None
        for head in range(heads):
            piece = jnp.where(lane == head, tall[16 * head : 16 * head + 16], 0.0)
            total = piece if total is None else total + piece
        pieces.append(factor * total)
    flat = t.attn_in_grad
    steps = 3 * width // 128
    for part, values in enumerate(pieces):
        for c in range(width // 128):
            flat[pl.ds(part * (width // 128) + c, span, stride=steps), :] = values[:span, 128 * c : 128 * (c + 1)]
    got_rows = t.rows[...]
    t.gains_grad[...] = jnp.concatenate([sums[0:1], got_rows[0:2]], axis=0)
    t.shifts_grad[...] = jnp.concatenate([sums[1:2], sums[2:3], got_rows[2:7]], axis=0)


def small_body(args, devices):
    image_tokens, image_lengths, caption_tokens, caption_eot, *weights, logit_scale = args
    names = ("gains", "shifts", "attn_in", "attn_out", "up", "up_bias", "down", "proj")
    w = {}
    for k in range(2):
        for j, name in enumerate(names):
            value = weights[8 * k + j]
            w[f"{name}{k}"] = value.reshape(-1, 128) if value.ndim == 1 else value
    width = image_tokens.shape[1]
    heads = width // HEAD
    hidden = w["up0"].shape[1]
    rows = devices * 8
    span = width // devices
    struct = jax.ShapeDtypeStruct
    full = {"0": padded(image_tokens.shape[0]), "1": padded(caption_tokens.shape[0])}
    hr = heads * 8

    outs = {}
    for k in "01":
        tower = dict(
            normal=struct((full[k], width), BF),
            inverse=struct((full[k], 1), F32),
            probs=struct((hr, full[k]), F32),
            pick=struct((8, full[k]), F32),
        )
        outs |= {name + k: value for name, value in tower.items()}
    outs |= both(
        pooled_normal=struct((8, width), F32),
        key_back=struct((hr, width), F32),
        probs_sum=struct((hr, 1), F32),
        blend_normal=struct((hr, width), F32),
        blend=struct((hr, width), F32),
    )
    a = kernel_call(
        ahead,
        dict(lengths=image_lengths, eot=caption_eot, x0=image_tokens, x1=caption_tokens, **select(w, *names[:3])),
        dict(own=struct((8, 3 * width), BF), **outs),
        near=("own",),
        order=("x0", "gains0", "shifts0", "attn_in0", "x1"),
        scratch=[("xs" + k, pltpu.VMEM((full[k], width), BF)) for k in "01"],
    )

    gathered = a["own"][None]
    bit = devices // 2
    while bit:
        other = lax.ppermute(gathered, "dp", [(d, d ^ bit) for d in range(devices)])
        gathered = jnp.concatenate([gathered, other], axis=0)
        bit //= 2

    narrow = struct((rows, width), BF)
    wide = struct((rows, width), F32)
    outs = both(pooled=narrow, mixed=narrow, middle=wide, out=wide, embed=wide, grad_unit=wide)
    outs |= both(terms=struct((128, 2 * width), BF))
    outs |= {"weights" + k: struct((128, full[k]), BF) for k in "01"}
    stored = tuple(outs)

    def centre_all(r):
        centre(r, devices)

    heavy = [name + k for k in "01" for name in ("attn_out", "shifts", "gains", "up_bias", "up", "down", "proj")]
    b = kernel_call(
        centre_all,
        dict(
            gathered=gathered, logit_scale=logit_scale.reshape(1, 1), **w,
            **{name: value for name, value in a.items() if name[:-1] not in ("ow", "inverse")},
        ),
        dict(
            message=struct((devices, 8, 3 * width), BF), loss=struct((1, 1), F32), scale_grad=struct((1, 1), F32),
            **outs,
        ),
        near=("gathered",),
        order=heavy,
        scratch=[("stage", pltpu.VMEM((3 * width // 128, rows, 128), F32)), ("tail", pltpu.VMEM((width // 128, rows, 128), F32))]
        + [("act" + k, pltpu.VMEM((rows, hidden), BF)) for k in "01"],
    )
    got = lax.all_to_all(b["message"], "dp", 0, 0, tiled=True)

    stay = both(
        query=narrow, first_cut=struct((16, rows), BF), grad_mixed=narrow, rows=struct((7, width), F32),
    )
    outs = both(
        attn_out_grad=struct((width // devices * width // 128, 128), F32),
        up_grad=struct((width // devices * hidden // 128, 128), F32),
        down_grad=struct((hidden // devices * width // 128, 128), F32),
        proj_grad=struct((width // devices * width // 128, 128), F32),
        up_bias_grad=struct((hidden // 128, 128), F32),
    )
    tall = struct((rows, hidden), BF)
    scratch = both(second=narrow, post=narrow, grad_embed=narrow, grad_z=narrow, grad_y=narrow, grad_pre=tall, act=tall)

    def rest_all(r):
        rest(r, devices)

    e = kernel_call(
        rest_all,
        {
            **w, **select(a, "normal", "inverse"),
            **{name: b[name] for name in stored},
        },
        dict(
            grad_tokens0=struct(image_tokens.shape, BF), grad_tokens1=struct(caption_tokens.shape, BF), **outs, **stay,
        ),
        order=[
            name + k for k in "01" for name in (
                "middle", "gains", "shifts", "out", "embed", "grad_unit", "proj", "up_bias", "up", "down", "attn_out",
                "mixed", "pooled", "attn_in", "weights", "terms", "normal", "inverse",
            )
        ],
        scratch=[(name, pltpu.VMEM(value.shape, value.dtype)) for name, value in scratch.items()],
        cost=pl.CostEstimate(flops=4 * 10**9, bytes_accessed=8 * 10**6, transcendentals=0),
    )

    def ending(r):
        for at, t in enumerate(r.t):
            ending_tower(t, r.got, at, devices)

    d = kernel_call(
        ending,
        {"got": got, **{name: e[name] for name in stay}},
        both(
            attn_in_grad=struct((span * 3 * width // 128, 128), F32),
            gains_grad=struct((3, width), F32),
            shifts_grad=struct((7, width), F32),
        ),
        near=("got",),
    )
    found = {**e, **d}
    results = []
    for k in "01":
        results += [found["gains_grad" + k], found["shifts_grad" + k]]
        for name in names[2:]:
            results.append(found[f"{name}_grad{k}"].reshape(-1))
    return (b["loss"].reshape(()), e["grad_tokens0"], e["grad_tokens1"], *results, b["scale_grad"].reshape(()))


def fits(args, devices):
    width = args[0].shape[1]
    return (
        devices & (devices - 1) == 0
        and width % devices == 0
        and width // devices <= 16
        and devices * 8 <= 512
        and args[3].shape[0] == 6
        and width == 384
        and devices % 8 == 0
    )


def body(*args):
    devices = lax.axis_size("dp")
    if fits(args, devices):
        return small_body(args, devices)
    return general_body(*args)


def solution(mesh):
    rows = P("dp", None)
    part = P("dp")
    whole = P()
    tower = (whole, whole, part, part, part, whole, part, part)
    return jax.shard_map(
        body,
        mesh=mesh,
        in_specs=(rows, whole, rows, part) + (whole,) * 17,
        out_specs=(whole, rows, rows, *tower, *tower, whole),
        check_vma=False,
    )
```

```python
from types import SimpleNamespace

import jax
import jax.numpy as jnp
from jax import lax
from jax.experimental import pallas as pl
from jax.experimental.pallas import tpu as pltpu
from jax.sharding import PartitionSpec as P

HEAD = 64
CTX = 77

LAYER_EPSILON = 1e-05
UNIT_EPSILON = 1e-06

BF = jnp.bfloat16
F32 = jnp.float32


def dot(left, right, dims=((1,), (0,))):
    return lax.dot_general(left.astype(BF), right.astype(BF), (dims, ((), ())), preferred_element_type=F32)


NT = ((1,), (1,))
TN = ((0,), (0,))


def normalize(values):
    centred = values - jnp.mean(values, axis=-1, keepdims=True)
    inverse = lax.rsqrt(jnp.mean(centred * centred, axis=-1, keepdims=True) + LAYER_EPSILON)
    return centred * inverse, inverse


def norm_back(incoming, normal, inverse, gain):
    scaled = incoming * gain
    return inverse * (
        scaled
        - jnp.mean(scaled, axis=-1, keepdims=True)
        - normal * jnp.mean(scaled * normal, axis=-1, keepdims=True)
    )


def head_mask(count, width):
    heads = width // HEAD
    rows = lax.broadcasted_iota(jnp.int32, (heads * count, width), 0) // count
    lanes = lax.broadcasted_iota(jnp.int32, (heads * count, width), 1) // HEAD
    return rows == lanes


def spread(values):
    count, width = values.shape
    tiled = jnp.tile(values, (width // HEAD, 1))
    return jnp.where(head_mask(count, width), tiled, jnp.zeros_like(tiled))


def collect(values, count):
    rows, width = values.shape
    kept = jnp.where(head_mask(count, width), values, 0.0)
    return jnp.sum(kept.reshape(rows // count, count, width), axis=0)


def attend_forward(tokens, low, high, place, gains, shifts, attn_in):
    rows, width = tokens.shape
    count = low.shape[0]
    heads = width // HEAD
    normal, inverse = normalize(tokens.astype(F32))
    normal_low = normal.astype(BF)
    picked = place[:, None] == jnp.arange(rows, dtype=jnp.int32)[None, :]
    pooled = dot(picked, tokens).astype(BF)
    pooled_normal, _ = normalize(pooled.astype(F32))
    first = (pooled_normal * gains[0] + shifts[0]).astype(BF)
    query = (dot(first, attn_in[:, :width]) + shifts[1]).astype(BF)
    key_back = dot(spread(query), attn_in[:, width : 2 * width], NT) * 0.125
    offset = jnp.sum(key_back * shifts[0], axis=-1, keepdims=True)
    scores = dot(key_back * gains[0], normal_low, NT) + offset
    columns = jnp.arange(rows, dtype=jnp.int32)[None, :]
    allowed = (columns >= jnp.tile(low, heads)[:, None]) & (columns < jnp.tile(high, heads)[:, None])
    scores = jnp.where(allowed, scores, -1e30)
    expo = jnp.where(allowed, jnp.exp(scores - jnp.max(scores, axis=-1, keepdims=True)), 0.0)
    probs = expo / jnp.sum(expo, axis=-1, keepdims=True)
    probs_low = probs.astype(BF)
    probs_sum = jnp.sum(probs_low.astype(F32), axis=-1, keepdims=True)
    blend_normal = dot(probs_low, normal_low)
    blend = blend_normal * gains[0] + shifts[0] * probs_sum
    mixed = collect(dot(blend, attn_in[:, 2 * width :]) + probs_sum * shifts[2], count).astype(BF)
    kept = (normal, inverse, normal_low, picked, pooled_normal, key_back, probs, probs_low, probs_sum, blend_normal)
    return pooled, mixed, blend.astype(BF), kept


def attend_backward(grad_mixed, grad_middle, kept, gains, shifts, attn_in):
    normal, inverse, normal_low, picked, pooled_normal, key_back, probs, probs_low, probs_sum, blend_normal = kept
    rows, width = normal.shape
    count = grad_mixed.shape[0]
    wide = spread(grad_mixed)
    value_back = dot(wide, attn_in[:, 2 * width :], NT)
    offset = jnp.sum(value_back * shifts[0] + wide.astype(F32) * shifts[2], axis=-1, keepdims=True)
    grad_probs = dot(value_back * gains[0], normal_low, NT) + offset
    grad_scores = probs * (grad_probs - jnp.sum(grad_probs * probs, axis=-1, keepdims=True))
    scores_low = grad_scores.astype(BF)
    scores_sum = jnp.sum(scores_low.astype(F32), axis=-1, keepdims=True)
    turn_normal = dot(scores_low, normal_low)
    turn = turn_normal * gains[0] + shifts[0] * scores_sum
    grad_query = (collect(dot(turn, attn_in[:, width : 2 * width]), count) * 0.125).astype(BF)
    query_back = dot(grad_query, attn_in[:, :width], NT)
    gain_part = (
        jnp.sum(turn_normal * key_back, axis=0)
        + jnp.sum(blend_normal * value_back, axis=0)
        + jnp.sum(pooled_normal * query_back, axis=0)
    )
    shift_part = (
        jnp.sum(scores_sum * key_back, axis=0)
        + jnp.sum(probs_sum * value_back, axis=0)
        + jnp.sum(query_back, axis=0)
    )
    grad_first = (
        dot(scores_low, key_back, TN) + dot(probs_low, value_back, TN) + dot(picked, query_back, TN)
    )
    high = grad_middle.astype(BF)
    rest = (grad_middle - high.astype(F32)).astype(BF)
    grad_tokens = (
        norm_back(grad_first, normal, inverse, gains[0]) + dot(picked, high, TN) + dot(picked, rest, TN)
    )
    return grad_tokens.astype(BF), grad_query, turn.astype(BF), jnp.stack([gain_part, shift_part])


def pooled_forward(pooled, mixed, gains, shifts, attn_out, up, up_bias, down, proj):
    middle = pooled.astype(F32) + dot(mixed, attn_out) + shifts[3]
    second_normal, second_inv = normalize(middle)
    second = (second_normal * gains[1] + shifts[4]).astype(BF)
    pre = dot(second, up) + up_bias
    gate = jax.nn.sigmoid(1.702 * pre)
    act = (pre * gate).astype(BF)
    out = middle + dot(act, down) + shifts[5]
    post_normal, post_inv = normalize(out)
    post = (post_normal * gains[2] + shifts[6]).astype(BF)
    embed = dot(post, proj)
    radius = lax.rsqrt(jnp.sum(embed * embed, axis=-1, keepdims=True) + UNIT_EPSILON)
    unit = (embed * radius).astype(BF)
    return unit, (second_normal, second_inv, second, pre, gate, act, post_normal, post_inv, post, embed, radius)


def pooled_backward(grad_unit, kept, gains, attn_out, up, down, proj):
    second_normal, second_inv, second, pre, gate, act, post_normal, post_inv, post, embed, radius = kept
    along = jnp.sum(embed * grad_unit, axis=-1, keepdims=True)
    grad_embed = (radius * grad_unit - radius * radius * radius * embed * along).astype(BF)
    grad_post = dot(grad_embed, proj, NT)
    grad_out = norm_back(grad_post, post_normal, post_inv, gains[2])
    grad_z = grad_out.astype(BF)
    slope = gate + 1.702 * pre * gate * (1.0 - gate)
    grad_pre = (dot(grad_z, down, NT) * slope).astype(BF)
    grad_second = dot(grad_pre, up, NT)
    grad_middle = grad_out + norm_back(grad_second, second_normal, second_inv, gains[1])
    grad_y = grad_middle.astype(BF)
    grad_mixed = dot(grad_y, attn_out, NT).astype(BF)
    gain_rows = (
        jnp.sum(grad_second * second_normal, axis=0),
        jnp.sum(grad_post * post_normal, axis=0),
    )

    def total(values):
        return jnp.sum(values.astype(F32), axis=0)

    shift_rows = (total(grad_mixed), total(grad_y), total(grad_second), total(grad_z), total(grad_post))
    return grad_mixed, grad_middle, gain_rows, shift_rows, total(grad_pre), (grad_y, grad_pre, grad_z, grad_embed)


def window(total_rows, columns, devices, index):
    part = total_rows * columns // devices
    start = index * part
    first = start // columns
    if part % columns == 0:
        span = part // columns
    else:
        span = max((d * part + part - 1) // columns - d * part // columns + 1 for d in range(devices))
    first = jnp.minimum(first, total_rows - span)
    return first, span, start - first * columns, part


def cut(left, right, devices, index):
    total_rows, columns = left.shape[1], right.shape[1]
    first, span, offset, part = window(total_rows, columns, devices, index)
    rows = dot(lax.dynamic_slice_in_dim(left, first, span, 1), right, TN)
    return finish(rows, offset, part)


def finish(rows, offset, part):
    flat = rows.reshape(-1)
    if flat.shape[0] == part:
        return flat
    return lax.dynamic_slice_in_dim(flat, offset, part)


def slices_out(values, count, columns, devices):
    width = values.shape[1]
    heads = values.shape[0] // count
    cuts = []
    if (width * columns // devices) % columns == 0:
        span = width // devices
        return values.reshape(heads, count, devices, span).transpose(2, 1, 0, 3)
    for d in range(devices):
        part = width * columns // devices
        span = max((e * part + part - 1) // columns - e * part // columns + 1 for e in range(devices))
        first = min(d * part // columns, width - span)
        cuts.append(values[:, first : first + span].reshape(heads, count, span).transpose(1, 0, 2))
    return jnp.stack(cuts)


def exchange(parts):
    devices = parts[0].shape[0]
    flat = jnp.concatenate([part.reshape(devices, -1).astype(BF) for part in parts], axis=1)
    got = lax.all_to_all(flat, "dp", 0, 0, tiled=True)
    outs = []
    at = 0
    for part in parts:
        size = part[0].size
        outs.append(got[:, at : at + size].reshape(part.shape))
        at += size
    return outs


def general_body(
    image_tokens,
    image_lengths,
    caption_tokens,
    caption_eot,
    image_gains,
    image_shifts,
    image_attn_in,
    image_attn_out,
    image_up,
    image_up_bias,
    image_down,
    image_proj,
    caption_gains,
    caption_shifts,
    caption_attn_in,
    caption_attn_out,
    caption_up,
    caption_up_bias,
    caption_down,
    caption_proj,
    logit_scale,
):
    index = lax.axis_index("dp")
    devices = lax.axis_size("dp")
    count = caption_eot.shape[0]
    width = image_tokens.shape[1]
    heads = width // HEAD
    lengths = lax.dynamic_slice_in_dim(image_lengths, index * count, count)
    image_high = jnp.cumsum(lengths)
    image_low = image_high - lengths
    caption_low = jnp.arange(count, dtype=jnp.int32) * CTX
    caption_place = caption_low + caption_eot
    towers = (
        (
            image_tokens, image_low, image_high, image_low,
            image_gains.astype(F32), image_shifts.astype(F32), image_attn_in, image_attn_out,
            image_up, image_up_bias.astype(F32), image_down, image_proj,
        ),
        (
            caption_tokens, caption_low, caption_place + 1, caption_place,
            caption_gains.astype(F32), caption_shifts.astype(F32), caption_attn_in, caption_attn_out,
            caption_up, caption_up_bias.astype(F32), caption_down, caption_proj,
        ),
    )
    ahead = [attend_forward(t[0], t[1], t[2], t[3], t[4], t[5], t[6]) for t in towers]
    own = jnp.stack([ahead[0][0], ahead[0][1], ahead[1][0], ahead[1][1]])
    sent = [jnp.broadcast_to(own[None], (devices, *own.shape))]
    sent += [slices_out(a[2], count, 3 * width, devices) for a in ahead]
    got = exchange(sent)
    pairs = devices * count
    everyone = got[0].transpose(1, 0, 2, 3).reshape(4, pairs, width)
    blends = got[1:]

    units, kepts = [], []
    for k, t in enumerate(towers):
        unit, kept = pooled_forward(everyone[2 * k], everyone[2 * k + 1], t[4], t[5], t[7], t[8], t[9], t[10], t[11])
        units.append(unit)
        kepts.append(kept)
    scale = jnp.exp(logit_scale)
    logits = scale * dot(units[0], units[1], NT)
    row_top = jnp.max(logits, axis=1, keepdims=True)
    row_expo = jnp.exp(logits - row_top)
    row_sum = jnp.sum(row_expo, axis=1, keepdims=True)
    column_top = jnp.max(logits, axis=0, keepdims=True)
    column_expo = jnp.exp(logits - column_top)
    column_sum = jnp.sum(column_expo, axis=0, keepdims=True)
    diagonal = (
        lax.broadcasted_iota(jnp.int32, logits.shape, 0) == lax.broadcasted_iota(jnp.int32, logits.shape, 1)
    ).astype(F32)
    grad_logits = 0.5 * (row_expo / row_sum - diagonal) + 0.5 * (column_expo / column_sum - diagonal)
    total = (
        0.5 * jnp.sum(row_top + jnp.log(row_sum))
        + 0.5 * jnp.sum(column_top + jnp.log(column_sum))
        - jnp.sum(diagonal * logits)
    )
    scale_grad = jnp.sum(grad_logits * logits)
    grad_sim = (scale * grad_logits).astype(BF)
    grad_units = (dot(grad_sim, units[1]), dot(grad_sim, units[0], TN))

    backs, attends = [], []
    for k, t in enumerate(towers):
        back = pooled_backward(grad_units[k], kepts[k], t[4], t[7], t[8], t[10], t[11])
        backs.append(back)
        mine = lax.dynamic_slice_in_dim(back[0], index * count, count)
        mine_middle = lax.dynamic_slice_in_dim(back[1], index * count, count)
        attends.append(attend_backward(mine, mine_middle, ahead[k][3], t[4], t[5], t[6]))
    sent = []
    for a in attends:
        sent.append(jnp.broadcast_to(a[1][None], (devices, count, width)))
        sent.append(slices_out(a[2], count, 3 * width, devices))
        sent.append(jnp.broadcast_to(a[3].astype(BF)[None], (devices, 2, width)))
    got = exchange(sent)

    results = []
    for k, t in enumerate(towers):
        gains, shifts, attn_in = t[4], t[5], t[6]
        grad_query = got[3 * k].reshape(pairs, width)
        turns = got[3 * k + 1].reshape(pairs, heads, -1)
        blend = blends[k].reshape(pairs, heads, -1)
        sums = jnp.sum(got[3 * k + 2].astype(F32), axis=0)
        grad_mixed, _, gain_rows, shift_rows, up_bias_grad, factors = backs[k]
        second, act, post = kepts[k][2], kepts[k][5], kepts[k][8]
        grad_y, grad_pre, grad_z, grad_embed = factors
        pooled_normal, _ = normalize(everyone[2 * k].astype(F32))
        first_rows = (pooled_normal * gains[0] + shifts[0]).astype(BF)
        query = (dot(first_rows, attn_in[:, :width]) + shifts[1]).astype(BF)
        first, span, offset, part = window(width, 3 * width, devices, index)
        pieces = [dot(lax.dynamic_slice_in_dim(first_rows, first, span, 1), grad_query, TN)]
        for left, right, factor in ((turns, query, 0.125), (blend, grad_mixed, 1.0)):
            piece = jnp.einsum(
                "phc,phe->che", left, right.reshape(pairs, heads, HEAD), preferred_element_type=F32
            )
            pieces.append(factor * piece.reshape(span, width))
        attn_in_grad = finish(jnp.concatenate(pieces, axis=1), offset, part)
        query_shift = jnp.sum(grad_query.astype(F32), axis=0)
        gain_grad = jnp.stack([sums[0], gain_rows[0], gain_rows[1]])
        shift_grad = jnp.stack(
            [sums[1], query_shift, shift_rows[0], shift_rows[1], shift_rows[2], shift_rows[3], shift_rows[4]]
        )
        results.append(
            (
                gain_grad,
                shift_grad,
                attn_in_grad,
                cut(everyone[2 * k + 1], grad_y, devices, index),
                cut(second, grad_pre, devices, index),
                up_bias_grad,
                cut(act, grad_z, devices, index),
                cut(post, grad_embed, devices, index),
            )
        )
    return (total / pairs, attends[0][0], attends[1][0], *results[0], *results[1], scale_grad)


NEG = -1e30


def both(**entries):
    return {name + k: value for name, value in entries.items() for k in "01"}


class Late:
    def __init__(self, source, buffer, semaphore):
        self.copy = pltpu.make_async_copy(source, buffer, semaphore)
        self.buffer, self.shape = buffer, buffer.shape
        self.here = False
        self.copy.start()

    def ready(self):
        if not self.here:
            self.copy.wait()
            self.here = True
        return self.buffer

    def __getitem__(self, at):
        return self.ready()[at]


class Posted:
    def __init__(self, target, buffer, semaphore):
        self.copy = pltpu.make_async_copy(buffer, target, semaphore)
        self.buffer, self.shape = buffer, buffer.shape
        self.sent = False

    def send(self):
        if not self.sent:
            self.copy.start()
            self.sent = True

    def put(self, value):
        self.buffer[...] = value
        self.send()

    def __setitem__(self, at, value):
        self.buffer[at] = value

    def __getitem__(self, at):
        return self.buffer[at]


class Plain:
    def __init__(self, ref):
        self.buffer, self.shape = ref, ref.shape

    def ready(self):
        return self.buffer

    def send(self):
        pass

    def put(self, value):
        self.buffer[...] = value

    def __setitem__(self, at, value):
        self.buffer[at] = value

    def __getitem__(self, at):
        return self.buffer[at]


def kernel_call(fn, ins, outs, near=(), order=(), raw=(), scratch=(), cost=None, moving=True):
    shapes = {**ins, **outs}
    integer = lambda name: shapes[name].ndim == 1 and shapes[name].dtype == jnp.int32
    still = [name for name in shapes if name in near or name in raw or integer(name)]
    moved = [*order, *(name for name in shapes if name not in still and name not in order)] if moving else []
    names = [*shapes, *(name for name, _ in scratch)]

    def kernel(*refs):
        r = SimpleNamespace(t=(SimpleNamespace(), SimpleNamespace()))
        found = dict(zip(names, refs))
        semaphores, buffers = refs[-1], refs[len(names) : -1]
        for k, name in enumerate(moved):
            kind = Late if name in ins else Posted
            found[name] = kind(found[name], buffers[k], semaphores.at[k])
        for name in shapes:
            if name not in moved and name not in raw and not integer(name):
                found[name] = Plain(found[name])
        for name, ref in found.items():
            if name[-1] in "01":
                setattr(r.t[int(name[-1])], name[:-1], ref)
            else:
                setattr(r, name, ref)
        fn(r)
        posted = [found[name] for name in moved if name in outs]
        for ref in posted:
            ref.send()
        for ref in posted:
            ref.copy.wait()
        for name in moved:
            if name in ins:
                found[name].ready()

    def spec(name):
        space = pl.ANY if name in moved or name in raw else pltpu.SMEM if integer(name) else pltpu.VMEM
        return pl.BlockSpec(memory_space=space)

    results = pl.pallas_call(
        kernel,
        out_shape=tuple(pltpu.VMEM(out.shape, out.dtype) if name in near else out for name, out in outs.items()),
        in_specs=[spec(name) for name in ins],
        out_specs=tuple(spec(name) for name in outs),
        scratch_shapes=[shape for _, shape in scratch]
        + [pltpu.VMEM(shapes[name].shape, shapes[name].dtype) for name in moved]
        + [pltpu.SemaphoreType.DMA((max(len(moved), 1),))],
        cost_estimate=cost,
        name=fn.__name__,
    )(
        *(
            pltpu.with_memory_space_constraint(value, pltpu.VMEM) if name in near else value
            for name, value in ins.items()
        )
    )
    return dict(zip(outs, results))


def select(space, *names):
    return {name + k: space[name + k] for name in names for k in "01"}


def iota(shape, axis):
    return lax.broadcasted_iota(jnp.int32, shape, axis)


def tiles(values, copies):
    return jnp.concatenate([values] * copies, axis=0)


def spread8(values):
    width = values.shape[1]
    heads = width // HEAD
    tiled = tiles(values, heads)
    keep = (iota(tiled.shape, 0) >> 3) == (iota(tiled.shape, 1) >> 6)
    return jnp.where(keep, tiled, 0.0).astype(BF)


def collect8(values):
    rows, width = values.shape
    total = None
    lane = iota((8, width), 1) >> 6
    for head in range(rows // 8):
        piece = jnp.where(lane == head, values[8 * head : 8 * head + 8], 0.0)
        total = piece if total is None else total + piece
    return total


def row_vector(scalars, rows, rest):
    place = iota((rows, 1), 0) & 7
    values = jnp.full((rows, 1), rest, jnp.int32)
    for k, scalar in enumerate(scalars):
        values = jnp.where(place == k, scalar, values)
    return values


def padded(rows):
    return -(-rows // 128) * 128


def ahead_tower(t, lows, highs, places):
    x, xs, normal, inverse = t.x.ready(), t.xs, t.normal.buffer, t.inverse.buffer
    gains, shifts, attn_in = t.gains, t.shifts, t.attn_in
    rows, width = x.shape
    full = normal.shape[0]
    size = 144 if rows % 144 < 16 else 112
    main = rows // size * size

    def norm_rows(at, count):
        raw = x[pl.ds(at, count), :]
        low_normal, inv = normalize(raw.astype(F32))
        xs[pl.ds(at, count), :] = raw
        normal[pl.ds(at, count), :] = low_normal.astype(BF)
        inverse[pl.ds(at, count), :] = inv

    @pl.loop(0, main // size)
    def _(step):
        norm_rows(pl.multiple_of(step * size, 16), size)

    xs[pl.ds(main, full - main), :] = jnp.zeros((full - main, width), BF)
    normal[pl.ds(main, full - main), :] = jnp.zeros((full - main, width), BF)
    inverse[pl.ds(main, full - main), :] = jnp.zeros((full - main, 1), F32)
    if rows > main:
        norm_rows(main, rows - main)
    t.normal.send()
    t.inverse.send()
    yield
    gain, shift = gains[0:1, :].astype(F32), shifts[0:1, :].astype(F32)
    pick = (row_vector(places, 8, -1) == iota((8, full), 1)).astype(F32)
    pooled = dot(pick, xs[...])
    pooled_normal, _ = normalize(pooled)
    first = pooled_normal * gain + shift
    query = (dot(first, attn_in[:, :width]) + shifts[1:2, :].astype(F32)).astype(BF).astype(F32)
    yield
    key_back = dot(spread8(query), attn_in[:, width : 2 * width], NT) * 0.125
    offset = jnp.sum(key_back * shift, axis=-1, keepdims=True)
    yield
    scores = dot(key_back * gain, normal[...], NT) + offset
    rows_all = scores.shape[0]
    columns = iota(scores.shape, 1)
    allowed = (columns >= row_vector(lows, rows_all, 0)) & (columns < row_vector(highs, rows_all, 1))
    yield
    scores = jnp.where(allowed, scores, NEG)
    expo = jnp.where(allowed, jnp.exp(scores - jnp.max(scores, axis=-1, keepdims=True)), 0.0)
    probs = expo / jnp.sum(expo, axis=-1, keepdims=True)
    probs_low = probs.astype(BF)
    probs_sum = jnp.sum(probs_low.astype(F32), axis=-1, keepdims=True)
    yield
    blend_normal = dot(probs_low, normal[...])
    blend = blend_normal * gain + shift * probs_sum
    yield
    mixed = collect8(dot(blend, attn_in[:, 2 * width :]) + probs_sum * shifts[2:3, :].astype(F32))
    t.probs.put(probs)
    t.pick[...] = pick
    t.pooled_normal[...] = pooled_normal
    t.key_back[...] = key_back
    t.probs_sum[...] = probs_sum
    t.blend_normal[...] = blend_normal
    t.blend[...] = blend
    t.found = pooled, mixed


def slots(main, extra):
    row = iota(main.shape, 0)
    return jnp.where(row == 6, extra[0], jnp.where(row == 7, extra[1], main))


def ahead(r):
    me = lax.axis_index("dp")
    at = me * 6
    highs, lows, total = [], [], jnp.int32(0)
    for k in range(6):
        lows.append(total)
        total = total + r.lengths[at + k]
        highs.append(total)
    one = ahead_tower(r.t[0], lows, highs, lows)
    lows = [k * CTX for k in range(6)]
    places = [k * CTX + r.eot[k] for k in range(6)]
    highs = [place + 1 for place in places]
    together(one, ahead_tower(r.t[1], lows, highs, places))
    (pooled, mixed), (pooled1, mixed1) = r.t[0].found, r.t[1].found
    width = pooled.shape[1]
    for b, main in enumerate((pooled, mixed, pooled1)):
        r.own[:, b * width : (b + 1) * width] = slots(main, (mixed1[b : b + 1], mixed1[3 + b : 4 + b])).astype(BF)


def place_matrix(width, devices):
    span = width // devices
    source, target = iota((width, devices * 16), 0), iota((width, devices * 16), 1)
    spot = target & 15
    return jnp.where((source == (target >> 4) * span + spot) & (spot < span), 1.0, 0.0).astype(BF)


def pieces_of(parts, place, devices, first):
    lane = iota((8, 128), 1)
    apart = dot(jnp.concatenate(parts, axis=0), place)
    found = [[] for _ in parts]
    for group in range(devices // 8):
        columns = slice(128 * group, 128 * group + 128)
        for j in range(len(parts)):
            pieces = [apart[48 * j + 8 * h : 48 * j + 8 * h + 8, columns] for h in range(6)]
            pieces += [jnp.zeros((8, 128), F32)] * 2
            for bit in (1, 2, 4):
                low = (lane & (16 * bit)) == 0
                turned = list(pieces)
                for h in range(8):
                    if h & bit == 0:
                        one, two = pieces[h], pieces[h + bit]
                        turned[h] = jnp.where(low, one, pltpu.roll(two, 16 * bit, 1))
                        turned[h + bit] = jnp.where(low, pltpu.roll(one, 128 - 16 * bit, 1), two)
                pieces = turned
            shift = 96 * (first + j) % 128
            found[j] += [pltpu.roll(piece, shift, 1) if shift else piece for piece in pieces]
    return found


def row(ref, j):
    return ref[j : j + 1, :].astype(F32)


def bias_part(t, at):
    j = at // 128
    return jnp.concatenate([row(t.up_bias, j), row(t.up_bias, j + 1)], axis=1)


def gate_of(pre):
    return 0.5 + 0.5 * jnp.tanh(0.851 * pre)


def slope_of(pre, gate):
    return gate + 1.702 * pre * gate * (1.0 - gate)


def radius_of(embed):
    return lax.rsqrt(jnp.sum(embed * embed, axis=-1, keepdims=True) + UNIT_EPSILON)


def together(one, two):
    for _ in zip(one, two, strict=True):
        pass


def slot_rows(devices):
    return [slice(devices * slot, devices * (slot + 1)) for slot in range(6)]


def own_row(found, slot, values):
    piece = values[:8]
    return jnp.where(iota(piece.shape, 0) == slot, pltpu.roll(piece, slot, 0) if slot else piece, found)


def own_rows(values, devices):
    found = jnp.zeros((8, values.shape[1]), F32)
    for slot, rows in enumerate(slot_rows(devices)):
        found = own_row(found, slot, values[rows, :])
    return found


def normal_rows(values, gain, shift):
    normal, _ = normalize(values)
    return (normal * gain + shift).astype(BF)


def middle_tower(x, mixed, t, devices):
    slots_of = slot_rows(devices)
    for slot, rows in enumerate(slots_of):
        t.mixed[rows, :] = mixed(slot).astype(BF)
    t.mixed.send()
    blend = dot(t.mixed[...], t.attn_out[...])
    gain, shift, add = row(t.gains, 1), row(t.shifts, 4), row(t.shifts, 3)
    for slot, rows in enumerate(slots_of):
        pooled = x(slot)
        t.pooled[rows, :] = pooled.astype(BF)
        middle = pooled + blend[rows] + add
        t.middle[rows, :] = middle
        t.second[rows, :] = normal_rows(middle, gain, shift)
    t.pooled.send()
    t.middle.send()
    own_slope = []
    for at in range(0, t.up.shape[1], 256):
        cols = slice(at, at + 256)
        whole, bias = dot(t.second[...], t.up[:, cols]), bias_part(t, at)
        own = jnp.zeros((8, 256), F32)
        for slot, rows in enumerate(slots_of):
            pre = whole[rows] + bias
            t.act[rows, cols] = (pre * gate_of(pre)).astype(BF)
            own = own_row(own, slot, pre)
        own_slope.append(slope_of(own, gate_of(own)))
    fall = dot(t.act[...], t.down[...])
    gain, shift, add = row(t.gains, 2), row(t.shifts, 6), row(t.shifts, 5)
    for rows in slots_of:
        out = t.middle[rows, :] + fall[rows] + add
        t.out[rows, :] = out
        t.post[rows, :] = normal_rows(out, gain, shift)
    t.out.send()
    embeds = dot(t.post[...], t.proj[...])
    for rows in slots_of:
        embed = embeds[rows]
        t.embed[rows, :] = embed
        t.unit[rows, :] = (embed * radius_of(embed)).astype(BF)
    t.embed.send()
    t.own = (own_rows(t.middle, devices), own_slope, own_rows(t.out, devices), own_rows(t.embed, devices))


def total_row(values):
    return jnp.sum(values.astype(F32), axis=0, keepdims=True)


def unit_back(grad_unit, embed, radius):
    along = jnp.sum(embed * grad_unit, axis=-1, keepdims=True)
    return (radius * grad_unit - radius * radius * radius * embed * along).astype(BF)


def fold(values):
    return jnp.sum(values.astype(F32).reshape(-1, 8, values.shape[1]), axis=0)


def middle_back(t, devices):
    slots_of = slot_rows(devices)
    width = t.gains.shape[1]
    sums = [jnp.zeros((8, width), F32)] * 7

    def count(values, *places):
        for j, value in zip(places, values, strict=True):
            sums[j] = sums[j] + fold(value)

    gain, shift = row(t.gains, 1), row(t.shifts, 4)
    for rows in slots_of:
        t.second[rows, :] = normal_rows(t.middle[rows, :], gain, shift)
    for rows in slots_of:
        embed = t.embed[rows, :]
        t.grad_embed[rows, :] = unit_back(t.grad_unit[rows, :], embed, radius_of(embed))
    posts = dot(t.grad_embed[...], t.proj[...], NT)
    gain, shift = row(t.gains, 2), row(t.shifts, 6)
    for rows in slots_of:
        normal, inverse = normalize(t.out[rows, :])
        t.post[rows, :] = (normal * gain + shift).astype(BF)
        grad_post = posts[rows]
        grad_out = norm_back(grad_post, normal, inverse, gain)
        grad_z = grad_out.astype(BF)
        t.grad_out[rows, :] = grad_out
        t.grad_z[rows, :] = grad_z
        count((grad_post * normal, grad_z, grad_post), 1, 5, 6)
    for at in range(0, t.up.shape[1], 256):
        cols = slice(at, at + 256)
        whole, bias = dot(t.second[...], t.up[:, cols]), bias_part(t, at)
        back = dot(t.grad_z[...], t.down[cols, :], NT)
        total = jnp.zeros((8, 256), F32)
        for rows in slots_of:
            pre = whole[rows] + bias
            gate = gate_of(pre)
            t.act[rows, cols] = (pre * gate).astype(BF)
            grad_pre = (back[rows] * slope_of(pre, gate)).astype(BF)
            t.grad_pre[rows, cols] = grad_pre
            total = total + fold(grad_pre)
        total = total_row(total)
        for j in range(2):
            t.up_bias_grad[at // 128 + j : at // 128 + j + 1, :] = total[:, 128 * j : 128 * j + 128]
    seconds = dot(t.grad_pre[...], t.up[...], NT)
    gain = row(t.gains, 1)
    for rows in slots_of:
        normal, inverse = normalize(t.middle[rows, :])
        grad_second = seconds[rows]
        grad_y = (t.grad_out[rows, :] + norm_back(grad_second, normal, inverse, gain)).astype(BF)
        t.grad_y[rows, :] = grad_y
        count((grad_second * normal, grad_y, grad_second), 0, 3, 4)
    mixeds = dot(t.grad_y[...], t.attn_out[...], NT)
    for rows in slots_of:
        grad_mixed = mixeds[rows].astype(BF)
        t.grad_mixed_here[rows, :] = grad_mixed
        count((grad_mixed,), 2)
    for j, value in enumerate(sums):
        t.rows[j : j + 1, :] = total_row(value)


def own_back(t, grad_unit):
    middle, own_slope, out, embed = t.own
    second_normal, second_inv = normalize(middle)
    post_normal, post_inv = normalize(out)
    radius = radius_of(embed)
    gain, shift = row(t.gains, 0), row(t.shifts, 0)
    width = gain.shape[1]
    grad_embed = unit_back(grad_unit, embed, radius)
    grad_post = dot(grad_embed, t.proj[...], NT)
    yield
    grad_out = norm_back(grad_post, post_normal, post_inv, row(t.gains, 2))
    grad_act = dot(grad_out, t.down[...], NT)
    yield
    grad_pre = (grad_act * jnp.concatenate(own_slope, axis=1)).astype(BF)
    grad_second = dot(grad_pre, t.up[...], NT)
    yield
    grad_middle = grad_out + norm_back(grad_second, second_normal, second_inv, row(t.gains, 1))
    grad_mixed = dot(grad_middle, t.attn_out[...], NT).astype(BF)
    yield
    wide = spread8(grad_mixed.astype(F32))
    value_back = dot(wide, t.attn_in[:, 2 * width :], NT)
    yield
    offset = jnp.sum(value_back * shift + wide.astype(F32) * row(t.shifts, 2), axis=-1, keepdims=True)
    grad_probs = dot(value_back * gain, t.normal[...], NT) + offset
    yield
    probs = t.probs[...]
    grad_scores = probs * (grad_probs - jnp.sum(grad_probs * probs, axis=-1, keepdims=True))
    scores_low = grad_scores.astype(BF)
    scores_sum = jnp.sum(scores_low.astype(F32), axis=-1, keepdims=True)
    turn_normal = dot(scores_low, t.normal[...])
    yield
    turn = turn_normal * gain + shift * scores_sum
    grad_query = (collect8(dot(turn, t.attn_in[:, width : 2 * width])) * 0.125).astype(BF)
    yield
    query_back = dot(grad_query, t.attn_in[:, :width], NT)
    yield
    key_back, probs_sum = t.key_back[...], t.probs_sum[...]
    gain_part = total_row(
        turn_normal * key_back + t.blend_normal[...] * value_back
    ) + total_row(t.pooled_normal[...] * query_back)
    shift_part = total_row(scores_sum * key_back + probs_sum * value_back) + total_row(query_back)
    t.weights[0:48, :] = scores_low
    t.weights[48:96, :] = probs.astype(BF)
    pick = t.pick[...]
    t.weights[96:112, :] = jnp.concatenate([pick, pick], axis=0).astype(BF)
    t.weights[112:, :] = jnp.zeros((16, probs.shape[1]), BF)
    t.weights.send()
    high = grad_middle.astype(BF).astype(F32)
    none = jnp.zeros((24, width), F32)
    t.terms[:, :width] = jnp.concatenate([key_back, value_back, query_back, none], axis=0).astype(BF)
    t.terms[:, width:] = jnp.concatenate(
        [jnp.zeros((96, width), F32), high, grad_middle - high, none[:16]], axis=0
    ).astype(BF)
    t.terms.send()
    t.turn, t.sent = turn, slots(grad_query.astype(F32), (gain_part, shift_part)).astype(BF)


def gather_steps(devices):
    steps = []
    bit = devices // 2
    while bit >= 8:
        steps.append([bit])
        bit //= 2
    return steps + [[6, 4, 2], [1]]


def block_of(distance, devices):
    high = devices.bit_length() - 4
    bit = lambda k: (distance >> k) & 1
    out = (bit(1) << high) | ((bit(2) ^ bit(1)) << (high + 1)) | (bit(0) << (high + 2))
    for k in range(high):
        out |= bit(high + 2 - k) << k
    return out


def centre(r, devices):
    width = r.t[0].attn_out.shape[0]
    rows = devices * 6
    steps = width // 128
    for c in range(3 * steps):
        lanes = slice(128 * c, 128 * (c + 1))
        r.stage[c] = r.gathered[:, :, lanes].astype(F32).reshape(devices * 8, 128)
    group = lambda b, slot: jnp.concatenate(
        [r.stage[b * steps + k, pl.ds(slot, devices, stride=8), :] for k in range(steps)], axis=1
    )
    middle_tower(lambda slot: group(0, slot), lambda slot: group(1, slot), r.t[0], devices)
    middle_tower(lambda slot: group(2, slot), lambda slot: group(slot % 3, 6 + slot // 3), r.t[1], devices)
    unit0, unit1 = r.t[0].unit[...], r.t[1].unit[...]
    to, source = iota((rows, rows), 0), iota((rows, rows), 1)
    scale = jnp.exp(r.logit_scale[...])
    logits = scale * dot(unit0, unit1, NT)
    row_top = jnp.max(logits, axis=1, keepdims=True)
    row_expo = jnp.exp(logits - row_top)
    row_total = jnp.sum(row_expo, axis=1, keepdims=True)
    column_top = jnp.max(logits, axis=0, keepdims=True)
    column_expo = jnp.exp(logits - column_top)
    column_total = jnp.sum(column_expo, axis=0, keepdims=True)
    diagonal = (to == source).astype(F32)
    grad_logits = 0.5 * (row_expo / row_total - diagonal) + 0.5 * (column_expo / column_total - diagonal)
    whole = lambda values: jnp.sum(jnp.sum(values, axis=1, keepdims=True), axis=0, keepdims=True)
    tops = 0.5 * whole(row_top + jnp.log(row_total)) + 0.5 * whole(column_top + jnp.log(column_total))
    r.loss[...] = (tops - whole(diagonal * logits)) / rows
    r.scale_grad[...] = whole(grad_logits * logits)
    grad_sim = (scale * grad_logits).astype(BF)
    grad_unit0, grad_unit1 = dot(grad_sim, unit1), dot(grad_sim, unit0, TN)
    r.t[0].grad_unit.put(grad_unit0)
    r.t[1].grad_unit.put(grad_unit1)
    together(own_back(r.t[0], own_rows(grad_unit0, devices)), own_back(r.t[1], own_rows(grad_unit1, devices)))
    for k, t in enumerate(r.t):
        r.letter[:, k * width : (k + 1) * width] = t.sent
    copies = [
        pltpu.make_async_copy(r.letter, r.message.at[d, :, pl.ds(0, 2 * width)], r.semaphores.at[d])
        for d in range(devices)
    ]
    for copy in copies:
        copy.start()
    lane = iota((8, 128), 1)
    first, second = pieces_of([t.turn for t in r.t], r.place[...], devices, 0)
    for d in range(devices):
        r.slices[d, :, :128] = jnp.where(lane < 96, first[d], second[d]).astype(BF)
        r.slices[d, :, 128:256] = jnp.where(lane < 64, second[d], r.packed[d, :, :128]).astype(BF)
        r.slices[d, :, 256:] = r.packed[d, :, 128:].astype(BF)
    copies.append(
        pltpu.make_async_copy(r.slices, r.message.at[:, :, pl.ds(2 * width, width)], r.semaphores.at[devices])
    )
    copies[-1].start()
    for copy in copies:
        copy.wait()


def store_flat(ref, values):
    span, columns = values.shape
    steps = columns // 128
    for c in range(steps):
        ref[pl.ds(c, span, stride=steps), :] = values[:, 128 * c : 128 * (c + 1)]


def picked_rows(first, span, total):
    tall = -(-span // 16) * 16
    near = iota((tall, total), 1) - first
    return ((near == iota((tall, total), 0)) & (near < span)).astype(F32)


def weight_cuts(t, order, devices):
    me = lax.axis_index("dp")
    width = t.gains.shape[1]
    for left, right, out in (
        (t.mixed, t.grad_y, t.attn_out_grad),
        (t.second, t.grad_pre, t.up_grad),
        (t.act, t.grad_z, t.down_grad),
        (t.post, t.grad_embed, t.proj_grad),
    ):
        depth = left.shape[1]
        span = depth // devices
        chosen = picked_rows(me * span, span, depth)
        cut_rows = dot(chosen, left[...], NT)
        store_flat(out, dot(cut_rows, right[...])[:span])
    pooled_normal, _ = normalize(dot(order, t.pooled[...]))
    first = (pooled_normal * row(t.gains, 0) + row(t.shifts, 0)).astype(BF)
    t.query[...] = (dot(first, t.attn_in[:, :width]) + row(t.shifts, 1)).astype(BF)
    span = width // devices
    t.first_cut[...] = dot(picked_rows(me * span, span, width), first, NT).astype(BF)


def token_grads(t):
    gain = row(t.gains, 0)
    rows, width = t.grad_tokens.shape
    for at in range(0, rows, 128):
        count = min(128, rows - at)
        joint = dot(t.weights[:, at : at + 128], t.terms[...], TN)
        for part in range(0, count, 32):
            size = min(32, count - part)
            here = slice(at + part, at + part + 32)
            piece = joint[part : part + 32]
            normal = t.normal[here, :].astype(F32)
            values = norm_back(piece[:, :width], normal, t.inverse[here, :], gain) + piece[:, width:]
            t.grad_tokens[at + part : at + part + size, :] = values[:size].astype(BF)


def rest(r, devices):
    shape = (devices * 8, devices * 6)
    to, source = iota(shape, 0), iota(shape, 1)
    block = block_of(lax.axis_index("dp") ^ (to >> 3), devices)
    slot = to & 7
    order = jnp.where((source == slot * devices + block) & (slot < 6), 1.0, 0.0).astype(BF)
    for t in r.t:
        middle_back(t, devices)
        t.grad_mixed[...] = dot(order, t.grad_mixed_here[...]).astype(BF)
        weight_cuts(t, order, devices)
        token_grads(t)
        t.grad_tokens.send()


def ending_tower(t, got, at, devices):
    width = t.query.shape[1]
    heads = width // HEAD
    span = width // devices
    rows = devices * 8
    raw = got[:, :, at * width : (at + 1) * width].astype(F32).reshape(rows, width)
    slot = iota((rows, width), 0) & 7
    grad_query = jnp.where(slot < 6, raw, 0.0)
    kind, place = iota((8, rows), 0), iota((8, rows), 1) & 7
    chooser = ((kind == 0) & (place == 6)) | ((kind == 1) & (place == 7)) | ((kind == 2) & (place < 6))
    sums = dot(jnp.where(chooser, 1.0, 0.0), raw)
    pieces = [dot(t.first_cut[...], grad_query)]
    for j, right, factor in ((at, t.query, 0.125), (2 + at, t.grad_mixed, 1.0)):
        first = 96 * j // 128 * 128
        left = got[:, :, 2 * width + first : 2 * width + (96 * j + 223) // 128 * 128].astype(F32)
        tall = dot(left.reshape(rows, left.shape[2]), right[...], TN)[96 * j - first :]
        lane = iota((16, width), 1) >> 6
        total = None
        for head in range(heads):
            piece = jnp.where(lane == head, tall[16 * head : 16 * head + 16], 0.0)
            total = piece if total is None else total + piece
        pieces.append(factor * total)
    flat = t.attn_in_grad
    steps = 3 * width // 128
    for part, values in enumerate(pieces):
        for c in range(width // 128):
            flat[pl.ds(part * (width // 128) + c, span, stride=steps), :] = values[:span, 128 * c : 128 * (c + 1)]
    got_rows = t.rows[...]
    t.gains_grad[...] = jnp.concatenate([sums[0:1], got_rows[0:2]], axis=0)
    t.shifts_grad[...] = jnp.concatenate([sums[1:2], sums[2:3], got_rows[2:7]], axis=0)


def small_body(args, devices):
    image_tokens, image_lengths, caption_tokens, caption_eot, *weights, logit_scale = args
    names = ("gains", "shifts", "attn_in", "attn_out", "up", "up_bias", "down", "proj")
    w = {}
    for k in range(2):
        for j, name in enumerate(names):
            value = weights[8 * k + j]
            w[f"{name}{k}"] = value.reshape(-1, 128) if value.ndim == 1 else value
    width = image_tokens.shape[1]
    heads = width // HEAD
    hidden = w["up0"].shape[1]
    rows, spaced = devices * 6, devices * 8
    span = width // devices
    struct = jax.ShapeDtypeStruct
    full = {"0": padded(image_tokens.shape[0]), "1": padded(caption_tokens.shape[0])}
    hr = heads * 8

    outs = {}
    for k in "01":
        tower = dict(
            normal=struct((full[k], width), BF),
            inverse=struct((full[k], 1), F32),
            probs=struct((hr, full[k]), F32),
            pick=struct((8, full[k]), F32),
        )
        outs |= {name + k: value for name, value in tower.items()}
    outs |= both(
        pooled_normal=struct((8, width), F32),
        key_back=struct((hr, width), F32),
        probs_sum=struct((hr, 1), F32),
        blend_normal=struct((hr, width), F32),
        blend=struct((hr, width), F32),
    )
    a = kernel_call(
        ahead,
        dict(lengths=image_lengths, eot=caption_eot, x0=image_tokens, x1=caption_tokens, **select(w, *names[:3])),
        dict(own=struct((8, 3 * width), BF), **outs),
        near=("own",),
        moving=False,
        scratch=[("xs" + k, pltpu.VMEM((full[k], width), BF)) for k in "01"],
    )

    gathered = a["own"][None]
    steps = gather_steps(devices)
    for step in steps:
        if step == [1]:
            gathered, packed = lax.optimization_barrier((gathered, packed))
        others = [lax.ppermute(gathered, "dp", [(d, d ^ away) for d in range(devices)]) for away in step]
        if step == steps[0]:

            def pack_blend(r):
                lane = iota((8, 128), 1)
                place = place_matrix(width, devices)
                r.place[...] = place
                first, second = pieces_of([t.blend[...] for t in r.t], place, devices, 2)
                for d in range(devices):
                    r.packed[d, :, :128] = first[d]
                    r.packed[d, :, 128:] = jnp.where(lane < 32, first[d], second[d])

            packed = kernel_call(
                pack_blend, select(a, "blend"),
                dict(packed=struct((devices, 8, 256), F32), place=struct((width, devices * 16), BF)), moving=False,
                cost=pl.CostEstimate(flops=10**8, bytes_accessed=400000, transcendentals=0),
            )
        gathered = jnp.concatenate([gathered, *others], axis=0)

    narrow = struct((rows, width), BF)
    wide = struct((rows, width), F32)
    outs = both(pooled=narrow, mixed=narrow, middle=wide, out=wide, embed=wide, grad_unit=wide)
    outs |= both(terms=struct((128, 2 * width), BF))
    outs |= {"weights" + k: struct((128, full[k]), BF) for k in "01"}
    stored = tuple(outs)

    inner = both(act=struct((rows, hidden), BF), second=narrow, post=narrow, unit=narrow)

    def centre_all(r):
        centre(r, devices)

    heavy = [name + k for k in "01" for name in ("attn_out", "shifts", "gains", "up_bias", "up", "down", "proj")]
    b = kernel_call(
        centre_all,
        dict(
            gathered=gathered, logit_scale=logit_scale.reshape(1, 1), **w, **packed,
            **{name: value for name, value in a.items() if name[:-1] not in ("ow", "inverse", "blend")},
        ),
        dict(
            message=struct((devices, 8, 3 * width), BF), loss=struct((1, 1), F32), scale_grad=struct((1, 1), F32),
            **outs,
        ),
        near=("gathered",),
        order=heavy,
        raw=("message",),
        scratch=[
            ("letter", pltpu.VMEM((8, 2 * width), BF)), ("slices", pltpu.VMEM((devices, 8, width), BF)),
            ("semaphores", pltpu.SemaphoreType.DMA((devices + 1,))),
        ]
        + [("stage", pltpu.VMEM((3 * width // 128, spaced, 128), F32))]
        + [(name, pltpu.VMEM(value.shape, value.dtype)) for name, value in inner.items()],
    )
    got = lax.all_to_all(b["message"], "dp", 0, 0, tiled=True)

    stay = both(
        query=struct((spaced, width), BF), first_cut=struct((16, spaced), BF), grad_mixed=struct((spaced, width), BF), rows=struct((7, width), F32),
    )
    outs = both(
        attn_out_grad=struct((width // devices * width // 128, 128), F32),
        up_grad=struct((width // devices * hidden // 128, 128), F32),
        down_grad=struct((hidden // devices * width // 128, 128), F32),
        proj_grad=struct((width // devices * width // 128, 128), F32),
        up_bias_grad=struct((hidden // 128, 128), F32),
    )
    tall = struct((rows, hidden), BF)
    scratch = both(second=narrow, post=narrow, grad_embed=narrow, grad_z=narrow, grad_y=narrow, grad_pre=tall, act=tall)
    scratch |= both(grad_out=wide, grad_mixed_here=narrow)

    def rest_all(r):
        rest(r, devices)

    e = kernel_call(
        rest_all,
        {
            **w, **select(a, "normal", "inverse"),
            **{name: b[name] for name in stored},
        },
        dict(
            grad_tokens0=struct(image_tokens.shape, BF), grad_tokens1=struct(caption_tokens.shape, BF), **outs, **stay,
        ),
        near=tuple(stay),
        order=[
            name + k for k in "01" for name in (
                "middle", "gains", "shifts", "out", "embed", "grad_unit", "proj", "up_bias", "up", "down", "attn_out",
                "mixed", "pooled", "attn_in", "weights", "terms", "normal", "inverse",
            )
        ],
        scratch=[(name, pltpu.VMEM(value.shape, value.dtype)) for name, value in scratch.items()],
        cost=pl.CostEstimate(flops=4 * 10**9, bytes_accessed=8 * 10**6, transcendentals=0),
    )

    def ending(r):
        for at, t in enumerate(r.t):
            ending_tower(t, r.got, at, devices)

    d = kernel_call(
        ending,
        {"got": got, **{name: e[name] for name in stay}},
        both(
            attn_in_grad=struct((span * 3 * width // 128, 128), F32),
            gains_grad=struct((3, width), F32),
            shifts_grad=struct((7, width), F32),
        ),
        near=("got", *stay),
        moving=False,
    )
    found = {**e, **d}
    results = []
    for k in "01":
        results += [found["gains_grad" + k], found["shifts_grad" + k]]
        for name in names[2:]:
            results.append(found[f"{name}_grad{k}"].reshape(-1))
    return (b["loss"].reshape(()), e["grad_tokens0"], e["grad_tokens1"], *results, b["scale_grad"].reshape(()))


def fits(args, devices):
    width = args[0].shape[1]
    return (
        devices & (devices - 1) == 0
        and width % devices == 0
        and width // devices <= 16
        and devices * 8 <= 512
        and args[3].shape[0] == 6
        and width == 384
        and devices % 8 == 0
    )


def body(*args):
    devices = lax.axis_size("dp")
    if fits(args, devices):
        return small_body(args, devices)
    return general_body(*args)


def solution(mesh):
    rows = P("dp", None)
    part = P("dp")
    whole = P()
    tower = (whole, whole, part, part, part, whole, part, part)
    return jax.shard_map(
        body,
        mesh=mesh,
        in_specs=(rows, whole, rows, part) + (whole,) * 17,
        out_specs=(whole, rows, rows, *tower, *tower, whole),
        check_vma=False,
    )
```

```python
from types import SimpleNamespace

import jax
import jax.numpy as jnp
from jax import lax
from jax.experimental import pallas as pl
from jax.experimental.pallas import tpu as pltpu
from jax.sharding import PartitionSpec as P

HEAD = 64
CTX = 77

LAYER_EPSILON = 1e-05
UNIT_EPSILON = 1e-06

BF = jnp.bfloat16
F32 = jnp.float32


def dot(left, right, dims=((1,), (0,))):
    return lax.dot_general(left.astype(BF), right.astype(BF), (dims, ((), ())), preferred_element_type=F32)


NT = ((1,), (1,))
TN = ((0,), (0,))


def normalize(values):
    centred = values - jnp.mean(values, axis=-1, keepdims=True)
    inverse = lax.rsqrt(jnp.mean(centred * centred, axis=-1, keepdims=True) + LAYER_EPSILON)
    return centred * inverse, inverse


def norm_back(incoming, normal, inverse, gain):
    scaled = incoming * gain
    return inverse * (
        scaled
        - jnp.mean(scaled, axis=-1, keepdims=True)
        - normal * jnp.mean(scaled * normal, axis=-1, keepdims=True)
    )


def head_mask(count, width):
    heads = width // HEAD
    rows = lax.broadcasted_iota(jnp.int32, (heads * count, width), 0) // count
    lanes = lax.broadcasted_iota(jnp.int32, (heads * count, width), 1) // HEAD
    return rows == lanes


def spread(values):
    count, width = values.shape
    tiled = jnp.tile(values, (width // HEAD, 1))
    return jnp.where(head_mask(count, width), tiled, jnp.zeros_like(tiled))


def collect(values, count):
    rows, width = values.shape
    kept = jnp.where(head_mask(count, width), values, 0.0)
    return jnp.sum(kept.reshape(rows // count, count, width), axis=0)


def attend_forward(tokens, low, high, place, gains, shifts, attn_in):
    rows, width = tokens.shape
    count = low.shape[0]
    heads = width // HEAD
    normal, inverse = normalize(tokens.astype(F32))
    normal_low = normal.astype(BF)
    picked = place[:, None] == jnp.arange(rows, dtype=jnp.int32)[None, :]
    pooled = dot(picked, tokens).astype(BF)
    pooled_normal, _ = normalize(pooled.astype(F32))
    first = (pooled_normal * gains[0] + shifts[0]).astype(BF)
    query = (dot(first, attn_in[:, :width]) + shifts[1]).astype(BF)
    key_back = dot(spread(query), attn_in[:, width : 2 * width], NT) * 0.125
    offset = jnp.sum(key_back * shifts[0], axis=-1, keepdims=True)
    scores = dot(key_back * gains[0], normal_low, NT) + offset
    columns = jnp.arange(rows, dtype=jnp.int32)[None, :]
    allowed = (columns >= jnp.tile(low, heads)[:, None]) & (columns < jnp.tile(high, heads)[:, None])
    scores = jnp.where(allowed, scores, -1e30)
    expo = jnp.where(allowed, jnp.exp(scores - jnp.max(scores, axis=-1, keepdims=True)), 0.0)
    probs = expo / jnp.sum(expo, axis=-1, keepdims=True)
    probs_low = probs.astype(BF)
    probs_sum = jnp.sum(probs_low.astype(F32), axis=-1, keepdims=True)
    blend_normal = dot(probs_low, normal_low)
    blend = blend_normal * gains[0] + shifts[0] * probs_sum
    mixed = collect(dot(blend, attn_in[:, 2 * width :]) + probs_sum * shifts[2], count).astype(BF)
    kept = (normal, inverse, normal_low, picked, pooled_normal, key_back, probs, probs_low, probs_sum, blend_normal)
    return pooled, mixed, blend.astype(BF), kept


def attend_backward(grad_mixed, grad_middle, kept, gains, shifts, attn_in):
    normal, inverse, normal_low, picked, pooled_normal, key_back, probs, probs_low, probs_sum, blend_normal = kept
    rows, width = normal.shape
    count = grad_mixed.shape[0]
    wide = spread(grad_mixed)
    value_back = dot(wide, attn_in[:, 2 * width :], NT)
    offset = jnp.sum(value_back * shifts[0] + wide.astype(F32) * shifts[2], axis=-1, keepdims=True)
    grad_probs = dot(value_back * gains[0], normal_low, NT) + offset
    grad_scores = probs * (grad_probs - jnp.sum(grad_probs * probs, axis=-1, keepdims=True))
    scores_low = grad_scores.astype(BF)
    scores_sum = jnp.sum(scores_low.astype(F32), axis=-1, keepdims=True)
    turn_normal = dot(scores_low, normal_low)
    turn = turn_normal * gains[0] + shifts[0] * scores_sum
    grad_query = (collect(dot(turn, attn_in[:, width : 2 * width]), count) * 0.125).astype(BF)
    query_back = dot(grad_query, attn_in[:, :width], NT)
    gain_part = (
        jnp.sum(turn_normal * key_back, axis=0)
        + jnp.sum(blend_normal * value_back, axis=0)
        + jnp.sum(pooled_normal * query_back, axis=0)
    )
    shift_part = (
        jnp.sum(scores_sum * key_back, axis=0)
        + jnp.sum(probs_sum * value_back, axis=0)
        + jnp.sum(query_back, axis=0)
    )
    grad_first = (
        dot(scores_low, key_back, TN) + dot(probs_low, value_back, TN) + dot(picked, query_back, TN)
    )
    high = grad_middle.astype(BF)
    rest = (grad_middle - high.astype(F32)).astype(BF)
    grad_tokens = (
        norm_back(grad_first, normal, inverse, gains[0]) + dot(picked, high, TN) + dot(picked, rest, TN)
    )
    return grad_tokens.astype(BF), grad_query, turn.astype(BF), jnp.stack([gain_part, shift_part])


def pooled_forward(pooled, mixed, gains, shifts, attn_out, up, up_bias, down, proj):
    middle = pooled.astype(F32) + dot(mixed, attn_out) + shifts[3]
    second_normal, second_inv = normalize(middle)
    second = (second_normal * gains[1] + shifts[4]).astype(BF)
    pre = dot(second, up) + up_bias
    gate = jax.nn.sigmoid(1.702 * pre)
    act = (pre * gate).astype(BF)
    out = middle + dot(act, down) + shifts[5]
    post_normal, post_inv = normalize(out)
    post = (post_normal * gains[2] + shifts[6]).astype(BF)
    embed = dot(post, proj)
    radius = lax.rsqrt(jnp.sum(embed * embed, axis=-1, keepdims=True) + UNIT_EPSILON)
    unit = (embed * radius).astype(BF)
    return unit, (second_normal, second_inv, second, pre, gate, act, post_normal, post_inv, post, embed, radius)


def pooled_backward(grad_unit, kept, gains, attn_out, up, down, proj):
    second_normal, second_inv, second, pre, gate, act, post_normal, post_inv, post, embed, radius = kept
    along = jnp.sum(embed * grad_unit, axis=-1, keepdims=True)
    grad_embed = (radius * grad_unit - radius * radius * radius * embed * along).astype(BF)
    grad_post = dot(grad_embed, proj, NT)
    grad_out = norm_back(grad_post, post_normal, post_inv, gains[2])
    grad_z = grad_out.astype(BF)
    slope = gate + 1.702 * pre * gate * (1.0 - gate)
    grad_pre = (dot(grad_z, down, NT) * slope).astype(BF)
    grad_second = dot(grad_pre, up, NT)
    grad_middle = grad_out + norm_back(grad_second, second_normal, second_inv, gains[1])
    grad_y = grad_middle.astype(BF)
    grad_mixed = dot(grad_y, attn_out, NT).astype(BF)
    gain_rows = (
        jnp.sum(grad_second * second_normal, axis=0),
        jnp.sum(grad_post * post_normal, axis=0),
    )

    def total(values):
        return jnp.sum(values.astype(F32), axis=0)

    shift_rows = (total(grad_mixed), total(grad_y), total(grad_second), total(grad_z), total(grad_post))
    return grad_mixed, grad_middle, gain_rows, shift_rows, total(grad_pre), (grad_y, grad_pre, grad_z, grad_embed)


def window(total_rows, columns, devices, index):
    part = total_rows * columns // devices
    start = index * part
    first = start // columns
    if part % columns == 0:
        span = part // columns
    else:
        span = max((d * part + part - 1) // columns - d * part // columns + 1 for d in range(devices))
    first = jnp.minimum(first, total_rows - span)
    return first, span, start - first * columns, part


def cut(left, right, devices, index):
    total_rows, columns = left.shape[1], right.shape[1]
    first, span, offset, part = window(total_rows, columns, devices, index)
    rows = dot(lax.dynamic_slice_in_dim(left, first, span, 1), right, TN)
    return finish(rows, offset, part)


def finish(rows, offset, part):
    flat = rows.reshape(-1)
    if flat.shape[0] == part:
        return flat
    return lax.dynamic_slice_in_dim(flat, offset, part)


def slices_out(values, count, columns, devices):
    width = values.shape[1]
    heads = values.shape[0] // count
    cuts = []
    if (width * columns // devices) % columns == 0:
        span = width // devices
        return values.reshape(heads, count, devices, span).transpose(2, 1, 0, 3)
    for d in range(devices):
        part = width * columns // devices
        span = max((e * part + part - 1) // columns - e * part // columns + 1 for e in range(devices))
        first = min(d * part // columns, width - span)
        cuts.append(values[:, first : first + span].reshape(heads, count, span).transpose(1, 0, 2))
    return jnp.stack(cuts)


def exchange(parts):
    devices = parts[0].shape[0]
    flat = jnp.concatenate([part.reshape(devices, -1).astype(BF) for part in parts], axis=1)
    got = lax.all_to_all(flat, "dp", 0, 0, tiled=True)
    outs = []
    at = 0
    for part in parts:
        size = part[0].size
        outs.append(got[:, at : at + size].reshape(part.shape))
        at += size
    return outs


def general_body(
    image_tokens,
    image_lengths,
    caption_tokens,
    caption_eot,
    image_gains,
    image_shifts,
    image_attn_in,
    image_attn_out,
    image_up,
    image_up_bias,
    image_down,
    image_proj,
    caption_gains,
    caption_shifts,
    caption_attn_in,
    caption_attn_out,
    caption_up,
    caption_up_bias,
    caption_down,
    caption_proj,
    logit_scale,
):
    index = lax.axis_index("dp")
    devices = lax.axis_size("dp")
    count = caption_eot.shape[0]
    width = image_tokens.shape[1]
    heads = width // HEAD
    lengths = lax.dynamic_slice_in_dim(image_lengths, index * count, count)
    image_high = jnp.cumsum(lengths)
    image_low = image_high - lengths
    caption_low = jnp.arange(count, dtype=jnp.int32) * CTX
    caption_place = caption_low + caption_eot
    towers = (
        (
            image_tokens, image_low, image_high, image_low,
            image_gains.astype(F32), image_shifts.astype(F32), image_attn_in, image_attn_out,
            image_up, image_up_bias.astype(F32), image_down, image_proj,
        ),
        (
            caption_tokens, caption_low, caption_place + 1, caption_place,
            caption_gains.astype(F32), caption_shifts.astype(F32), caption_attn_in, caption_attn_out,
            caption_up, caption_up_bias.astype(F32), caption_down, caption_proj,
        ),
    )
    ahead = [attend_forward(t[0], t[1], t[2], t[3], t[4], t[5], t[6]) for t in towers]
    own = jnp.stack([ahead[0][0], ahead[0][1], ahead[1][0], ahead[1][1]])
    sent = [jnp.broadcast_to(own[None], (devices, *own.shape))]
    sent += [slices_out(a[2], count, 3 * width, devices) for a in ahead]
    got = exchange(sent)
    pairs = devices * count
    everyone = got[0].transpose(1, 0, 2, 3).reshape(4, pairs, width)
    blends = got[1:]

    units, kepts = [], []
    for k, t in enumerate(towers):
        unit, kept = pooled_forward(everyone[2 * k], everyone[2 * k + 1], t[4], t[5], t[7], t[8], t[9], t[10], t[11])
        units.append(unit)
        kepts.append(kept)
    scale = jnp.exp(logit_scale)
    logits = scale * dot(units[0], units[1], NT)
    row_top = jnp.max(logits, axis=1, keepdims=True)
    row_expo = jnp.exp(logits - row_top)
    row_sum = jnp.sum(row_expo, axis=1, keepdims=True)
    column_top = jnp.max(logits, axis=0, keepdims=True)
    column_expo = jnp.exp(logits - column_top)
    column_sum = jnp.sum(column_expo, axis=0, keepdims=True)
    diagonal = (
        lax.broadcasted_iota(jnp.int32, logits.shape, 0) == lax.broadcasted_iota(jnp.int32, logits.shape, 1)
    ).astype(F32)
    grad_logits = 0.5 * (row_expo / row_sum - diagonal) + 0.5 * (column_expo / column_sum - diagonal)
    total = (
        0.5 * jnp.sum(row_top + jnp.log(row_sum))
        + 0.5 * jnp.sum(column_top + jnp.log(column_sum))
        - jnp.sum(diagonal * logits)
    )
    scale_grad = jnp.sum(grad_logits * logits)
    grad_sim = (scale * grad_logits).astype(BF)
    grad_units = (dot(grad_sim, units[1]), dot(grad_sim, units[0], TN))

    backs, attends = [], []
    for k, t in enumerate(towers):
        back = pooled_backward(grad_units[k], kepts[k], t[4], t[7], t[8], t[10], t[11])
        backs.append(back)
        mine = lax.dynamic_slice_in_dim(back[0], index * count, count)
        mine_middle = lax.dynamic_slice_in_dim(back[1], index * count, count)
        attends.append(attend_backward(mine, mine_middle, ahead[k][3], t[4], t[5], t[6]))
    sent = []
    for a in attends:
        sent.append(jnp.broadcast_to(a[1][None], (devices, count, width)))
        sent.append(slices_out(a[2], count, 3 * width, devices))
        sent.append(jnp.broadcast_to(a[3].astype(BF)[None], (devices, 2, width)))
    got = exchange(sent)

    results = []
    for k, t in enumerate(towers):
        gains, shifts, attn_in = t[4], t[5], t[6]
        grad_query = got[3 * k].reshape(pairs, width)
        turns = got[3 * k + 1].reshape(pairs, heads, -1)
        blend = blends[k].reshape(pairs, heads, -1)
        sums = jnp.sum(got[3 * k + 2].astype(F32), axis=0)
        grad_mixed, _, gain_rows, shift_rows, up_bias_grad, factors = backs[k]
        second, act, post = kepts[k][2], kepts[k][5], kepts[k][8]
        grad_y, grad_pre, grad_z, grad_embed = factors
        pooled_normal, _ = normalize(everyone[2 * k].astype(F32))
        first_rows = (pooled_normal * gains[0] + shifts[0]).astype(BF)
        query = (dot(first_rows, attn_in[:, :width]) + shifts[1]).astype(BF)
        first, span, offset, part = window(width, 3 * width, devices, index)
        pieces = [dot(lax.dynamic_slice_in_dim(first_rows, first, span, 1), grad_query, TN)]
        for left, right, factor in ((turns, query, 0.125), (blend, grad_mixed, 1.0)):
            piece = jnp.einsum(
                "phc,phe->che", left, right.reshape(pairs, heads, HEAD), preferred_element_type=F32
            )
            pieces.append(factor * piece.reshape(span, width))
        attn_in_grad = finish(jnp.concatenate(pieces, axis=1), offset, part)
        query_shift = jnp.sum(grad_query.astype(F32), axis=0)
        gain_grad = jnp.stack([sums[0], gain_rows[0], gain_rows[1]])
        shift_grad = jnp.stack(
            [sums[1], query_shift, shift_rows[0], shift_rows[1], shift_rows[2], shift_rows[3], shift_rows[4]]
        )
        results.append(
            (
                gain_grad,
                shift_grad,
                attn_in_grad,
                cut(everyone[2 * k + 1], grad_y, devices, index),
                cut(second, grad_pre, devices, index),
                up_bias_grad,
                cut(act, grad_z, devices, index),
                cut(post, grad_embed, devices, index),
            )
        )
    return (total / pairs, attends[0][0], attends[1][0], *results[0], *results[1], scale_grad)


NEG = -1e30


def both(**entries):
    return {name + k: value for name, value in entries.items() for k in "01"}


class Late:
    def __init__(self, source, buffer, semaphore):
        self.copy = pltpu.make_async_copy(source, buffer, semaphore)
        self.buffer, self.shape = buffer, buffer.shape
        self.here = False
        self.copy.start()

    def ready(self):
        if not self.here:
            self.copy.wait()
            self.here = True
        return self.buffer

    def __getitem__(self, at):
        return self.ready()[at]


class Posted:
    def __init__(self, target, buffer, semaphore):
        self.copy = pltpu.make_async_copy(buffer, target, semaphore)
        self.buffer, self.shape = buffer, buffer.shape
        self.sent = False

    def send(self):
        if not self.sent:
            self.copy.start()
            self.sent = True

    def put(self, value):
        self.buffer[...] = value
        self.send()

    def __setitem__(self, at, value):
        self.buffer[at] = value

    def __getitem__(self, at):
        return self.buffer[at]


class Plain:
    def __init__(self, ref):
        self.buffer, self.shape = ref, ref.shape

    def ready(self):
        return self.buffer

    def send(self):
        pass

    def put(self, value):
        self.buffer[...] = value

    def __setitem__(self, at, value):
        self.buffer[at] = value

    def __getitem__(self, at):
        return self.buffer[at]


def kernel_call(fn, ins, outs, near=(), order=(), raw=(), scratch=(), cost=None, moving=True):
    shapes = {**ins, **outs}
    integer = lambda name: shapes[name].ndim == 1 and shapes[name].dtype == jnp.int32
    still = [name for name in shapes if name in near or name in raw or integer(name)]
    moved = [*order, *(name for name in shapes if name not in still and name not in order)] if moving else []
    names = [*shapes, *(name for name, _ in scratch)]

    def kernel(*refs):
        r = SimpleNamespace(t=(SimpleNamespace(), SimpleNamespace()))
        found = dict(zip(names, refs))
        semaphores, buffers = refs[-1], refs[len(names) : -1]
        for k, name in enumerate(moved):
            kind = Late if name in ins else Posted
            found[name] = kind(found[name], buffers[k], semaphores.at[k])
        for name in shapes:
            if name not in moved and name not in raw and not integer(name):
                found[name] = Plain(found[name])
        for name, ref in found.items():
            if name[-1] in "01":
                setattr(r.t[int(name[-1])], name[:-1], ref)
            else:
                setattr(r, name, ref)
        fn(r)
        posted = [found[name] for name in moved if name in outs]
        for ref in posted:
            ref.send()
        for ref in posted:
            ref.copy.wait()
        for name in moved:
            if name in ins:
                found[name].ready()

    def spec(name):
        space = pl.ANY if name in moved or name in raw else pltpu.SMEM if integer(name) else pltpu.VMEM
        return pl.BlockSpec(memory_space=space)

    results = pl.pallas_call(
        kernel,
        out_shape=tuple(pltpu.VMEM(out.shape, out.dtype) if name in near else out for name, out in outs.items()),
        in_specs=[spec(name) for name in ins],
        out_specs=tuple(spec(name) for name in outs),
        scratch_shapes=[shape for _, shape in scratch]
        + [pltpu.VMEM(shapes[name].shape, shapes[name].dtype) for name in moved]
        + [pltpu.SemaphoreType.DMA((max(len(moved), 1),))],
        cost_estimate=cost,
        name=fn.__name__,
    )(
        *(
            pltpu.with_memory_space_constraint(value, pltpu.VMEM) if name in near else value
            for name, value in ins.items()
        )
    )
    return dict(zip(outs, results))


def select(space, *names):
    return {name + k: space[name + k] for name in names for k in "01"}


def iota(shape, axis):
    return lax.broadcasted_iota(jnp.int32, shape, axis)


def tiles(values, copies):
    return jnp.concatenate([values] * copies, axis=0)


def spread8(values):
    width = values.shape[1]
    heads = width // HEAD
    tiled = tiles(values, heads)
    keep = (iota(tiled.shape, 0) >> 3) == (iota(tiled.shape, 1) >> 6)
    return jnp.where(keep, tiled, 0.0).astype(BF)


def collect8(values):
    rows, width = values.shape
    total = None
    lane = iota((8, width), 1) >> 6
    for head in range(rows // 8):
        piece = jnp.where(lane == head, values[8 * head : 8 * head + 8], 0.0)
        total = piece if total is None else total + piece
    return total


def row_vector(scalars, rows, rest):
    place = iota((rows, 1), 0) & 7
    values = jnp.full((rows, 1), rest, jnp.int32)
    for k, scalar in enumerate(scalars):
        values = jnp.where(place == k, scalar, values)
    return values


def padded(rows):
    return -(-rows // 128) * 128


def ahead_tower(t, lows, highs, places):
    x, xs, normal, inverse = t.x.ready(), t.xs, t.normal.buffer, t.inverse.buffer
    gains, shifts, attn_in = t.gains, t.shifts, t.attn_in
    rows, width = x.shape
    full = normal.shape[0]
    size = 144 if rows % 144 < 16 else 112
    main = rows // size * size

    def norm_rows(at, count):
        raw = x[pl.ds(at, count), :]
        low_normal, inv = normalize(raw.astype(F32))
        xs[pl.ds(at, count), :] = raw
        normal[pl.ds(at, count), :] = low_normal.astype(BF)
        inverse[pl.ds(at, count), :] = inv

    @pl.loop(0, main // size)
    def _(step):
        norm_rows(pl.multiple_of(step * size, 16), size)

    xs[pl.ds(main, full - main), :] = jnp.zeros((full - main, width), BF)
    normal[pl.ds(main, full - main), :] = jnp.zeros((full - main, width), BF)
    inverse[pl.ds(main, full - main), :] = jnp.zeros((full - main, 1), F32)
    if rows > main:
        norm_rows(main, rows - main)
    t.normal.send()
    t.inverse.send()
    yield
    gain, shift = gains[0:1, :].astype(F32), shifts[0:1, :].astype(F32)
    pick = (row_vector(places, 8, -1) == iota((8, full), 1)).astype(F32)
    pooled = dot(pick, xs[...])
    pooled_normal, _ = normalize(pooled)
    first = pooled_normal * gain + shift
    query = (dot(first, attn_in[:, :width]) + shifts[1:2, :].astype(F32)).astype(BF).astype(F32)
    yield
    key_back = dot(spread8(query), attn_in[:, width : 2 * width], NT) * 0.125
    offset = jnp.sum(key_back * shift, axis=-1, keepdims=True)
    yield
    scores = dot(key_back * gain, normal[...], NT) + offset
    rows_all = scores.shape[0]
    columns = iota(scores.shape, 1)
    allowed = (columns >= row_vector(lows, rows_all, 0)) & (columns < row_vector(highs, rows_all, 1))
    yield
    scores = jnp.where(allowed, scores, NEG)
    expo = jnp.where(allowed, jnp.exp(scores - jnp.max(scores, axis=-1, keepdims=True)), 0.0)
    probs = expo / jnp.sum(expo, axis=-1, keepdims=True)
    probs_low = probs.astype(BF)
    probs_sum = jnp.sum(probs_low.astype(F32), axis=-1, keepdims=True)
    yield
    blend_normal = dot(probs_low, normal[...])
    blend = blend_normal * gain + shift * probs_sum
    yield
    mixed = collect8(dot(blend, attn_in[:, 2 * width :]) + probs_sum * shifts[2:3, :].astype(F32))
    t.probs.put(probs)
    t.pick[...] = pick
    t.pooled_normal[...] = pooled_normal
    t.key_back[...] = key_back
    t.probs_sum[...] = probs_sum
    t.blend_normal[...] = blend_normal
    t.blend[...] = blend
    t.found = pooled, mixed


def slots(main, extra):
    row = iota(main.shape, 0)
    return jnp.where(row == 6, extra[0], jnp.where(row == 7, extra[1], main))


def ahead(r):
    me = lax.axis_index("dp")
    at = me * 6
    highs, lows, total = [], [], jnp.int32(0)
    for k in range(6):
        lows.append(total)
        total = total + r.lengths[at + k]
        highs.append(total)
    one = ahead_tower(r.t[0], lows, highs, lows)
    lows = [k * CTX for k in range(6)]
    places = [k * CTX + r.eot[k] for k in range(6)]
    highs = [place + 1 for place in places]
    together(one, ahead_tower(r.t[1], lows, highs, places))
    (pooled, mixed), (pooled1, mixed1) = r.t[0].found, r.t[1].found
    width = pooled.shape[1]
    for b, main in enumerate((pooled, mixed, pooled1)):
        r.own[:, b * width : (b + 1) * width] = slots(main, (mixed1[b : b + 1], mixed1[3 + b : 4 + b])).astype(BF)


def place_matrix(width, devices):
    span = width // devices
    source, target = iota((width, devices * 16), 0), iota((width, devices * 16), 1)
    spot = target & 15
    return jnp.where((source == (target >> 4) * span + spot) & (spot < span), 1.0, 0.0).astype(BF)


def pieces_of(parts, place, devices, first):
    lane = iota((8, 128), 1)
    apart = dot(jnp.concatenate(parts, axis=0), place)
    found = [[] for _ in parts]
    for group in range(devices // 8):
        columns = slice(128 * group, 128 * group + 128)
        for j in range(len(parts)):
            pieces = [apart[48 * j + 8 * h : 48 * j + 8 * h + 8, columns] for h in range(6)]
            pieces += [jnp.zeros((8, 128), F32)] * 2
            for bit in (1, 2, 4):
                low = (lane & (16 * bit)) == 0
                turned = list(pieces)
                for h in range(8):
                    if h & bit == 0:
                        one, two = pieces[h], pieces[h + bit]
                        turned[h] = jnp.where(low, one, pltpu.roll(two, 16 * bit, 1))
                        turned[h + bit] = jnp.where(low, pltpu.roll(one, 128 - 16 * bit, 1), two)
                pieces = turned
            shift = 96 * (first + j) % 128
            found[j] += [pltpu.roll(piece, shift, 1) if shift else piece for piece in pieces]
    return found


def row(ref, j):
    return ref[j : j + 1, :].astype(F32)


def bias_part(t, at):
    j = at // 128
    return jnp.concatenate([row(t.up_bias, j), row(t.up_bias, j + 1)], axis=1)


def gate_of(pre):
    return 0.5 + 0.5 * jnp.tanh(0.851 * pre)


def slope_of(pre, gate):
    return gate + 1.702 * pre * gate * (1.0 - gate)


def radius_of(embed):
    return lax.rsqrt(jnp.sum(embed * embed, axis=-1, keepdims=True) + UNIT_EPSILON)


def together(one, two):
    for _ in zip(one, two, strict=True):
        pass


def slot_rows(devices):
    return [slice(devices * slot, devices * (slot + 1)) for slot in range(6)]


def own_row(found, slot, values):
    piece = values[:8]
    return jnp.where(iota(piece.shape, 0) == slot, pltpu.roll(piece, slot, 0) if slot else piece, found)


def own_rows(values, devices):
    found = jnp.zeros((8, values.shape[1]), F32)
    for slot, rows in enumerate(slot_rows(devices)):
        found = own_row(found, slot, values[rows, :])
    return found


def normal_rows(values, gain, shift):
    normal, _ = normalize(values)
    return (normal * gain + shift).astype(BF)


def middle_tower(x, mixed, t, devices):
    slots_of = slot_rows(devices)
    for slot, rows in enumerate(slots_of):
        t.mixed[rows, :] = mixed(slot).astype(BF)
    t.mixed.send()
    blend = dot(t.mixed[...], t.attn_out[...])
    yield
    gain, shift, add = row(t.gains, 1), row(t.shifts, 4), row(t.shifts, 3)
    for slot, rows in enumerate(slots_of):
        pooled = x(slot)
        t.pooled[rows, :] = pooled.astype(BF)
        middle = pooled + blend[rows] + add
        t.middle[rows, :] = middle
        t.second[rows, :] = normal_rows(middle, gain, shift)
    t.pooled.send()
    t.middle.send()
    own_slope = []
    for at in range(0, t.up.shape[1], 256):
        cols = slice(at, at + 256)
        whole, bias = dot(t.second[...], t.up[:, cols]), bias_part(t, at)
        yield
        own = jnp.zeros((8, 256), F32)
        for slot, rows in enumerate(slots_of):
            pre = whole[rows] + bias
            t.act[rows, cols] = (pre * gate_of(pre)).astype(BF)
            own = own_row(own, slot, pre)
        own_slope.append(slope_of(own, gate_of(own)))
    fall = dot(t.act[...], t.down[...])
    yield
    gain, shift, add = row(t.gains, 2), row(t.shifts, 6), row(t.shifts, 5)
    for rows in slots_of:
        out = t.middle[rows, :] + fall[rows] + add
        t.out[rows, :] = out
        t.post[rows, :] = normal_rows(out, gain, shift)
    t.out.send()
    embeds = dot(t.post[...], t.proj[...])
    yield
    for rows in slots_of:
        embed = embeds[rows]
        t.embed[rows, :] = embed
        t.unit[rows, :] = (embed * radius_of(embed)).astype(BF)
    t.embed.send()
    t.own = (own_rows(t.middle, devices), own_slope, own_rows(t.out, devices), own_rows(t.embed, devices))


def total_row(values):
    return jnp.sum(values.astype(F32), axis=0, keepdims=True)


def unit_back(grad_unit, embed, radius):
    along = jnp.sum(embed * grad_unit, axis=-1, keepdims=True)
    return (radius * grad_unit - radius * radius * radius * embed * along).astype(BF)


def fold(values):
    return jnp.sum(values.astype(F32).reshape(-1, 8, values.shape[1]), axis=0)


def middle_back(t, devices):
    slots_of = slot_rows(devices)
    width = t.gains.shape[1]
    sums = [jnp.zeros((8, width), F32)] * 7

    def count(values, *places):
        for j, value in zip(places, values, strict=True):
            sums[j] = sums[j] + fold(value)

    gain, shift = row(t.gains, 1), row(t.shifts, 4)
    for rows in slots_of:
        t.second[rows, :] = normal_rows(t.middle[rows, :], gain, shift)
    for rows in slots_of:
        embed = t.embed[rows, :]
        t.grad_embed[rows, :] = unit_back(t.grad_unit[rows, :], embed, radius_of(embed))
    posts = dot(t.grad_embed[...], t.proj[...], NT)
    gain, shift = row(t.gains, 2), row(t.shifts, 6)
    for rows in slots_of:
        normal, inverse = normalize(t.out[rows, :])
        t.post[rows, :] = (normal * gain + shift).astype(BF)
        grad_post = posts[rows]
        grad_out = norm_back(grad_post, normal, inverse, gain)
        grad_z = grad_out.astype(BF)
        t.grad_out[rows, :] = grad_out
        t.grad_z[rows, :] = grad_z
        count((grad_post * normal, grad_z, grad_post), 1, 5, 6)
    for at in range(0, t.up.shape[1], 256):
        cols = slice(at, at + 256)
        whole, bias = dot(t.second[...], t.up[:, cols]), bias_part(t, at)
        back = dot(t.grad_z[...], t.down[cols, :], NT)
        total = jnp.zeros((8, 256), F32)
        for rows in slots_of:
            pre = whole[rows] + bias
            gate = gate_of(pre)
            t.act[rows, cols] = (pre * gate).astype(BF)
            grad_pre = (back[rows] * slope_of(pre, gate)).astype(BF)
            t.grad_pre[rows, cols] = grad_pre
            total = total + fold(grad_pre)
        total = total_row(total)
        for j in range(2):
            t.up_bias_grad[at // 128 + j : at // 128 + j + 1, :] = total[:, 128 * j : 128 * j + 128]
    seconds = dot(t.grad_pre[...], t.up[...], NT)
    gain = row(t.gains, 1)
    for rows in slots_of:
        normal, inverse = normalize(t.middle[rows, :])
        grad_second = seconds[rows]
        grad_y = (t.grad_out[rows, :] + norm_back(grad_second, normal, inverse, gain)).astype(BF)
        t.grad_y[rows, :] = grad_y
        count((grad_second * normal, grad_y, grad_second), 0, 3, 4)
    mixeds = dot(t.grad_y[...], t.attn_out[...], NT)
    for rows in slots_of:
        grad_mixed = mixeds[rows].astype(BF)
        t.grad_mixed_here[rows, :] = grad_mixed
        count((grad_mixed,), 2)
    for j, value in enumerate(sums):
        t.rows[j : j + 1, :] = total_row(value)


def own_back(t, grad_unit):
    middle, own_slope, out, embed = t.own
    second_normal, second_inv = normalize(middle)
    post_normal, post_inv = normalize(out)
    radius = radius_of(embed)
    gain, shift = row(t.gains, 0), row(t.shifts, 0)
    width = gain.shape[1]
    grad_embed = unit_back(grad_unit, embed, radius)
    grad_post = dot(grad_embed, t.proj[...], NT)
    yield
    grad_out = norm_back(grad_post, post_normal, post_inv, row(t.gains, 2))
    grad_act = dot(grad_out, t.down[...], NT)
    yield
    grad_pre = (grad_act * jnp.concatenate(own_slope, axis=1)).astype(BF)
    grad_second = dot(grad_pre, t.up[...], NT)
    yield
    grad_middle = grad_out + norm_back(grad_second, second_normal, second_inv, row(t.gains, 1))
    grad_mixed = dot(grad_middle, t.attn_out[...], NT).astype(BF)
    yield
    wide = spread8(grad_mixed.astype(F32))
    value_back = dot(wide, t.attn_in[:, 2 * width :], NT)
    yield
    offset = jnp.sum(value_back * shift + wide.astype(F32) * row(t.shifts, 2), axis=-1, keepdims=True)
    grad_probs = dot(value_back * gain, t.normal[...], NT) + offset
    yield
    probs = t.probs[...]
    grad_scores = probs * (grad_probs - jnp.sum(grad_probs * probs, axis=-1, keepdims=True))
    scores_low = grad_scores.astype(BF)
    scores_sum = jnp.sum(scores_low.astype(F32), axis=-1, keepdims=True)
    turn_normal = dot(scores_low, t.normal[...])
    yield
    turn = turn_normal * gain + shift * scores_sum
    grad_query = (collect8(dot(turn, t.attn_in[:, width : 2 * width])) * 0.125).astype(BF)
    yield
    query_back = dot(grad_query, t.attn_in[:, :width], NT)
    yield
    key_back, probs_sum = t.key_back[...], t.probs_sum[...]
    gain_part = total_row(
        turn_normal * key_back + t.blend_normal[...] * value_back
    ) + total_row(t.pooled_normal[...] * query_back)
    shift_part = total_row(scores_sum * key_back + probs_sum * value_back) + total_row(query_back)
    t.turn, t.sent = turn, slots(grad_query.astype(F32), (gain_part, shift_part)).astype(BF)

    def finish():
        t.weights[0:48, :] = scores_low
        t.weights[48:96, :] = probs.astype(BF)
        pick = t.pick[...]
        t.weights[96:112, :] = jnp.concatenate([pick, pick], axis=0).astype(BF)
        t.weights[112:, :] = jnp.zeros((16, probs.shape[1]), BF)
        t.weights.send()
        high = grad_middle.astype(BF).astype(F32)
        none = jnp.zeros((24, width), F32)
        t.terms[:, :width] = jnp.concatenate([key_back, value_back, query_back, none], axis=0).astype(BF)
        t.terms[:, width:] = jnp.concatenate(
            [jnp.zeros((96, width), F32), high, grad_middle - high, none[:16]], axis=0
        ).astype(BF)
        t.terms.send()

    t.finish = finish


def gather_steps(devices):
    steps = []
    bit = devices // 2
    while bit >= 8:
        steps.append([bit])
        bit //= 2
    return steps + [[6, 4, 2], [1]]


def block_of(distance, devices):
    high = devices.bit_length() - 4
    bit = lambda k: (distance >> k) & 1
    out = (bit(1) << high) | ((bit(2) ^ bit(1)) << (high + 1)) | (bit(0) << (high + 2))
    for k in range(high):
        out |= bit(high + 2 - k) << k
    return out


def centre(r, devices):
    width = r.t[0].attn_out.shape[0]
    rows = devices * 6
    steps = width // 128
    for c in range(3 * steps):
        lanes = slice(128 * c, 128 * (c + 1))
        r.stage[c] = r.gathered[:, :, lanes].astype(F32).reshape(devices * 8, 128)
    group = lambda b, slot: jnp.concatenate(
        [r.stage[b * steps + k, pl.ds(slot, devices, stride=8), :] for k in range(steps)], axis=1
    )
    together(
        middle_tower(lambda slot: group(0, slot), lambda slot: group(1, slot), r.t[0], devices),
        middle_tower(lambda slot: group(2, slot), lambda slot: group(slot % 3, 6 + slot // 3), r.t[1], devices),
    )
    unit0, unit1 = r.t[0].unit[...], r.t[1].unit[...]
    to, source = iota((rows, rows), 0), iota((rows, rows), 1)
    scale = jnp.exp(r.logit_scale[...])
    logits = scale * dot(unit0, unit1, NT)
    row_top = jnp.max(logits, axis=1, keepdims=True)
    row_expo = jnp.exp(logits - row_top)
    row_total = jnp.sum(row_expo, axis=1, keepdims=True)
    column_top = jnp.max(logits, axis=0, keepdims=True)
    column_expo = jnp.exp(logits - column_top)
    column_total = jnp.sum(column_expo, axis=0, keepdims=True)
    diagonal = (to == source).astype(F32)
    grad_logits = 0.5 * (row_expo / row_total - diagonal) + 0.5 * (column_expo / column_total - diagonal)
    whole = lambda values: jnp.sum(jnp.sum(values, axis=1, keepdims=True), axis=0, keepdims=True)
    tops = 0.5 * whole(row_top + jnp.log(row_total)) + 0.5 * whole(column_top + jnp.log(column_total))
    r.loss[...] = (tops - whole(diagonal * logits)) / rows
    r.scale_grad[...] = whole(grad_logits * logits)
    grad_sim = (scale * grad_logits).astype(BF)
    grad_unit0, grad_unit1 = dot(grad_sim, unit1), dot(grad_sim, unit0, TN)
    r.t[0].grad_unit.put(grad_unit0)
    r.t[1].grad_unit.put(grad_unit1)
    together(own_back(r.t[0], own_rows(grad_unit0, devices)), own_back(r.t[1], own_rows(grad_unit1, devices)))
    for k, t in enumerate(r.t):
        r.letter[:, k * width : (k + 1) * width] = t.sent
    copies = [
        pltpu.make_async_copy(r.letter, r.message.at[d, :, pl.ds(0, 2 * width)], r.semaphores.at[d])
        for d in range(devices)
    ]
    for copy in copies:
        copy.start()
    lane = iota((8, 128), 1)
    first, second = pieces_of([t.turn for t in r.t], r.place[...], devices, 0)
    for d in range(devices):
        r.slices[d, :, :128] = jnp.where(lane < 96, first[d], second[d]).astype(BF)
        r.slices[d, :, 128:256] = jnp.where(lane < 64, second[d], r.packed[d, :, :128]).astype(BF)
        r.slices[d, :, 256:] = r.packed[d, :, 128:].astype(BF)
    copies.append(
        pltpu.make_async_copy(r.slices, r.message.at[:, :, pl.ds(2 * width, width)], r.semaphores.at[devices])
    )
    copies[-1].start()
    for t in r.t:
        t.finish()
    for copy in copies:
        copy.wait()


def store_flat(ref, values):
    span, columns = values.shape
    steps = columns // 128
    for c in range(steps):
        ref[pl.ds(c, span, stride=steps), :] = values[:, 128 * c : 128 * (c + 1)]


def picked_rows(first, span, total):
    tall = -(-span // 16) * 16
    near = iota((tall, total), 1) - first
    return ((near == iota((tall, total), 0)) & (near < span)).astype(F32)


def weight_cuts(t, order, devices):
    me = lax.axis_index("dp")
    width = t.gains.shape[1]
    for left, right, out in (
        (t.mixed, t.grad_y, t.attn_out_grad),
        (t.second, t.grad_pre, t.up_grad),
        (t.act, t.grad_z, t.down_grad),
        (t.post, t.grad_embed, t.proj_grad),
    ):
        depth = left.shape[1]
        span = depth // devices
        chosen = picked_rows(me * span, span, depth)
        cut_rows = dot(chosen, left[...], NT)
        store_flat(out, dot(cut_rows, right[...])[:span])
    pooled_normal, _ = normalize(dot(order, t.pooled[...]))
    first = (pooled_normal * row(t.gains, 0) + row(t.shifts, 0)).astype(BF)
    t.query[...] = (dot(first, t.attn_in[:, :width]) + row(t.shifts, 1)).astype(BF)
    span = width // devices
    t.first_cut[...] = dot(picked_rows(me * span, span, width), first, NT).astype(BF)


def token_grads(t):
    gain = row(t.gains, 0)
    rows, width = t.grad_tokens.shape
    for at in range(0, rows, 128):
        count = min(128, rows - at)
        joint = dot(t.weights[:, at : at + 128], t.terms[...], TN)
        for part in range(0, count, 32):
            size = min(32, count - part)
            here = slice(at + part, at + part + 32)
            piece = joint[part : part + 32]
            normal = t.normal[here, :].astype(F32)
            values = norm_back(piece[:, :width], normal, t.inverse[here, :], gain) + piece[:, width:]
            t.grad_tokens[at + part : at + part + size, :] = values[:size].astype(BF)


def rest(r, devices):
    shape = (devices * 8, devices * 6)
    to, source = iota(shape, 0), iota(shape, 1)
    block = block_of(lax.axis_index("dp") ^ (to >> 3), devices)
    slot = to & 7
    order = jnp.where((source == slot * devices + block) & (slot < 6), 1.0, 0.0).astype(BF)
    for t in r.t:
        middle_back(t, devices)
        t.grad_mixed[...] = dot(order, t.grad_mixed_here[...]).astype(BF)
        weight_cuts(t, order, devices)
        token_grads(t)
        t.grad_tokens.send()


def ending_tower(t, got, at, devices):
    width = t.query.shape[1]
    heads = width // HEAD
    span = width // devices
    rows = devices * 8
    raw = got[:, :, at * width : (at + 1) * width].astype(F32).reshape(rows, width)
    slot = iota((rows, width), 0) & 7
    grad_query = jnp.where(slot < 6, raw, 0.0)
    kind, place = iota((8, rows), 0), iota((8, rows), 1) & 7
    chooser = ((kind == 0) & (place == 6)) | ((kind == 1) & (place == 7)) | ((kind == 2) & (place < 6))
    sums = dot(jnp.where(chooser, 1.0, 0.0), raw)
    pieces = [dot(t.first_cut[...], grad_query)]
    for j, right, factor in ((at, t.query, 0.125), (2 + at, t.grad_mixed, 1.0)):
        first = 96 * j // 128 * 128
        left = got[:, :, 2 * width + first : 2 * width + (96 * j + 223) // 128 * 128].astype(F32)
        tall = dot(left.reshape(rows, left.shape[2]), right[...], TN)[96 * j - first :]
        lane = iota((16, width), 1) >> 6
        total = None
        for head in range(heads):
            piece = jnp.where(lane == head, tall[16 * head : 16 * head + 16], 0.0)
            total = piece if total is None else total + piece
        pieces.append(factor * total)
    flat = t.attn_in_grad
    steps = 3 * width // 128
    for part, values in enumerate(pieces):
        for c in range(width // 128):
            flat[pl.ds(part * (width // 128) + c, span, stride=steps), :] = values[:span, 128 * c : 128 * (c + 1)]
    got_rows = t.rows[...]
    t.gains_grad[...] = jnp.concatenate([sums[0:1], got_rows[0:2]], axis=0)
    t.shifts_grad[...] = jnp.concatenate([sums[1:2], sums[2:3], got_rows[2:7]], axis=0)


def small_body(args, devices):
    image_tokens, image_lengths, caption_tokens, caption_eot, *weights, logit_scale = args
    names = ("gains", "shifts", "attn_in", "attn_out", "up", "up_bias", "down", "proj")
    w = {}
    for k in range(2):
        for j, name in enumerate(names):
            value = weights[8 * k + j]
            w[f"{name}{k}"] = value.reshape(-1, 128) if value.ndim == 1 else value
    width = image_tokens.shape[1]
    heads = width // HEAD
    hidden = w["up0"].shape[1]
    rows, spaced = devices * 6, devices * 8
    span = width // devices
    struct = jax.ShapeDtypeStruct
    full = {"0": padded(image_tokens.shape[0]), "1": padded(caption_tokens.shape[0])}
    hr = heads * 8

    outs = {}
    for k in "01":
        tower = dict(
            normal=struct((full[k], width), BF),
            inverse=struct((full[k], 1), F32),
            probs=struct((hr, full[k]), F32),
            pick=struct((8, full[k]), F32),
        )
        outs |= {name + k: value for name, value in tower.items()}
    outs |= both(
        pooled_normal=struct((8, width), F32),
        key_back=struct((hr, width), F32),
        probs_sum=struct((hr, 1), F32),
        blend_normal=struct((hr, width), F32),
        blend=struct((hr, width), F32),
    )
    a = kernel_call(
        ahead,
        dict(lengths=image_lengths, eot=caption_eot, x0=image_tokens, x1=caption_tokens, **select(w, *names[:3])),
        dict(own=struct((8, 3 * width), BF), **outs),
        near=("own",),
        moving=False,
        scratch=[("xs" + k, pltpu.VMEM((full[k], width), BF)) for k in "01"],
    )

    gathered = a["own"][None]
    steps = gather_steps(devices)
    for step in steps:
        if step == [1]:
            gathered, packed = lax.optimization_barrier((gathered, packed))
        others = [lax.ppermute(gathered, "dp", [(d, d ^ away) for d in range(devices)]) for away in step]
        if step == steps[0]:

            def pack_blend(r):
                lane = iota((8, 128), 1)
                place = place_matrix(width, devices)
                r.place[...] = place
                first, second = pieces_of([t.blend[...] for t in r.t], place, devices, 2)
                for d in range(devices):
                    r.packed[d, :, :128] = first[d]
                    r.packed[d, :, 128:] = jnp.where(lane < 32, first[d], second[d])

            packed = kernel_call(
                pack_blend, select(a, "blend"),
                dict(packed=struct((devices, 8, 256), F32), place=struct((width, devices * 16), BF)), moving=False,
                cost=pl.CostEstimate(flops=10**8, bytes_accessed=400000, transcendentals=0),
            )
        gathered = jnp.concatenate([gathered, *others], axis=0)

    narrow = struct((rows, width), BF)
    wide = struct((rows, width), F32)
    outs = both(pooled=narrow, mixed=narrow, middle=wide, out=wide, embed=wide, grad_unit=wide)
    outs |= both(terms=struct((128, 2 * width), BF))
    outs |= {"weights" + k: struct((128, full[k]), BF) for k in "01"}
    stored = tuple(outs)

    inner = both(act=struct((rows, hidden), BF), second=narrow, post=narrow, unit=narrow)

    def centre_all(r):
        centre(r, devices)

    early = ("attn_out0", "attn_out1", "up0")
    heavy = [name + k for name in ("shifts", "gains", "up_bias", "up", "down", "proj") for k in "01" if name + k not in early]
    b = kernel_call(
        centre_all,
        dict(
            gathered=gathered, logit_scale=logit_scale.reshape(1, 1), **w, **packed,
            **{name: value for name, value in a.items() if name[:-1] not in ("ow", "inverse", "blend")},
        ),
        dict(
            message=struct((devices, 8, 3 * width), BF), loss=struct((1, 1), F32), scale_grad=struct((1, 1), F32),
            **outs,
        ),
        near=("gathered", *early),
        order=heavy,
        raw=("message",),
        scratch=[
            ("letter", pltpu.VMEM((8, 2 * width), BF)), ("slices", pltpu.VMEM((devices, 8, width), BF)),
            ("semaphores", pltpu.SemaphoreType.DMA((devices + 1,))),
        ]
        + [("stage", pltpu.VMEM((3 * width // 128, spaced, 128), F32))]
        + [(name, pltpu.VMEM(value.shape, value.dtype)) for name, value in inner.items()],
    )
    got = lax.all_to_all(b["message"], "dp", 0, 0, tiled=True)

    stay = both(
        query=struct((spaced, width), BF), first_cut=struct((16, spaced), BF), grad_mixed=struct((spaced, width), BF), rows=struct((7, width), F32),
    )
    outs = both(
        attn_out_grad=struct((width // devices * width // 128, 128), F32),
        up_grad=struct((width // devices * hidden // 128, 128), F32),
        down_grad=struct((hidden // devices * width // 128, 128), F32),
        proj_grad=struct((width // devices * width // 128, 128), F32),
        up_bias_grad=struct((hidden // 128, 128), F32),
    )
    tall = struct((rows, hidden), BF)
    scratch = both(second=narrow, post=narrow, grad_embed=narrow, grad_z=narrow, grad_y=narrow, grad_pre=tall, act=tall)
    scratch |= both(grad_out=wide, grad_mixed_here=narrow)

    def rest_all(r):
        rest(r, devices)

    e = kernel_call(
        rest_all,
        {
            **w, **select(a, "normal", "inverse"),
            **{name: b[name] for name in stored},
        },
        dict(
            grad_tokens0=struct(image_tokens.shape, BF), grad_tokens1=struct(caption_tokens.shape, BF), **outs, **stay,
        ),
        near=tuple(stay),
        order=[
            name + k for k in "01" for name in (
                "middle", "gains", "shifts", "out", "embed", "grad_unit", "proj", "up_bias", "up", "down", "attn_out",
                "mixed", "pooled", "attn_in", "weights", "terms", "normal", "inverse",
            )
        ],
        scratch=[(name, pltpu.VMEM(value.shape, value.dtype)) for name, value in scratch.items()],
        cost=pl.CostEstimate(flops=4 * 10**9, bytes_accessed=8 * 10**6, transcendentals=0),
    )

    def ending(r):
        for at, t in enumerate(r.t):
            ending_tower(t, r.got, at, devices)

    d = kernel_call(
        ending,
        {"got": got, **{name: e[name] for name in stay}},
        both(
            attn_in_grad=struct((span * 3 * width // 128, 128), F32),
            gains_grad=struct((3, width), F32),
            shifts_grad=struct((7, width), F32),
        ),
        near=("got", *stay),
        moving=False,
    )
    found = {**e, **d}
    results = []
    for k in "01":
        results += [found["gains_grad" + k], found["shifts_grad" + k]]
        for name in names[2:]:
            results.append(found[f"{name}_grad{k}"].reshape(-1))
    return (b["loss"].reshape(()), e["grad_tokens0"], e["grad_tokens1"], *results, b["scale_grad"].reshape(()))


def fits(args, devices):
    width = args[0].shape[1]
    return (
        devices & (devices - 1) == 0
        and width % devices == 0
        and width // devices <= 16
        and devices * 8 <= 512
        and args[3].shape[0] == 6
        and width == 384
        and devices % 8 == 0
    )


def body(*args):
    devices = lax.axis_size("dp")
    if fits(args, devices):
        return small_body(args, devices)
    return general_body(*args)


def solution(mesh):
    rows = P("dp", None)
    part = P("dp")
    whole = P()
    tower = (whole, whole, part, part, part, whole, part, part)
    return jax.shard_map(
        body,
        mesh=mesh,
        in_specs=(rows, whole, rows, part) + (whole,) * 17,
        out_specs=(whole, rows, rows, *tower, *tower, whole),
        check_vma=False,
    )
```

```python
from types import SimpleNamespace

import jax
import jax.numpy as jnp
from jax import lax
from jax.experimental import pallas as pl
from jax.experimental.pallas import tpu as pltpu
from jax.sharding import PartitionSpec as P

HEAD = 64
CTX = 77

LAYER_EPSILON = 1e-05
UNIT_EPSILON = 1e-06

BF = jnp.bfloat16
F32 = jnp.float32


def dot(left, right, dims=((1,), (0,))):
    return lax.dot_general(left.astype(BF), right.astype(BF), (dims, ((), ())), preferred_element_type=F32)


NT = ((1,), (1,))
TN = ((0,), (0,))


def normalize(values):
    centred = values - jnp.mean(values, axis=-1, keepdims=True)
    inverse = lax.rsqrt(jnp.mean(centred * centred, axis=-1, keepdims=True) + LAYER_EPSILON)
    return centred * inverse, inverse


def norm_back(incoming, normal, inverse, gain):
    scaled = incoming * gain
    return inverse * (
        scaled
        - jnp.mean(scaled, axis=-1, keepdims=True)
        - normal * jnp.mean(scaled * normal, axis=-1, keepdims=True)
    )


def head_mask(count, width):
    heads = width // HEAD
    rows = lax.broadcasted_iota(jnp.int32, (heads * count, width), 0) // count
    lanes = lax.broadcasted_iota(jnp.int32, (heads * count, width), 1) // HEAD
    return rows == lanes


def spread(values):
    count, width = values.shape
    tiled = jnp.tile(values, (width // HEAD, 1))
    return jnp.where(head_mask(count, width), tiled, jnp.zeros_like(tiled))


def collect(values, count):
    rows, width = values.shape
    kept = jnp.where(head_mask(count, width), values, 0.0)
    return jnp.sum(kept.reshape(rows // count, count, width), axis=0)


def attend_forward(tokens, low, high, place, gains, shifts, attn_in):
    rows, width = tokens.shape
    count = low.shape[0]
    heads = width // HEAD
    normal, inverse = normalize(tokens.astype(F32))
    normal_low = normal.astype(BF)
    picked = place[:, None] == jnp.arange(rows, dtype=jnp.int32)[None, :]
    pooled = dot(picked, tokens).astype(BF)
    pooled_normal, _ = normalize(pooled.astype(F32))
    first = (pooled_normal * gains[0] + shifts[0]).astype(BF)
    query = (dot(first, attn_in[:, :width]) + shifts[1]).astype(BF)
    key_back = dot(spread(query), attn_in[:, width : 2 * width], NT) * 0.125
    offset = jnp.sum(key_back * shifts[0], axis=-1, keepdims=True)
    scores = dot(key_back * gains[0], normal_low, NT) + offset
    columns = jnp.arange(rows, dtype=jnp.int32)[None, :]
    allowed = (columns >= jnp.tile(low, heads)[:, None]) & (columns < jnp.tile(high, heads)[:, None])
    scores = jnp.where(allowed, scores, -1e30)
    expo = jnp.where(allowed, jnp.exp(scores - jnp.max(scores, axis=-1, keepdims=True)), 0.0)
    probs = expo / jnp.sum(expo, axis=-1, keepdims=True)
    probs_low = probs.astype(BF)
    probs_sum = jnp.sum(probs_low.astype(F32), axis=-1, keepdims=True)
    blend_normal = dot(probs_low, normal_low)
    blend = blend_normal * gains[0] + shifts[0] * probs_sum
    mixed = collect(dot(blend, attn_in[:, 2 * width :]) + probs_sum * shifts[2], count).astype(BF)
    kept = (normal, inverse, normal_low, picked, pooled_normal, key_back, probs, probs_low, probs_sum, blend_normal)
    return pooled, mixed, blend.astype(BF), kept


def attend_backward(grad_mixed, grad_middle, kept, gains, shifts, attn_in):
    normal, inverse, normal_low, picked, pooled_normal, key_back, probs, probs_low, probs_sum, blend_normal = kept
    rows, width = normal.shape
    count = grad_mixed.shape[0]
    wide = spread(grad_mixed)
    value_back = dot(wide, attn_in[:, 2 * width :], NT)
    offset = jnp.sum(value_back * shifts[0] + wide.astype(F32) * shifts[2], axis=-1, keepdims=True)
    grad_probs = dot(value_back * gains[0], normal_low, NT) + offset
    grad_scores = probs * (grad_probs - jnp.sum(grad_probs * probs, axis=-1, keepdims=True))
    scores_low = grad_scores.astype(BF)
    scores_sum = jnp.sum(scores_low.astype(F32), axis=-1, keepdims=True)
    turn_normal = dot(scores_low, normal_low)
    turn = turn_normal * gains[0] + shifts[0] * scores_sum
    grad_query = (collect(dot(turn, attn_in[:, width : 2 * width]), count) * 0.125).astype(BF)
    query_back = dot(grad_query, attn_in[:, :width], NT)
    gain_part = (
        jnp.sum(turn_normal * key_back, axis=0)
        + jnp.sum(blend_normal * value_back, axis=0)
        + jnp.sum(pooled_normal * query_back, axis=0)
    )
    shift_part = (
        jnp.sum(scores_sum * key_back, axis=0)
        + jnp.sum(probs_sum * value_back, axis=0)
        + jnp.sum(query_back, axis=0)
    )
    grad_first = (
        dot(scores_low, key_back, TN) + dot(probs_low, value_back, TN) + dot(picked, query_back, TN)
    )
    high = grad_middle.astype(BF)
    rest = (grad_middle - high.astype(F32)).astype(BF)
    grad_tokens = (
        norm_back(grad_first, normal, inverse, gains[0]) + dot(picked, high, TN) + dot(picked, rest, TN)
    )
    return grad_tokens.astype(BF), grad_query, turn.astype(BF), jnp.stack([gain_part, shift_part])


def pooled_forward(pooled, mixed, gains, shifts, attn_out, up, up_bias, down, proj):
    middle = pooled.astype(F32) + dot(mixed, attn_out) + shifts[3]
    second_normal, second_inv = normalize(middle)
    second = (second_normal * gains[1] + shifts[4]).astype(BF)
    pre = dot(second, up) + up_bias
    gate = jax.nn.sigmoid(1.702 * pre)
    act = (pre * gate).astype(BF)
    out = middle + dot(act, down) + shifts[5]
    post_normal, post_inv = normalize(out)
    post = (post_normal * gains[2] + shifts[6]).astype(BF)
    embed = dot(post, proj)
    radius = lax.rsqrt(jnp.sum(embed * embed, axis=-1, keepdims=True) + UNIT_EPSILON)
    unit = (embed * radius).astype(BF)
    return unit, (second_normal, second_inv, second, pre, gate, act, post_normal, post_inv, post, embed, radius)


def pooled_backward(grad_unit, kept, gains, attn_out, up, down, proj):
    second_normal, second_inv, second, pre, gate, act, post_normal, post_inv, post, embed, radius = kept
    along = jnp.sum(embed * grad_unit, axis=-1, keepdims=True)
    grad_embed = (radius * grad_unit - radius * radius * radius * embed * along).astype(BF)
    grad_post = dot(grad_embed, proj, NT)
    grad_out = norm_back(grad_post, post_normal, post_inv, gains[2])
    grad_z = grad_out.astype(BF)
    slope = gate + 1.702 * pre * gate * (1.0 - gate)
    grad_pre = (dot(grad_z, down, NT) * slope).astype(BF)
    grad_second = dot(grad_pre, up, NT)
    grad_middle = grad_out + norm_back(grad_second, second_normal, second_inv, gains[1])
    grad_y = grad_middle.astype(BF)
    grad_mixed = dot(grad_y, attn_out, NT).astype(BF)
    gain_rows = (
        jnp.sum(grad_second * second_normal, axis=0),
        jnp.sum(grad_post * post_normal, axis=0),
    )

    def total(values):
        return jnp.sum(values.astype(F32), axis=0)

    shift_rows = (total(grad_mixed), total(grad_y), total(grad_second), total(grad_z), total(grad_post))
    return grad_mixed, grad_middle, gain_rows, shift_rows, total(grad_pre), (grad_y, grad_pre, grad_z, grad_embed)


def window(total_rows, columns, devices, index):
    part = total_rows * columns // devices
    start = index * part
    first = start // columns
    if part % columns == 0:
        span = part // columns
    else:
        span = max((d * part + part - 1) // columns - d * part // columns + 1 for d in range(devices))
    first = jnp.minimum(first, total_rows - span)
    return first, span, start - first * columns, part


def cut(left, right, devices, index):
    total_rows, columns = left.shape[1], right.shape[1]
    first, span, offset, part = window(total_rows, columns, devices, index)
    rows = dot(lax.dynamic_slice_in_dim(left, first, span, 1), right, TN)
    return finish(rows, offset, part)


def finish(rows, offset, part):
    flat = rows.reshape(-1)
    if flat.shape[0] == part:
        return flat
    return lax.dynamic_slice_in_dim(flat, offset, part)


def slices_out(values, count, columns, devices):
    width = values.shape[1]
    heads = values.shape[0] // count
    cuts = []
    if (width * columns // devices) % columns == 0:
        span = width // devices
        return values.reshape(heads, count, devices, span).transpose(2, 1, 0, 3)
    for d in range(devices):
        part = width * columns // devices
        span = max((e * part + part - 1) // columns - e * part // columns + 1 for e in range(devices))
        first = min(d * part // columns, width - span)
        cuts.append(values[:, first : first + span].reshape(heads, count, span).transpose(1, 0, 2))
    return jnp.stack(cuts)


def exchange(parts):
    devices = parts[0].shape[0]
    flat = jnp.concatenate([part.reshape(devices, -1).astype(BF) for part in parts], axis=1)
    got = lax.all_to_all(flat, "dp", 0, 0, tiled=True)
    outs = []
    at = 0
    for part in parts:
        size = part[0].size
        outs.append(got[:, at : at + size].reshape(part.shape))
        at += size
    return outs


def general_body(
    image_tokens,
    image_lengths,
    caption_tokens,
    caption_eot,
    image_gains,
    image_shifts,
    image_attn_in,
    image_attn_out,
    image_up,
    image_up_bias,
    image_down,
    image_proj,
    caption_gains,
    caption_shifts,
    caption_attn_in,
    caption_attn_out,
    caption_up,
    caption_up_bias,
    caption_down,
    caption_proj,
    logit_scale,
):
    index = lax.axis_index("dp")
    devices = lax.axis_size("dp")
    count = caption_eot.shape[0]
    width = image_tokens.shape[1]
    heads = width // HEAD
    lengths = lax.dynamic_slice_in_dim(image_lengths, index * count, count)
    image_high = jnp.cumsum(lengths)
    image_low = image_high - lengths
    caption_low = jnp.arange(count, dtype=jnp.int32) * CTX
    caption_place = caption_low + caption_eot
    towers = (
        (
            image_tokens, image_low, image_high, image_low,
            image_gains.astype(F32), image_shifts.astype(F32), image_attn_in, image_attn_out,
            image_up, image_up_bias.astype(F32), image_down, image_proj,
        ),
        (
            caption_tokens, caption_low, caption_place + 1, caption_place,
            caption_gains.astype(F32), caption_shifts.astype(F32), caption_attn_in, caption_attn_out,
            caption_up, caption_up_bias.astype(F32), caption_down, caption_proj,
        ),
    )
    ahead = [attend_forward(t[0], t[1], t[2], t[3], t[4], t[5], t[6]) for t in towers]
    own = jnp.stack([ahead[0][0], ahead[0][1], ahead[1][0], ahead[1][1]])
    sent = [jnp.broadcast_to(own[None], (devices, *own.shape))]
    sent += [slices_out(a[2], count, 3 * width, devices) for a in ahead]
    got = exchange(sent)
    pairs = devices * count
    everyone = got[0].transpose(1, 0, 2, 3).reshape(4, pairs, width)
    blends = got[1:]

    units, kepts = [], []
    for k, t in enumerate(towers):
        unit, kept = pooled_forward(everyone[2 * k], everyone[2 * k + 1], t[4], t[5], t[7], t[8], t[9], t[10], t[11])
        units.append(unit)
        kepts.append(kept)
    scale = jnp.exp(logit_scale)
    logits = scale * dot(units[0], units[1], NT)
    row_top = jnp.max(logits, axis=1, keepdims=True)
    row_expo = jnp.exp(logits - row_top)
    row_sum = jnp.sum(row_expo, axis=1, keepdims=True)
    column_top = jnp.max(logits, axis=0, keepdims=True)
    column_expo = jnp.exp(logits - column_top)
    column_sum = jnp.sum(column_expo, axis=0, keepdims=True)
    diagonal = (
        lax.broadcasted_iota(jnp.int32, logits.shape, 0) == lax.broadcasted_iota(jnp.int32, logits.shape, 1)
    ).astype(F32)
    grad_logits = 0.5 * (row_expo / row_sum - diagonal) + 0.5 * (column_expo / column_sum - diagonal)
    total = (
        0.5 * jnp.sum(row_top + jnp.log(row_sum))
        + 0.5 * jnp.sum(column_top + jnp.log(column_sum))
        - jnp.sum(diagonal * logits)
    )
    scale_grad = jnp.sum(grad_logits * logits)
    grad_sim = (scale * grad_logits).astype(BF)
    grad_units = (dot(grad_sim, units[1]), dot(grad_sim, units[0], TN))

    backs, attends = [], []
    for k, t in enumerate(towers):
        back = pooled_backward(grad_units[k], kepts[k], t[4], t[7], t[8], t[10], t[11])
        backs.append(back)
        mine = lax.dynamic_slice_in_dim(back[0], index * count, count)
        mine_middle = lax.dynamic_slice_in_dim(back[1], index * count, count)
        attends.append(attend_backward(mine, mine_middle, ahead[k][3], t[4], t[5], t[6]))
    sent = []
    for a in attends:
        sent.append(jnp.broadcast_to(a[1][None], (devices, count, width)))
        sent.append(slices_out(a[2], count, 3 * width, devices))
        sent.append(jnp.broadcast_to(a[3].astype(BF)[None], (devices, 2, width)))
    got = exchange(sent)

    results = []
    for k, t in enumerate(towers):
        gains, shifts, attn_in = t[4], t[5], t[6]
        grad_query = got[3 * k].reshape(pairs, width)
        turns = got[3 * k + 1].reshape(pairs, heads, -1)
        blend = blends[k].reshape(pairs, heads, -1)
        sums = jnp.sum(got[3 * k + 2].astype(F32), axis=0)
        grad_mixed, _, gain_rows, shift_rows, up_bias_grad, factors = backs[k]
        second, act, post = kepts[k][2], kepts[k][5], kepts[k][8]
        grad_y, grad_pre, grad_z, grad_embed = factors
        pooled_normal, _ = normalize(everyone[2 * k].astype(F32))
        first_rows = (pooled_normal * gains[0] + shifts[0]).astype(BF)
        query = (dot(first_rows, attn_in[:, :width]) + shifts[1]).astype(BF)
        first, span, offset, part = window(width, 3 * width, devices, index)
        pieces = [dot(lax.dynamic_slice_in_dim(first_rows, first, span, 1), grad_query, TN)]
        for left, right, factor in ((turns, query, 0.125), (blend, grad_mixed, 1.0)):
            piece = jnp.einsum(
                "phc,phe->che", left, right.reshape(pairs, heads, HEAD), preferred_element_type=F32
            )
            pieces.append(factor * piece.reshape(span, width))
        attn_in_grad = finish(jnp.concatenate(pieces, axis=1), offset, part)
        query_shift = jnp.sum(grad_query.astype(F32), axis=0)
        gain_grad = jnp.stack([sums[0], gain_rows[0], gain_rows[1]])
        shift_grad = jnp.stack(
            [sums[1], query_shift, shift_rows[0], shift_rows[1], shift_rows[2], shift_rows[3], shift_rows[4]]
        )
        results.append(
            (
                gain_grad,
                shift_grad,
                attn_in_grad,
                cut(everyone[2 * k + 1], grad_y, devices, index),
                cut(second, grad_pre, devices, index),
                up_bias_grad,
                cut(act, grad_z, devices, index),
                cut(post, grad_embed, devices, index),
            )
        )
    return (total / pairs, attends[0][0], attends[1][0], *results[0], *results[1], scale_grad)


NEG = -1e30


def both(**entries):
    return {name + k: value for name, value in entries.items() for k in "01"}


class Late:
    def __init__(self, source, buffer, semaphore):
        self.copy = pltpu.make_async_copy(source, buffer, semaphore)
        self.buffer, self.shape = buffer, buffer.shape
        self.here = False
        self.copy.start()

    def ready(self):
        if not self.here:
            self.copy.wait()
            self.here = True
        return self.buffer

    def __getitem__(self, at):
        return self.ready()[at]


class Posted:
    def __init__(self, target, buffer, semaphore):
        self.copy = pltpu.make_async_copy(buffer, target, semaphore)
        self.buffer, self.shape = buffer, buffer.shape
        self.sent = False

    def send(self):
        if not self.sent:
            self.copy.start()
            self.sent = True

    def put(self, value):
        self.buffer[...] = value
        self.send()

    def __setitem__(self, at, value):
        self.buffer[at] = value

    def __getitem__(self, at):
        return self.buffer[at]


class Plain:
    def __init__(self, ref):
        self.buffer, self.shape = ref, ref.shape

    def ready(self):
        return self.buffer

    def send(self):
        pass

    def put(self, value):
        self.buffer[...] = value

    def __setitem__(self, at, value):
        self.buffer[at] = value

    def __getitem__(self, at):
        return self.buffer[at]


def kernel_call(fn, ins, outs, near=(), order=(), raw=(), scratch=(), cost=None, moving=True):
    shapes = {**ins, **outs}
    integer = lambda name: shapes[name].ndim == 1 and shapes[name].dtype == jnp.int32
    still = [name for name in shapes if name in near or name in raw or integer(name)]
    moved = [*order, *(name for name in shapes if name not in still and name not in order)] if moving else []
    names = [*shapes, *(name for name, _ in scratch)]

    def kernel(*refs):
        r = SimpleNamespace(t=(SimpleNamespace(), SimpleNamespace()))
        found = dict(zip(names, refs))
        semaphores, buffers = refs[-1], refs[len(names) : -1]
        for k, name in enumerate(moved):
            kind = Late if name in ins else Posted
            found[name] = kind(found[name], buffers[k], semaphores.at[k])
        for name in shapes:
            if name not in moved and name not in raw and not integer(name):
                found[name] = Plain(found[name])
        for name, ref in found.items():
            if name[-1] in "01":
                setattr(r.t[int(name[-1])], name[:-1], ref)
            else:
                setattr(r, name, ref)
        fn(r)
        posted = [found[name] for name in moved if name in outs]
        for ref in posted:
            ref.send()
        for ref in posted:
            ref.copy.wait()
        for name in moved:
            if name in ins:
                found[name].ready()

    def spec(name):
        space = pl.ANY if name in moved or name in raw else pltpu.SMEM if integer(name) else pltpu.VMEM
        return pl.BlockSpec(memory_space=space)

    results = pl.pallas_call(
        kernel,
        out_shape=tuple(pltpu.VMEM(out.shape, out.dtype) if name in near else out for name, out in outs.items()),
        in_specs=[spec(name) for name in ins],
        out_specs=tuple(spec(name) for name in outs),
        scratch_shapes=[shape for _, shape in scratch]
        + [pltpu.VMEM(shapes[name].shape, shapes[name].dtype) for name in moved]
        + [pltpu.SemaphoreType.DMA((max(len(moved), 1),))],
        cost_estimate=cost,
        name=fn.__name__,
    )(
        *(
            pltpu.with_memory_space_constraint(value, pltpu.VMEM) if name in near else value
            for name, value in ins.items()
        )
    )
    return dict(zip(outs, results))


def select(space, *names):
    return {name + k: space[name + k] for name in names for k in "01"}


def iota(shape, axis):
    return lax.broadcasted_iota(jnp.int32, shape, axis)


def tiles(values, copies):
    return jnp.concatenate([values] * copies, axis=0)


def spread8(values):
    width = values.shape[1]
    heads = width // HEAD
    tiled = tiles(values, heads)
    keep = (iota(tiled.shape, 0) >> 3) == (iota(tiled.shape, 1) >> 6)
    return jnp.where(keep, tiled, 0.0).astype(BF)


def collect8(values):
    rows, width = values.shape
    total = None
    lane = iota((8, width), 1) >> 6
    for head in range(rows // 8):
        piece = jnp.where(lane == head, values[8 * head : 8 * head + 8], 0.0)
        total = piece if total is None else total + piece
    return total


def row_vector(scalars, rows, rest):
    place = iota((rows, 1), 0) & 7
    values = jnp.full((rows, 1), rest, jnp.int32)
    for k, scalar in enumerate(scalars):
        values = jnp.where(place == k, scalar, values)
    return values


def padded(rows):
    return -(-rows // 128) * 128


def ahead_tower(t, lows, highs, places):
    x, xs, normal, inverse = t.x.ready(), t.xs, t.normal.buffer, t.inverse.buffer
    gains, shifts, attn_in = t.gains, t.shifts, t.attn_in
    rows, width = x.shape
    full = normal.shape[0]
    size = 144 if rows % 144 < 16 else 112
    main = rows // size * size

    def norm_rows(at, count):
        raw = x[pl.ds(at, count), :]
        low_normal, inv = normalize(raw.astype(F32))
        xs[pl.ds(at, count), :] = raw
        normal[pl.ds(at, count), :] = low_normal.astype(BF)
        inverse[pl.ds(at, count), :] = inv

    @pl.loop(0, main // size)
    def _(step):
        norm_rows(pl.multiple_of(step * size, 16), size)

    xs[pl.ds(main, full - main), :] = jnp.zeros((full - main, width), BF)
    normal[pl.ds(main, full - main), :] = jnp.zeros((full - main, width), BF)
    inverse[pl.ds(main, full - main), :] = jnp.zeros((full - main, 1), F32)
    if rows > main:
        norm_rows(main, rows - main)
    t.normal.send()
    t.inverse.send()
    yield
    gain, shift = gains[0:1, :].astype(F32), shifts[0:1, :].astype(F32)
    pick = (row_vector(places, 8, -1) == iota((8, full), 1)).astype(F32)
    pooled = dot(pick, xs[...])
    pooled_normal, _ = normalize(pooled)
    first = pooled_normal * gain + shift
    query = (dot(first, attn_in[:, :width]) + shifts[1:2, :].astype(F32)).astype(BF).astype(F32)
    yield
    key_back = dot(spread8(query), attn_in[:, width : 2 * width], NT) * 0.125
    offset = jnp.sum(key_back * shift, axis=-1, keepdims=True)
    yield
    scores = dot(key_back * gain, normal[...], NT) + offset
    rows_all = scores.shape[0]
    columns = iota(scores.shape, 1)
    allowed = (columns >= row_vector(lows, rows_all, 0)) & (columns < row_vector(highs, rows_all, 1))
    yield
    scores = jnp.where(allowed, scores, NEG)
    expo = jnp.where(allowed, jnp.exp(scores - jnp.max(scores, axis=-1, keepdims=True)), 0.0)
    probs = expo / jnp.sum(expo, axis=-1, keepdims=True)
    probs_low = probs.astype(BF)
    probs_sum = jnp.sum(probs_low.astype(F32), axis=-1, keepdims=True)
    yield
    blend_normal = dot(probs_low, normal[...])
    blend = blend_normal * gain + shift * probs_sum
    yield
    mixed = collect8(dot(blend, attn_in[:, 2 * width :]) + probs_sum * shifts[2:3, :].astype(F32))
    t.probs.put(probs)
    t.pick[...] = pick
    t.pooled_normal[...] = pooled_normal
    t.key_back[...] = key_back
    t.probs_sum[...] = probs_sum
    t.blend_normal[...] = blend_normal
    t.blend[...] = blend
    t.found = pooled, mixed


def slots(main, extra):
    row = iota(main.shape, 0)
    return jnp.where(row == 6, extra[0], jnp.where(row == 7, extra[1], main))


def ahead(r):
    me = lax.axis_index("dp")
    at = me * 6
    highs, lows, total = [], [], jnp.int32(0)
    for k in range(6):
        lows.append(total)
        total = total + r.lengths[at + k]
        highs.append(total)
    one = ahead_tower(r.t[0], lows, highs, lows)
    lows = [k * CTX for k in range(6)]
    places = [k * CTX + r.eot[k] for k in range(6)]
    highs = [place + 1 for place in places]
    together(one, ahead_tower(r.t[1], lows, highs, places))
    (pooled, mixed), (pooled1, mixed1) = r.t[0].found, r.t[1].found
    width = pooled.shape[1]
    for b, main in enumerate((pooled, mixed, pooled1)):
        r.own[:, b * width : (b + 1) * width] = slots(main, (mixed1[b : b + 1], mixed1[3 + b : 4 + b])).astype(BF)


def place_matrix(width, devices):
    span = width // devices
    source, target = iota((width, devices * 16), 0), iota((width, devices * 16), 1)
    spot = target & 15
    return jnp.where((source == (target >> 4) * span + spot) & (spot < span), 1.0, 0.0).astype(BF)


def pieces_of(parts, place, devices, first):
    lane = iota((8, 128), 1)
    apart = dot(jnp.concatenate(parts, axis=0), place)
    found = [[] for _ in parts]
    for group in range(devices // 8):
        columns = slice(128 * group, 128 * group + 128)
        for j in range(len(parts)):
            pieces = [apart[48 * j + 8 * h : 48 * j + 8 * h + 8, columns] for h in range(6)]
            pieces += [jnp.zeros((8, 128), F32)] * 2
            for bit in (1, 2, 4):
                low = (lane & (16 * bit)) == 0
                turned = list(pieces)
                for h in range(8):
                    if h & bit == 0:
                        one, two = pieces[h], pieces[h + bit]
                        turned[h] = jnp.where(low, one, pltpu.roll(two, 16 * bit, 1))
                        turned[h + bit] = jnp.where(low, pltpu.roll(one, 128 - 16 * bit, 1), two)
                pieces = turned
            shift = 96 * (first + j) % 128
            found[j] += [pltpu.roll(piece, shift, 1) if shift else piece for piece in pieces]
    return found


def row(ref, j):
    return ref[j : j + 1, :].astype(F32)


def bias_part(t, at):
    j = at // 128
    return jnp.concatenate([row(t.up_bias, j), row(t.up_bias, j + 1)], axis=1)


def gate_of(pre):
    return 0.5 + 0.5 * jnp.tanh(0.851 * pre)


def slope_of(pre, gate):
    return gate + 1.702 * pre * gate * (1.0 - gate)


def radius_of(embed):
    return lax.rsqrt(jnp.sum(embed * embed, axis=-1, keepdims=True) + UNIT_EPSILON)


def together(one, two):
    for _ in zip(one, two, strict=True):
        pass


def slot_rows(devices):
    return [slice(devices * slot, devices * (slot + 1)) for slot in range(6)]


def own_row(found, slot, values):
    piece = values[:8]
    return jnp.where(iota(piece.shape, 0) == slot, pltpu.roll(piece, slot, 0) if slot else piece, found)


def own_rows(values, devices):
    found = jnp.zeros((8, values.shape[1]), F32)
    for slot, rows in enumerate(slot_rows(devices)):
        found = own_row(found, slot, values[rows, :])
    return found


def normal_rows(values, gain, shift):
    normal, _ = normalize(values)
    return (normal * gain + shift).astype(BF)


def middle_tower(x, mixed, t, devices):
    slots_of = slot_rows(devices)
    for slot, rows in enumerate(slots_of):
        t.mixed[rows, :] = mixed(slot).astype(BF)
    t.mixed.send()
    blend = dot(t.mixed[...], t.attn_out[...])
    yield
    gain, shift, add = row(t.gains, 1), row(t.shifts, 4), row(t.shifts, 3)
    for slot, rows in enumerate(slots_of):
        pooled = x(slot)
        t.pooled[rows, :] = pooled.astype(BF)
        middle = pooled + blend[rows] + add
        t.middle[rows, :] = middle
        t.second[rows, :] = normal_rows(middle, gain, shift)
    t.pooled.send()
    t.middle.send()
    own_slope = []
    for at in range(0, t.up.shape[1], 256):
        cols = slice(at, at + 256)
        whole, bias = dot(t.second[...], t.up[:, cols]), bias_part(t, at)
        yield
        own = jnp.zeros((8, 256), F32)
        for slot, rows in enumerate(slots_of):
            pre = whole[rows] + bias
            t.act[rows, cols] = (pre * gate_of(pre)).astype(BF)
            own = own_row(own, slot, pre)
        own_slope.append(slope_of(own, gate_of(own)))
    fall = dot(t.act[...], t.down[...])
    yield
    gain, shift, add = row(t.gains, 2), row(t.shifts, 6), row(t.shifts, 5)
    for rows in slots_of:
        out = t.middle[rows, :] + fall[rows] + add
        t.out[rows, :] = out
        t.post[rows, :] = normal_rows(out, gain, shift)
    t.out.send()
    embeds = dot(t.post[...], t.proj[...])
    yield
    for rows in slots_of:
        embed = embeds[rows]
        t.embed[rows, :] = embed
        t.unit[rows, :] = (embed * radius_of(embed)).astype(BF)
    t.embed.send()
    t.own = (own_rows(t.middle, devices), own_slope, own_rows(t.out, devices), own_rows(t.embed, devices))


def total_row(values):
    return jnp.sum(values.astype(F32), axis=0, keepdims=True)


def unit_back(grad_unit, embed, radius):
    along = jnp.sum(embed * grad_unit, axis=-1, keepdims=True)
    return (radius * grad_unit - radius * radius * radius * embed * along).astype(BF)


def fold(values):
    return jnp.sum(values.astype(F32).reshape(-1, 8, values.shape[1]), axis=0)


def middle_back(t, devices):
    slots_of = slot_rows(devices)
    width = t.gains.shape[1]
    sums = [jnp.zeros((8, width), F32)] * 7

    def count(values, *places):
        for j, value in zip(places, values, strict=True):
            sums[j] = sums[j] + fold(value)

    gain, shift = row(t.gains, 1), row(t.shifts, 4)
    for rows in slots_of:
        t.second[rows, :] = normal_rows(t.middle[rows, :], gain, shift)
    for rows in slots_of:
        embed = t.embed[rows, :]
        t.grad_embed[rows, :] = unit_back(t.grad_unit[rows, :], embed, radius_of(embed))
    posts = dot(t.grad_embed[...], t.proj[...], NT)
    gain, shift = row(t.gains, 2), row(t.shifts, 6)
    for rows in slots_of:
        normal, inverse = normalize(t.out[rows, :])
        t.post[rows, :] = (normal * gain + shift).astype(BF)
        grad_post = posts[rows]
        grad_out = norm_back(grad_post, normal, inverse, gain)
        grad_z = grad_out.astype(BF)
        t.grad_out[rows, :] = grad_out
        t.grad_z[rows, :] = grad_z
        count((grad_post * normal, grad_z, grad_post), 1, 5, 6)
    for at in range(0, t.up.shape[1], 256):
        cols = slice(at, at + 256)
        whole, bias = dot(t.second[...], t.up[:, cols]), bias_part(t, at)
        back = dot(t.grad_z[...], t.down[cols, :], NT)
        total = jnp.zeros((8, 256), F32)
        for rows in slots_of:
            pre = whole[rows] + bias
            gate = gate_of(pre)
            t.act[rows, cols] = (pre * gate).astype(BF)
            grad_pre = (back[rows] * slope_of(pre, gate)).astype(BF)
            t.grad_pre[rows, cols] = grad_pre
            total = total + fold(grad_pre)
        total = total_row(total)
        for j in range(2):
            t.up_bias_grad[at // 128 + j : at // 128 + j + 1, :] = total[:, 128 * j : 128 * j + 128]
    seconds = dot(t.grad_pre[...], t.up[...], NT)
    gain = row(t.gains, 1)
    for rows in slots_of:
        normal, inverse = normalize(t.middle[rows, :])
        grad_second = seconds[rows]
        grad_y = (t.grad_out[rows, :] + norm_back(grad_second, normal, inverse, gain)).astype(BF)
        t.grad_y[rows, :] = grad_y
        count((grad_second * normal, grad_y, grad_second), 0, 3, 4)
    mixeds = dot(t.grad_y[...], t.attn_out[...], NT)
    for rows in slots_of:
        grad_mixed = mixeds[rows].astype(BF)
        t.grad_mixed_here[rows, :] = grad_mixed
        count((grad_mixed,), 2)
    for j, value in enumerate(sums):
        t.rows[j : j + 1, :] = total_row(value)


def own_back(t, grad_unit):
    middle, own_slope, out, embed = t.own
    second_normal, second_inv = normalize(middle)
    post_normal, post_inv = normalize(out)
    radius = radius_of(embed)
    gain, shift = row(t.gains, 0), row(t.shifts, 0)
    width = gain.shape[1]
    grad_embed = unit_back(grad_unit, embed, radius)
    grad_post = dot(grad_embed, t.proj[...], NT)
    yield
    grad_out = norm_back(grad_post, post_normal, post_inv, row(t.gains, 2))
    grad_act = dot(grad_out, t.down[...], NT)
    yield
    grad_pre = (grad_act * jnp.concatenate(own_slope, axis=1)).astype(BF)
    grad_second = dot(grad_pre, t.up[...], NT)
    yield
    grad_middle = grad_out + norm_back(grad_second, second_normal, second_inv, row(t.gains, 1))
    grad_mixed = dot(grad_middle, t.attn_out[...], NT).astype(BF)
    yield
    wide = spread8(grad_mixed.astype(F32))
    value_back = dot(wide, t.attn_in[:, 2 * width :], NT)
    yield
    offset = jnp.sum(value_back * shift + wide.astype(F32) * row(t.shifts, 2), axis=-1, keepdims=True)
    grad_probs = dot(value_back * gain, t.normal[...], NT) + offset
    yield
    probs = t.probs[...]
    grad_scores = probs * (grad_probs - jnp.sum(grad_probs * probs, axis=-1, keepdims=True))
    scores_low = grad_scores.astype(BF)
    scores_sum = jnp.sum(scores_low.astype(F32), axis=-1, keepdims=True)
    turn_normal = dot(scores_low, t.normal[...])
    yield
    turn = turn_normal * gain + shift * scores_sum
    grad_query = (collect8(dot(turn, t.attn_in[:, width : 2 * width])) * 0.125).astype(BF)
    yield
    query_back = dot(grad_query, t.attn_in[:, :width], NT)
    yield
    key_back, probs_sum = t.key_back[...], t.probs_sum[...]
    gain_part = total_row(
        turn_normal * key_back + t.blend_normal[...] * value_back
    ) + total_row(t.pooled_normal[...] * query_back)
    shift_part = total_row(scores_sum * key_back + probs_sum * value_back) + total_row(query_back)
    t.turn, t.sent = turn, slots(grad_query.astype(F32), (gain_part, shift_part)).astype(BF)

    def finish():
        t.weights[0:48, :] = scores_low
        t.weights[48:96, :] = probs.astype(BF)
        pick = t.pick[...]
        t.weights[96:112, :] = jnp.concatenate([pick, pick], axis=0).astype(BF)
        t.weights[112:, :] = jnp.zeros((16, probs.shape[1]), BF)
        t.weights.send()
        high = grad_middle.astype(BF).astype(F32)
        none = jnp.zeros((24, width), F32)
        t.terms[:, :width] = jnp.concatenate([key_back, value_back, query_back, none], axis=0).astype(BF)
        t.terms[:, width:] = jnp.concatenate(
            [jnp.zeros((96, width), F32), high, grad_middle - high, none[:16]], axis=0
        ).astype(BF)
        t.terms.send()

    t.finish = finish


def gather_steps(devices):
    steps = []
    bit = devices // 2
    while bit >= 8:
        steps.append([bit])
        bit //= 2
    return steps + [[6, 4, 2], [1]]


def block_of(distance, devices):
    high = devices.bit_length() - 4
    bit = lambda k: (distance >> k) & 1
    out = (bit(1) << high) | ((bit(2) ^ bit(1)) << (high + 1)) | (bit(0) << (high + 2))
    for k in range(high):
        out |= bit(high + 2 - k) << k
    return out


def centre(r, devices):
    width = r.t[0].attn_out.shape[0]
    rows = devices * 6
    steps = width // 128
    for c in range(3 * steps):
        lanes = slice(128 * c, 128 * (c + 1))
        r.stage[c] = r.gathered[:, :, lanes].astype(F32).reshape(devices * 8, 128)
    group = lambda b, slot: jnp.concatenate(
        [r.stage[b * steps + k, pl.ds(slot, devices, stride=8), :] for k in range(steps)], axis=1
    )
    together(
        middle_tower(lambda slot: group(0, slot), lambda slot: group(1, slot), r.t[0], devices),
        middle_tower(lambda slot: group(2, slot), lambda slot: group(slot % 3, 6 + slot // 3), r.t[1], devices),
    )
    unit0, unit1 = r.t[0].unit[...], r.t[1].unit[...]
    to, source = iota((rows, rows), 0), iota((rows, rows), 1)
    scale = jnp.exp(r.logit_scale[...])
    logits = scale * dot(unit0, unit1, NT)
    row_top = jnp.max(logits, axis=1, keepdims=True)
    row_expo = jnp.exp(logits - row_top)
    row_total = jnp.sum(row_expo, axis=1, keepdims=True)
    column_top = jnp.max(logits, axis=0, keepdims=True)
    column_expo = jnp.exp(logits - column_top)
    column_total = jnp.sum(column_expo, axis=0, keepdims=True)
    diagonal = (to == source).astype(F32)
    grad_logits = 0.5 * (row_expo / row_total - diagonal) + 0.5 * (column_expo / column_total - diagonal)
    whole = lambda values: jnp.sum(jnp.sum(values, axis=1, keepdims=True), axis=0, keepdims=True)
    tops = 0.5 * whole(row_top + jnp.log(row_total)) + 0.5 * whole(column_top + jnp.log(column_total))
    r.loss[...] = (tops - whole(diagonal * logits)) / rows
    r.scale_grad[...] = whole(grad_logits * logits)
    grad_sim = (scale * grad_logits).astype(BF)
    grad_unit0, grad_unit1 = dot(grad_sim, unit1), dot(grad_sim, unit0, TN)
    r.t[0].grad_unit.put(grad_unit0)
    r.t[1].grad_unit.put(grad_unit1)
    together(own_back(r.t[0], own_rows(grad_unit0, devices)), own_back(r.t[1], own_rows(grad_unit1, devices)))
    for k, t in enumerate(r.t):
        r.letter[:, k * width : (k + 1) * width] = t.sent
    copies = [
        pltpu.make_async_copy(r.letter, r.message.at[d, :, pl.ds(0, 2 * width)], r.semaphores.at[d])
        for d in range(devices)
    ]
    for copy in copies:
        copy.start()
    lane = iota((8, 128), 1)
    first, second = pieces_of([t.turn for t in r.t], r.place[...], devices, 0)
    for d in range(devices):
        r.slices[d, :, :128] = jnp.where(lane < 96, first[d], second[d]).astype(BF)
        r.slices[d, :, 128:256] = jnp.where(lane < 64, second[d], r.packed[d, :, :128]).astype(BF)
        r.slices[d, :, 256:] = r.packed[d, :, 128:].astype(BF)
    copies.append(
        pltpu.make_async_copy(r.slices, r.message.at[:, :, pl.ds(2 * width, width)], r.semaphores.at[devices])
    )
    copies[-1].start()
    for t in r.t:
        t.finish()
    for copy in copies:
        copy.wait()


def store_flat(ref, values):
    span, columns = values.shape
    steps = columns // 128
    for c in range(steps):
        ref[pl.ds(c, span, stride=steps), :] = values[:, 128 * c : 128 * (c + 1)]


def picked_rows(first, span, total):
    tall = -(-span // 16) * 16
    near = iota((tall, total), 1) - first
    return ((near == iota((tall, total), 0)) & (near < span)).astype(F32)


def weight_cuts(t, order, devices):
    me = lax.axis_index("dp")
    width = t.gains.shape[1]
    for left, right, out in (
        (t.mixed, t.grad_y, t.attn_out_grad),
        (t.second, t.grad_pre, t.up_grad),
        (t.act, t.grad_z, t.down_grad),
        (t.post, t.grad_embed, t.proj_grad),
    ):
        depth = left.shape[1]
        span = depth // devices
        chosen = picked_rows(me * span, span, depth)
        cut_rows = dot(chosen, left[...], NT)
        store_flat(out, dot(cut_rows, right[...])[:span])
    pooled_normal, _ = normalize(dot(order, t.pooled[...]))
    first = (pooled_normal * row(t.gains, 0) + row(t.shifts, 0)).astype(BF)
    t.query[...] = (dot(first, t.attn_in[:, :width]) + row(t.shifts, 1)).astype(BF)
    span = width // devices
    t.first_cut[...] = dot(picked_rows(me * span, span, width), first, NT).astype(BF)


def token_grads(t):
    gain = row(t.gains, 0)
    rows, width = t.grad_tokens.shape
    for at in range(0, rows, 128):
        count = min(128, rows - at)
        joint = dot(t.weights[:, at : at + 128], t.terms[...], TN)
        for part in range(0, count, 32):
            size = min(32, count - part)
            here = slice(at + part, at + part + 32)
            piece = joint[part : part + 32]
            normal = t.normal[here, :].astype(F32)
            values = norm_back(piece[:, :width], normal, t.inverse[here, :], gain) + piece[:, width:]
            t.grad_tokens[at + part : at + part + size, :] = values[:size].astype(BF)


def rest(r, devices):
    shape = (devices * 8, devices * 6)
    to, source = iota(shape, 0), iota(shape, 1)
    block = block_of(lax.axis_index("dp") ^ (to >> 3), devices)
    slot = to & 7
    order = jnp.where((source == slot * devices + block) & (slot < 6), 1.0, 0.0).astype(BF)
    for t in r.t:
        middle_back(t, devices)
        t.grad_mixed[...] = dot(order, t.grad_mixed_here[...]).astype(BF)
        weight_cuts(t, order, devices)
        token_grads(t)
        t.grad_tokens.send()


def ending_tower(t, got, at, devices):
    width = t.query.shape[1]
    heads = width // HEAD
    span = width // devices
    rows = devices * 8
    raw = got[:, :, at * width : (at + 1) * width].astype(F32).reshape(rows, width)
    slot = iota((rows, width), 0) & 7
    grad_query = jnp.where(slot < 6, raw, 0.0)
    kind, place = iota((8, rows), 0), iota((8, rows), 1) & 7
    chooser = ((kind == 0) & (place == 6)) | ((kind == 1) & (place == 7)) | ((kind == 2) & (place < 6))
    sums = dot(jnp.where(chooser, 1.0, 0.0), raw)
    pieces = [dot(t.first_cut[...], grad_query)]
    for j, right, factor in ((at, t.query, 0.125), (2 + at, t.grad_mixed, 1.0)):
        first = 96 * j // 128 * 128
        left = got[:, :, 2 * width + first : 2 * width + (96 * j + 223) // 128 * 128].astype(F32)
        tall = dot(left.reshape(rows, left.shape[2]), right[...], TN)[96 * j - first :]
        lane = iota((16, width), 1) >> 6
        total = None
        for head in range(heads):
            piece = jnp.where(lane == head, tall[16 * head : 16 * head + 16], 0.0)
            total = piece if total is None else total + piece
        pieces.append(factor * total)
    flat = t.attn_in_grad
    steps = 3 * width // 128
    for part, values in enumerate(pieces):
        for c in range(width // 128):
            flat[pl.ds(part * (width // 128) + c, span, stride=steps), :] = values[:span, 128 * c : 128 * (c + 1)]
    got_rows = t.rows[...]
    t.gains_grad[...] = jnp.concatenate([sums[0:1], got_rows[0:2]], axis=0)
    t.shifts_grad[...] = jnp.concatenate([sums[1:2], sums[2:3], got_rows[2:7]], axis=0)


def small_body(args, devices):
    image_tokens, image_lengths, caption_tokens, caption_eot, *weights, logit_scale = args
    names = ("gains", "shifts", "attn_in", "attn_out", "up", "up_bias", "down", "proj")
    w = {}
    for k in range(2):
        for j, name in enumerate(names):
            value = weights[8 * k + j]
            w[f"{name}{k}"] = value.reshape(-1, 128) if value.ndim == 1 else value
    width = image_tokens.shape[1]
    heads = width // HEAD
    hidden = w["up0"].shape[1]
    rows, spaced = devices * 6, devices * 8
    span = width // devices
    struct = jax.ShapeDtypeStruct
    full = {"0": padded(image_tokens.shape[0]), "1": padded(caption_tokens.shape[0])}
    hr = heads * 8

    outs = {}
    for k in "01":
        tower = dict(
            normal=struct((full[k], width), BF),
            inverse=struct((full[k], 1), F32),
            probs=struct((hr, full[k]), F32),
            pick=struct((8, full[k]), F32),
        )
        outs |= {name + k: value for name, value in tower.items()}
    outs |= both(
        pooled_normal=struct((8, width), F32),
        key_back=struct((hr, width), F32),
        probs_sum=struct((hr, 1), F32),
        blend_normal=struct((hr, width), F32),
        blend=struct((hr, width), F32),
    )
    a = kernel_call(
        ahead,
        dict(lengths=image_lengths, eot=caption_eot, x0=image_tokens, x1=caption_tokens, **select(w, *names[:3])),
        dict(own=struct((8, 3 * width), BF), **outs),
        near=("own",),
        moving=False,
        scratch=[("xs" + k, pltpu.VMEM((full[k], width), BF)) for k in "01"],
    )

    gathered = a["own"][None]
    steps = gather_steps(devices)
    for step in steps:
        if step == [1]:
            gathered, packed = lax.optimization_barrier((gathered, packed))
        if step == steps[-2]:
            gathered, blends = lax.optimization_barrier((gathered, select(a, "blend")))
        others = [lax.ppermute(gathered, "dp", [(d, d ^ away) for d in range(devices)]) for away in step]
        if step == steps[-2]:

            def pack_blend(r):
                lane = iota((8, 128), 1)
                place = place_matrix(width, devices)
                r.place[...] = place
                first, second = pieces_of([t.blend[...] for t in r.t], place, devices, 2)
                for d in range(devices):
                    r.packed[d, :, :128] = first[d]
                    r.packed[d, :, 128:] = jnp.where(lane < 32, first[d], second[d])

            packed = kernel_call(
                pack_blend, blends,
                dict(packed=struct((devices, 8, 256), F32), place=struct((width, devices * 16), BF)), moving=False,
                cost=pl.CostEstimate(flops=10**8, bytes_accessed=400000, transcendentals=0),
            )
        gathered = jnp.concatenate([gathered, *others], axis=0)

    narrow = struct((rows, width), BF)
    wide = struct((rows, width), F32)
    outs = both(pooled=narrow, mixed=narrow, middle=wide, out=wide, embed=wide, grad_unit=wide)
    outs |= both(terms=struct((128, 2 * width), BF))
    outs |= {"weights" + k: struct((128, full[k]), BF) for k in "01"}
    stored = tuple(outs)

    inner = both(act=struct((rows, hidden), BF), second=narrow, post=narrow, unit=narrow)

    def centre_all(r):
        centre(r, devices)

    early = ("attn_out0", "attn_out1", "up0", "proj0", "proj1")
    heavy = [name + k for name in ("shifts", "gains", "up_bias", "up", "down", "proj") for k in "01" if name + k not in early]
    b = kernel_call(
        centre_all,
        dict(
            gathered=gathered, logit_scale=logit_scale.reshape(1, 1), **w, **packed,
            **{name: value for name, value in a.items() if name[:-1] not in ("ow", "inverse", "blend")},
        ),
        dict(
            message=struct((devices, 8, 3 * width), BF), loss=struct((1, 1), F32), scale_grad=struct((1, 1), F32),
            **outs,
        ),
        near=("gathered", *early),
        order=heavy,
        raw=("message",),
        scratch=[
            ("letter", pltpu.VMEM((8, 2 * width), BF)), ("slices", pltpu.VMEM((devices, 8, width), BF)),
            ("semaphores", pltpu.SemaphoreType.DMA((devices + 1,))),
        ]
        + [("stage", pltpu.VMEM((3 * width // 128, spaced, 128), F32))]
        + [(name, pltpu.VMEM(value.shape, value.dtype)) for name, value in inner.items()],
    )
    got = lax.all_to_all(b["message"], "dp", 0, 0, tiled=True)

    stay = both(
        query=struct((spaced, width), BF), first_cut=struct((16, spaced), BF), grad_mixed=struct((spaced, width), BF), rows=struct((7, width), F32),
    )
    outs = both(
        attn_out_grad=struct((width // devices * width // 128, 128), F32),
        up_grad=struct((width // devices * hidden // 128, 128), F32),
        down_grad=struct((hidden // devices * width // 128, 128), F32),
        proj_grad=struct((width // devices * width // 128, 128), F32),
        up_bias_grad=struct((hidden // 128, 128), F32),
    )
    tall = struct((rows, hidden), BF)
    scratch = both(second=narrow, post=narrow, grad_embed=narrow, grad_z=narrow, grad_y=narrow, grad_pre=tall, act=tall)
    scratch |= both(grad_out=wide, grad_mixed_here=narrow)

    def rest_all(r):
        rest(r, devices)

    e = kernel_call(
        rest_all,
        {
            **w, **select(a, "normal", "inverse"),
            **{name: b[name] for name in stored},
        },
        dict(
            grad_tokens0=struct(image_tokens.shape, BF), grad_tokens1=struct(caption_tokens.shape, BF), **outs, **stay,
        ),
        near=tuple(stay),
        order=[
            name + k for k in "01" for name in (
                "middle", "gains", "shifts", "out", "embed", "grad_unit", "proj", "up_bias", "up", "down", "attn_out",
                "mixed", "pooled", "attn_in", "weights", "terms", "normal", "inverse",
            )
        ],
        scratch=[(name, pltpu.VMEM(value.shape, value.dtype)) for name, value in scratch.items()],
        cost=pl.CostEstimate(flops=4 * 10**9, bytes_accessed=8 * 10**6, transcendentals=0),
    )

    def ending(r):
        for at, t in enumerate(r.t):
            ending_tower(t, r.got, at, devices)

    d = kernel_call(
        ending,
        {"got": got, **{name: e[name] for name in stay}},
        both(
            attn_in_grad=struct((span * 3 * width // 128, 128), F32),
            gains_grad=struct((3, width), F32),
            shifts_grad=struct((7, width), F32),
        ),
        near=("got", *stay),
        moving=False,
    )
    found = {**e, **d}
    results = []
    for k in "01":
        results += [found["gains_grad" + k], found["shifts_grad" + k]]
        for name in names[2:]:
            results.append(found[f"{name}_grad{k}"].reshape(-1))
    return (b["loss"].reshape(()), e["grad_tokens0"], e["grad_tokens1"], *results, b["scale_grad"].reshape(()))


def fits(args, devices):
    width = args[0].shape[1]
    return (
        devices & (devices - 1) == 0
        and width % devices == 0
        and width // devices <= 16
        and devices * 8 <= 512
        and args[3].shape[0] == 6
        and width == 384
        and devices % 8 == 0
    )


def body(*args):
    devices = lax.axis_size("dp")
    if fits(args, devices):
        return small_body(args, devices)
    return general_body(*args)


def solution(mesh):
    rows = P("dp", None)
    part = P("dp")
    whole = P()
    tower = (whole, whole, part, part, part, whole, part, part)
    return jax.shard_map(
        body,
        mesh=mesh,
        in_specs=(rows, whole, rows, part) + (whole,) * 17,
        out_specs=(whole, rows, rows, *tower, *tower, whole),
        check_vma=False,
    )
```
